32 devices in a mesh: seq: 8 (over z, y), mp: 4 (over x, core).
Axes of the slice: x: 2, y: 2, z: 4, core: 2. Of those that a mesh axis runs over, the one named last changes fastest.
Arguments:
- inputs: bfloat16 [16384, 768], P(('seq', 'mp')), may hold values from -6 to 6
- doc_bounds: int32 [2, 16384], P(None, 'seq'), may hold values from 0 to 16384, as said below
- qkv_weight: bfloat16 [2, 3, 768, 768], P(None, None, None, 'mp'), may hold values from -0.21875 to 0.21875
- qv_bias: float32 [2, 2, 768], P(None, None, 'mp'), may hold values from -1.8 to 1.8
- conv_weight: float32 [2, 2, 5, 768], P(None, None, None, 'mp'), may hold values from -2.7 to 2.7
- conv_bias: float32 [2, 2, 768], P(None, None, 'mp'), may hold values from -1.8 to 1.8
- out_weight: bfloat16 [2, 768, 768], P(None, 'mp'), may hold values from -1.75 to 1.75
- up_weight: bfloat16 [2, 768, 3072], P(None, None, 'mp'), may hold values from -0.21875 to 0.21875
- up_bias: float32 [2, 3072], P(None, 'mp'), may hold values from -1.8 to 1.8
- down_weight: bfloat16 [2, 3072, 768], P(None, 'mp'), may hold values from -0.109375 to 0.109375
- norm_gains: float32 [2, 2, 768], replicated, may hold values from 0.5 to 1.5
- shared_biases: float32 [2, 4, 768], replicated, may hold values from -1.8 to 1.8
- cotangent: bfloat16 [16384, 768], P(('seq', 'mp')), may hold values from -6 to 6
Outputs:
- outputs: float32 [16384, 768], P(('seq', 'mp'))
- grad_input: float32 [16384, 768], P(('seq', 'mp'))
- grad_qkv: float32 [2, 3, 768, 768], P(None, None, None, 'mp')
- grad_qv_bias: float32 [2, 2, 768], P(None, None, 'mp')
- grad_conv_weight: float32 [2, 2, 5, 768], P(None, None, None, 'mp')
- grad_conv_bias: float32 [2, 2, 768], P(None, None, 'mp')
- grad_out_weight: float32 [2, 768, 768], P(None, 'mp')
- grad_up_weight: float32 [2, 768, 3072], P(None, None, 'mp')
- grad_up_bias: float32 [2, 3072], P(None, 'mp')
- grad_down_weight: float32 [2, 3072, 768], P(None, 'mp')
- grad_gains: float32 [2, 2, 768], replicated
- grad_biases: float32 [2, 4, 768], replicated
The draws below stay inside these ranges and needn't reach their ends.
Inputs may be any that keep to these rules, and one draw needn't show every extreme that they name: Documents are contiguous runs that cover all 16384 tokens in order; for every token i, doc_bounds[0, i] is the first token of its document and doc_bounds[1, i] one past its last. One document holds 8192 tokens and starts at token 4096; the document right after it holds exactly 2048; every other holds at most 2048.
All inputs are finite; a program needn't handle non-finite values.
Results may differ from the reference program's by a relative error of at most 0.023.
Values may be sent and summed in bfloat16 or wider, within the bound.
A program may use at most 192 MiB of HBM per device.

```python
import jax
import jax.numpy as jnp
from jax import lax

D = 768
HEADS = 12
HEAD_DIM = 64
FF = 3072
LAYERS = 2
SCORE_ROWS = 512
WINDOW = 64
POOL_REACH = 64
DOC_MOST = 2048
LONG_DOC = 8192
TOKENS = 16384


def region_docs(key, begin, finish_at, first_exact):
    doc_count = (finish_at - begin) // (DOC_MOST // 2) + 2
    lengths = jax.random.randint(key, (doc_count,), DOC_MOST // 2, DOC_MOST + 1, dtype=jnp.int32)
    if first_exact:
        lengths = lengths.at[0].set(DOC_MOST)
    ends = jnp.minimum(begin + jnp.cumsum(lengths).astype(jnp.int32), finish_at).astype(jnp.int32)
    firsts = jnp.concatenate([jnp.full((1,), begin, jnp.int32), ends[:-1]])
    return (firsts, ends)


def draw_doc_bounds(key, part):
    long_start = TOKENS // 2 - LONG_DOC // 2
    long_end = long_start + LONG_DOC
    front_first, front_end = region_docs(jax.random.fold_in(key, 11), 0, long_start, False)
    back_first, back_end = region_docs(jax.random.fold_in(key, 12), long_end, TOKENS, True)
    starts = jnp.concatenate([front_first, jnp.full((1,), long_start, jnp.int32), back_first])
    finish = jnp.concatenate([front_end, jnp.full((1,), long_end, jnp.int32), back_end])
    places = jnp.arange(TOKENS, dtype=jnp.int32)
    inside = (places[:, None] >= starts[None]) & (places[:, None] < finish[None])
    first_token = jnp.sum(jnp.where(inside, starts[None], 0), axis=1)
    past_end = jnp.sum(jnp.where(inside, finish[None], 0), axis=1)
    return jnp.stack([first_token, past_end]).astype(jnp.int32)


def block_levels(stream_key, dims, cuts, smallest, largest):
    gain = 1.0
    for axis_at, blocks in cuts:
        draws = jax.random.uniform(jax.random.fold_in(jax.random.fold_in(stream_key, 6), axis_at), (blocks,), jnp.float32, smallest / len(cuts), largest / len(cuts))
        gain = gain * jnp.repeat(jnp.exp(draws), dims[axis_at] // blocks).reshape((-1,) + (1,) * (len(dims) - 1 - axis_at))
    return gain


def gaussian(stream_key, extent, scale, limit, pieces=(), kind=jnp.bfloat16):
    loudness = block_levels(stream_key, extent, pieces, -0.22, 0.18) if pieces else 1.0
    values = jax.random.normal(stream_key, extent, jnp.float32) * scale * loudness
    return jnp.minimum(jnp.maximum(values, -limit), limit).astype(kind)


def setup_inputs(seed: int = 0) -> dict:
    streams_of = jax.random.split(jax.random.key(seed), 14)
    inputs = gaussian(streams_of[0], (TOKENS, D), 1.0, 6.0, ((0, 32),))
    doc_bounds = draw_doc_bounds(jax.random.fold_in(streams_of[13], 71), 0)
    qkv_weight = gaussian(streams_of[2], (LAYERS, 3, D, D), D ** -0.5, 0.21875, ((3, 4),))
    qv_bias = gaussian(streams_of[3], (LAYERS, 2, D), 0.3, 1.8, ((2, 4),), jnp.float32)
    conv_weight = gaussian(streams_of[4], (LAYERS, 2, 5, D), 0.45, 2.7, ((3, 4),), jnp.float32)
    conv_bias = gaussian(streams_of[5], (LAYERS, 2, D), 0.3, 1.8, ((2, 4),), jnp.float32)
    out_weight = gaussian(streams_of[6], (LAYERS, D, D), (D // 64) ** -0.5, 1.75, ((1, 4),))
    up_weight = gaussian(streams_of[7], (LAYERS, D, FF), D ** -0.5, 0.21875, ((2, 4),))
    up_bias = gaussian(streams_of[8], (LAYERS, FF), 0.3, 1.8, ((1, 4),), jnp.float32)
    down_weight = gaussian(streams_of[9], (LAYERS, FF, D), FF ** -0.5, 0.109375, ((1, 4),))
    norm_gains = jnp.clip(1.0 + 0.1 * jax.random.normal(streams_of[10], (LAYERS, 2, D), jnp.float32), 0.5, 1.5)
    shared_biases = gaussian(streams_of[11], (LAYERS, 4, D), 0.3, 1.8, (), jnp.float32)
    cotangent = gaussian(streams_of[12], (TOKENS, D), 1.0, 6.0, ((0, 32),))
    return dict(inputs=inputs, doc_bounds=doc_bounds, qkv_weight=qkv_weight, qv_bias=qv_bias, conv_weight=conv_weight, conv_bias=conv_bias, out_weight=out_weight, up_weight=up_weight, up_bias=up_bias, down_weight=down_weight, norm_gains=norm_gains, shared_biases=shared_biases, cotangent=cotangent)


@jax.custom_vjp
def low(v):
    return lax.optimization_barrier(v.astype(jnp.bfloat16)).astype(jnp.float32)

@jax.custom_vjp
def low_back(v):
    return v

def low_keep(v):
    return (low(v), None)

def low_pass(kept, grad):
    return (grad,)

def back_keep(v):
    return (v, None)

def back_low(kept, grad):
    return (low(grad),)
low.defvjp(low_keep, low_pass)
low_back.defvjp(back_keep, back_low)
NORM_EPSILON = 1e-05
HIGHEST_PRECISION = lax.Precision.HIGHEST

def layer_norm(values, scale_gain, offset):
    average = lax.optimization_barrier(jnp.mean(values, axis=-1, keepdims=True))
    centered = values - average
    spread = lax.optimization_barrier(jnp.mean(centered * centered, axis=-1, keepdims=True))
    return centered * lax.rsqrt(spread + NORM_EPSILON) * scale_gain + offset

def exact_gelu(values):
    return jax.nn.gelu(values, approximate=False)

def matmul_high(left, right):
    return jnp.dot(left, right, precision=HIGHEST_PRECISION, preferred_element_type=jnp.float32)

def allowed_keys(first_row, starts, finish):
    row_ids = first_row + jnp.arange(SCORE_ROWS, dtype=jnp.int32)
    window_ids = first_row - WINDOW + jnp.arange(SCORE_ROWS + 2 * WINDOW, dtype=jnp.int32)
    pooled_ids = 4 * (first_row // 4 - POOL_REACH + jnp.arange(SCORE_ROWS // 4 + 2 * POOL_REACH, dtype=jnp.int32))
    near_rows = jnp.abs(row_ids[:, None] - window_ids[None]) <= WINDOW
    same_doc = (window_ids[None] >= starts[:, None]) & (window_ids[None] < finish[:, None])
    near_pooled = jnp.abs(row_ids[:, None] - pooled_ids[None]) <= 4 * POOL_REACH
    same_pooled = (pooled_ids[None] >= starts[:, None]) & (pooled_ids[None] < finish[:, None])
    return jnp.concatenate([near_rows & same_doc, near_pooled & same_pooled], axis=1)

def pool_conv(values, tap_weights, starts, finish):
    total = values.shape[0]
    padded = jnp.pad(values, ((2, 2), (0, 0)))
    leading = padded[:total].reshape(total // 4, 4, -1)
    trailing = padded[4:total + 4].reshape(total // 4, 4, -1)[:, :1]
    tap_values = jnp.concatenate([leading, trailing], axis=1)
    places = 4 * jnp.arange(total // 4, dtype=jnp.int32)[:, None] + jnp.arange(5, dtype=jnp.int32)[None] - 2
    first_token = starts.reshape(-1, 4)[:, 0]
    past_end = finish.reshape(-1, 4)[:, 0]
    tap_keep = (places >= first_token[:, None]) & (places < past_end[:, None])
    tap_values = jnp.where(tap_keep[:, :, None], tap_values, 0.0)
    return lax.optimization_barrier(jnp.sum(tap_values * tap_weights[None], axis=1))

def split_heads(rows):
    return rows.reshape(rows.shape[0], HEADS, HEAD_DIM)

def attend(queries, key_rows, value_rows, pooled_keys, pooled_values, starts, finish):
    total = queries.shape[0]
    score_scale = HEAD_DIM ** (-0.5)
    key_pad = jnp.pad(key_rows, ((WINDOW, WINDOW), (0, 0), (0, 0)))
    value_pad = jnp.pad(value_rows, ((WINDOW, WINDOW), (0, 0), (0, 0)))
    pooled_key_pad = jnp.pad(pooled_keys, ((POOL_REACH, POOL_REACH), (0, 0), (0, 0)))
    pooled_value_pad = jnp.pad(pooled_values, ((POOL_REACH, POOL_REACH), (0, 0), (0, 0)))

    def one_block(block_index):
        row_zero = block_index * SCORE_ROWS
        query_block = lax.dynamic_slice_in_dim(queries, row_zero, SCORE_ROWS, 0)
        key_block = jnp.concatenate([lax.dynamic_slice_in_dim(key_pad, row_zero, SCORE_ROWS + 2 * WINDOW, 0), lax.dynamic_slice_in_dim(pooled_key_pad, row_zero // 4, SCORE_ROWS // 4 + 2 * POOL_REACH, 0)], axis=0)
        value_block = jnp.concatenate([lax.dynamic_slice_in_dim(value_pad, row_zero, SCORE_ROWS + 2 * WINDOW, 0), lax.dynamic_slice_in_dim(pooled_value_pad, row_zero // 4, SCORE_ROWS // 4 + 2 * POOL_REACH, 0)], axis=0)
        allowed = allowed_keys(row_zero, lax.dynamic_slice_in_dim(starts, row_zero, SCORE_ROWS, 0), lax.dynamic_slice_in_dim(finish, row_zero, SCORE_ROWS, 0))
        scores = low_back(jnp.einsum('qhe,khe->hqk', query_block, key_block, precision=HIGHEST_PRECISION) * score_scale)
        masked = jnp.where(allowed[None], scores, -1e+30)
        log_total = jax.nn.logsumexp(masked, axis=-1, keepdims=True)
        weights = low(jnp.exp(masked - log_total))
        return jnp.einsum('hqk,khe->qhe', weights, value_block, precision=HIGHEST_PRECISION)
    mixed = lax.map(jax.checkpoint(one_block), jnp.arange(total // SCORE_ROWS, dtype=jnp.int32))
    return mixed.reshape(total, -1)

def one_layer(hidden, starts, finish, qkv_layer, qv_layer, conv_layer, conv_bias_layer, out_layer, up_layer, up_bias_layer, down_layer, gains, biases):
    entry = low(hidden)
    queries = low(low_back(matmul_high(entry, qkv_layer[0])) + qv_layer[0])
    key_rows = low(low_back(matmul_high(entry, qkv_layer[1])))
    value_rows = low(low_back(matmul_high(entry, qkv_layer[2])) + qv_layer[1])
    pooled_keys = low(pool_conv(key_rows, conv_layer[0], starts, finish) + conv_bias_layer[0])
    pooled_values = low(pool_conv(value_rows, conv_layer[1], starts, finish) + conv_bias_layer[1])
    mixed = attend(split_heads(queries), split_heads(key_rows), split_heads(value_rows), split_heads(pooled_keys), split_heads(pooled_values), starts, finish)
    mixed = low_back(low(mixed))
    resid = hidden + (low_back(matmul_high(mixed, out_layer)) + biases[0])
    normed = layer_norm(resid, gains[0], biases[1])
    pre = low_back(matmul_high(low(normed), up_layer)) + up_bias_layer
    act = low(exact_gelu(pre))
    middle = normed + (low_back(matmul_high(act, down_layer)) + biases[2])
    return layer_norm(middle, gains[1], biases[3])

def reference(inputs, doc_bounds, qkv_weight, qv_bias, conv_weight, conv_bias, out_weight, up_weight, up_bias, down_weight, norm_gains, shared_biases, cotangent):
    starts = doc_bounds[0]
    finish = doc_bounds[1]

    def run(hidden, qkv_all, qv_all, conv_weights, conv_biases, out_all, up_all, up_biases, down_all, gains_all, biases_all):
        for layer_index in range(LAYERS):
            hidden = one_layer(hidden, starts, finish, qkv_all[layer_index], qv_all[layer_index], conv_weights[layer_index], conv_biases[layer_index], out_all[layer_index], up_all[layer_index], up_biases[layer_index], down_all[layer_index], gains_all[layer_index], biases_all[layer_index])
        return hidden
    result, pullback = jax.vjp(run, inputs.astype(jnp.float32), qkv_weight.astype(jnp.float32), qv_bias, conv_weight, conv_bias, out_weight.astype(jnp.float32), up_weight.astype(jnp.float32), up_bias, down_weight.astype(jnp.float32), norm_gains, shared_biases)
    grads = pullback(cotangent.astype(jnp.float32))
    return (result, grads[0], grads[1], grads[2], grads[3], grads[4], grads[5], grads[6], grads[7], grads[8], grads[9], grads[10])
```

```python
import jax
import jax.numpy as jnp
from jax import lax
from jax.experimental import pallas as pl
from jax.experimental.pallas import tpu as pltpu
from jax.sharding import PartitionSpec as P

HEAD_DIM = 64
LAYERS = 2
WINDOW = 64
POOL_REACH = 64
NORM_EPSILON = 1e-05
LEFT = 320
LEFT_SENT = 272
RIGHT = 256
BOTH = ("seq", "mp")
BF16 = jnp.bfloat16
F32 = jnp.float32


def product(left, right):
    return jnp.dot(left, right, preferred_element_type=F32)


def product_left_t(left, right):
    return lax.dot_general(left, right, (((0,), (0,)), ((), ())), preferred_element_type=F32)


def product_right_t(left, right):
    return lax.dot_general(left, right, (((1,), (1,)), ((), ())), preferred_element_type=F32)


def swap(values, axis, bit):
    count = lax.axis_size(axis)
    return lax.ppermute(values, axis, [(i, i ^ bit) for i in range(count)])


def shift(values, step):
    count = lax.axis_size("seq") * lax.axis_size("mp")
    return lax.ppermute(
        values, BOTH, [(i, i + step) for i in range(count) if 0 <= i + step < count]
    )


def gather_parts(own):
    across = swap(own, "mp", 2)
    return [own, swap(own, "mp", 1), across, swap(across, "mp", 1)]


def gather_small(own):
    return gather_parts(own)


def norm_forward(values, gain, offset):
    average = jnp.mean(values, axis=-1, keepdims=True)
    centered = values - average
    spread = jnp.mean(centered * centered, axis=-1, keepdims=True)
    inverse = lax.rsqrt(spread + NORM_EPSILON)
    unit = centered * inverse
    return unit * gain + offset, unit, inverse


def norm_backward(grad, unit, inverse, gain):
    scaled = grad * gain
    result = (
        scaled
        - jnp.mean(scaled, axis=-1, keepdims=True)
        - unit * jnp.mean(scaled * unit, axis=-1, keepdims=True)
    ) * inverse
    return result, jnp.sum(grad * unit, axis=0), jnp.sum(grad, axis=0)


def with_halo(rows):
    left = shift(rows[rows.shape[0] - LEFT_SENT :], 1)
    right = shift(rows[:RIGHT], -1)
    empty = jnp.zeros((LEFT - LEFT_SENT, rows.shape[1]), rows.dtype)
    return jnp.concatenate([empty, left, rows, right], axis=0)


def tap_mask(starts, finish, base_row):
    count = starts.shape[0] // 4
    reach = (POOL_REACH,)
    first = jnp.concatenate(
        [
            jnp.broadcast_to(starts[:1], reach),
            starts.reshape(count, 4)[:, 0],
            jnp.broadcast_to(starts[-1:], reach),
        ]
    )
    past = jnp.concatenate(
        [
            jnp.broadcast_to(finish[:1], reach),
            finish.reshape(count, 4)[:, 0],
            jnp.broadcast_to(finish[-1:], reach),
        ]
    )
    places = (
        base_row
        + 4 * (jnp.arange(count + 2 * POOL_REACH, dtype=jnp.int32)[:, None] - POOL_REACH)
        + jnp.arange(5, dtype=jnp.int32)[None]
        - 2
    )
    return (places >= first[:, None]) & (places < past[:, None])


PAIR = 128
TILE = 128
SPAN = TILE + 2 * WINDOW
POOL_SPAN = TILE // 4 + 2 * POOL_REACH
FAR = -1e30


def tile_bias(tile, first, past):
    lane = lax.broadcasted_iota(jnp.int32, (1, TILE), 1) + tile * TILE
    near = lax.broadcasted_iota(jnp.int32, (SPAN, 1), 0) + (tile * TILE - WINDOW)
    far = 4 * (lax.broadcasted_iota(jnp.int32, (POOL_SPAN, 1), 0) + (tile * (TILE // 4) - POOL_REACH))

    def one(keys, reach):
        low = jnp.maximum(lane - reach, first)
        high = jnp.minimum(lane + reach + 1, past)
        return jnp.where((keys >= low) & (keys < high), 0.0, FAR)

    return jnp.concatenate([one(near, WINDOW), one(far, 4 * POOL_REACH)], axis=0)


def pair_mask():
    return lax.broadcasted_iota(jnp.int32, (1, PAIR), 1) < HEAD_DIM


def stacked(rows):
    left = pair_mask()
    zero = jnp.zeros_like(rows)
    return jnp.concatenate([jnp.where(left, rows, zero), jnp.where(left, zero, rows)], axis=0)


def keys_of(wide_ref, pooled_ref, tile, lanes):
    near = wide_ref[pl.ds(pl.multiple_of(LEFT - WINDOW + tile * TILE, TILE), SPAN), lanes]
    far = pooled_ref[pl.ds(pl.multiple_of(tile * (TILE // 4), TILE // 4), POOL_SPAN), lanes]
    return jnp.concatenate([near, far], axis=0)


def unstack(both):
    return jnp.concatenate([both[:HEAD_DIM, :TILE], both[HEAD_DIM:, TILE:]], axis=0)


def pool_into(wide_ref, wide_f32, keep_ref, conv_ref, conv_bias_ref, which, pooled_ref):
    count = pooled_ref.shape[0]
    begin = LEFT - 4 * POOL_REACH - 2
    for pair in range(pooled_ref.shape[1] // PAIR):
        lanes = slice(pair * PAIR, (pair + 1) * PAIR)
        wide_f32[...] = wide_ref[:, lanes].astype(F32)
        total = jnp.broadcast_to(conv_bias_ref[which : which + 1, lanes], (count, PAIR))
        for tap in range(5):
            rows = wide_f32[pl.ds(begin + tap, count, stride=4), :]
            kept = jnp.where(keep_ref[:, tap : tap + 1] > 0.0, rows, 0.0)
            total = total + kept * conv_ref[which, tap : tap + 1, lanes]
        pooled_ref[:, lanes] = total.astype(BF16)


def attend_forward_kernel(
    q_ref, k_ref, v_ref, first_ref, past_ref, keep_ref, conv_ref, conv_bias_ref,
    mixed_ref, lse_ref, pooled_k_ref, pooled_v_ref, wide_f32,
):
    pool_into(k_ref, wide_f32, keep_ref, conv_ref, conv_bias_ref, 0, pooled_k_ref)
    pool_into(v_ref, wide_f32, keep_ref, conv_ref, conv_bias_ref, 1, pooled_v_ref)
    pairs = q_ref.shape[1] // PAIR

    @pl.loop(0, q_ref.shape[0] // TILE)
    def _(tile):
        rows = pl.ds(pl.multiple_of(tile * TILE, TILE), TILE)
        bias = tile_bias(tile, first_ref[tile], past_ref[tile])
        bias = jnp.concatenate([bias, bias], axis=1)
        for pair in range(pairs):
            lanes = slice(pair * PAIR, (pair + 1) * PAIR)
            query = stacked(q_ref[rows, lanes] * BF16(HEAD_DIM**-0.5))
            key = keys_of(k_ref, pooled_k_ref, tile, lanes)
            value = keys_of(v_ref, pooled_v_ref, tile, lanes)
            scores = product_right_t(key, query) + bias
            most = jnp.max(scores, axis=0, keepdims=True)
            weight = jnp.exp(scores - most)
            total = jnp.sum(weight, axis=0, keepdims=True)
            both = product_left_t(value, weight.astype(BF16)) * (1.0 / total)
            mixed_ref[rows, lanes] = unstack(both).T.astype(BF16)
            lse_ref[tile, pair : pair + 1, :] = most + jnp.log(total)


def attend_backward_kernel(
    q_ref, k_ref, v_ref, pooled_k_ref, pooled_v_ref, grad_ref, lse_ref,
    first_ref, past_ref, keep_ref, conv_ref,
    grad_q_ref, grad_k_ref, grad_v_ref, small_ref,
    wide_k, wide_v, far_k, far_v, wide_f32,
):
    pairs = q_ref.shape[1] // PAIR
    wide_k[...] = jnp.zeros_like(wide_k)
    wide_v[...] = jnp.zeros_like(wide_v)
    far_k[...] = jnp.zeros_like(far_k)
    far_v[...] = jnp.zeros_like(far_v)
    small_ref[...] = jnp.zeros_like(small_ref)

    @pl.loop(0, q_ref.shape[0] // TILE)
    def _(tile):
        rows = pl.ds(pl.multiple_of(tile * TILE, TILE), TILE)
        near = pl.ds(pl.multiple_of(LEFT - WINDOW + tile * TILE, TILE), SPAN)
        far = pl.ds(pl.multiple_of(tile * (TILE // 4), TILE // 4), POOL_SPAN)
        bias = tile_bias(tile, first_ref[tile], past_ref[tile])
        bias = jnp.concatenate([bias, bias], axis=1)
        for pair in range(pairs):
            lanes = slice(pair * PAIR, (pair + 1) * PAIR)
            query = stacked(q_ref[rows, lanes] * BF16(HEAD_DIM**-0.5))
            grad = stacked(grad_ref[rows, lanes])
            key = keys_of(k_ref, pooled_k_ref, tile, lanes)
            value = keys_of(v_ref, pooled_v_ref, tile, lanes)
            scores = product_right_t(key, query) + bias
            probs = jnp.exp(scores - lse_ref[tile, pair : pair + 1, :])
            grad_probs = product_right_t(value, grad)
            delta = jnp.sum(probs * grad_probs, axis=0, keepdims=True)
            grad_scores = (probs * (grad_probs - delta)).astype(BF16)
            grad_value = product(probs.astype(BF16), grad)
            grad_key = product(grad_scores, query)
            wide_v[pair, near, :] += grad_value[:SPAN]
            far_v[far, lanes] += grad_value[SPAN:]
            wide_k[pair, near, :] += grad_key[:SPAN]
            far_k[far, lanes] += grad_key[SPAN:]
            grad_query = unstack(product_left_t(key, grad_scores)).T * (HEAD_DIM**-0.5)
            grad_q_ref[rows, lanes] = grad_query.astype(BF16)
            small_ref[0:1, lanes] += jnp.sum(grad_query, axis=0, keepdims=True)

    count = far_k.shape[0]
    begin = LEFT - 4 * POOL_REACH - 2
    for which, (source, wide, pooled, result) in enumerate(
        ((k_ref, wide_k, far_k, grad_k_ref), (v_ref, wide_v, far_v, grad_v_ref))
    ):
        for pair in range(pairs):
            lanes = slice(pair * PAIR, (pair + 1) * PAIR)
            wide_f32[...] = source[:, lanes].astype(F32)
            grad = pooled[:, lanes]
            at = 12 + which
            small_ref[at : at + 1, lanes] = jnp.sum(grad, axis=0, keepdims=True)
            for tap in range(5):
                places = pl.ds(begin + tap, count, stride=4)
                kept = jnp.where(keep_ref[:, tap : tap + 1] > 0.0, grad, 0.0)
                at = 2 + 5 * which + tap
                small_ref[at : at + 1, lanes] = jnp.sum(
                    kept * wide_f32[places, :], axis=0, keepdims=True
                )
                wide[pair, places, :] += kept * conv_ref[which, tap : tap + 1, lanes]
            if which == 1:
                small_ref[1:2, lanes] = jnp.sum(wide[pair], axis=0, keepdims=True)
            result[:, lanes] = wide[pair].astype(BF16)


def in_vmem(count):
    return [pl.BlockSpec(memory_space=pltpu.VMEM)] * count


VMEM_LIMIT = 56 * 1024 * 1024


def attend_forward(queries, keys, values, first, past, keep, conv, conv_bias):
    total, width = queries.shape
    count = total // 4 + 2 * POOL_REACH
    shape = jax.ShapeDtypeStruct
    return pl.pallas_call(
        attend_forward_kernel,
        out_shape=(
            shape((total, width), BF16),
            shape((total // TILE, width // PAIR, 2 * TILE), F32),
            shape((count, width), BF16),
            shape((count, width), BF16),
        ),
        in_specs=in_vmem(8),
        out_specs=tuple(in_vmem(4)),
        scratch_shapes=[pltpu.VMEM((keys.shape[0], PAIR), F32)],
        compiler_params=pltpu.CompilerParams(vmem_limit_bytes=VMEM_LIMIT),
        name="attend_forward",
    )(queries, keys, values, first, past, keep, conv, conv_bias)


def attend_backward(queries, keys, values, pooled_k, pooled_v, grad, lse, first, past, keep, conv):
    total, width = queries.shape
    shape = jax.ShapeDtypeStruct
    return pl.pallas_call(
        attend_backward_kernel,
        out_shape=(
            shape((total, width), BF16),
            shape(keys.shape, BF16),
            shape(keys.shape, BF16),
            shape((16, width), F32),
        ),
        in_specs=in_vmem(11),
        out_specs=tuple(in_vmem(4)),
        scratch_shapes=[
            pltpu.VMEM((width // PAIR, keys.shape[0], PAIR), F32),
            pltpu.VMEM((width // PAIR, keys.shape[0], PAIR), F32),
            pltpu.VMEM(pooled_k.shape, F32),
            pltpu.VMEM(pooled_k.shape, F32),
            pltpu.VMEM((keys.shape[0], PAIR), F32),
        ],
        compiler_params=pltpu.CompilerParams(vmem_limit_bytes=VMEM_LIMIT),
        name="attend_backward",
    )(queries, keys, values, pooled_k, pooled_v, grad, lse, first, past, keep, conv)


def gelu_parts(pre):
    size = jnp.abs(pre) * (0.5**0.5)
    t = 1.0 / (1.0 + 0.5 * size)
    series = 0.17087277
    for term in (-0.82215223, 1.48851587, -1.13520398, 0.27886807, -0.18628806, 0.09678418,
                 0.37409196, 1.00002368, -1.26551223):
        series = series * t + term
    tail = 0.5 * t * jnp.exp(series - size * size)
    cdf = jnp.where(pre < 0.0, tail, 1.0 - tail)
    density = jnp.exp(-0.5 * pre * pre) * (0.5 / jnp.pi) ** 0.5
    return pre * cdf, cdf + pre * density


def layer_forward(hidden, masks, weights):
    first, past, keep = masks
    qkv, qv, conv, conv_bias, out, up, up_bias, down, gains, biases = weights
    total = hidden.shape[0]
    entry_wide = with_halo(hidden.astype(BF16))
    entry = entry_wide[LEFT : LEFT + total]
    queries = (product(entry, qkv[0]) + qv[0]).astype(BF16)
    keys = product(entry_wide, qkv[1]).astype(BF16)
    values = (product(entry_wide, qkv[2]) + qv[1]).astype(BF16)

    mixed, lse, pooled_k, pooled_v = attend_forward(
        queries, keys, values, first, past, keep, conv, conv_bias
    )
    resid = hidden + (product(mixed, out) + biases[0])
    normed, unit_one, inverse_one = norm_forward(resid, gains[0], biases[1])
    normed_low = normed.astype(BF16)
    pre = product(normed_low, up) + up_bias
    act, slope = gelu_parts(pre)
    act, slope = act.astype(BF16), slope.astype(BF16)
    middle = normed + (product(act, down) + biases[2])
    result, unit_two, inverse_two = norm_forward(middle, gains[1], biases[3])
    saved = (
        entry_wide,
        queries,
        keys,
        values,
        pooled_k,
        pooled_v,
        mixed,
        lse,
        unit_one,
        inverse_one,
        normed_low,
        act,
        slope,
        unit_two,
        inverse_two,
    )
    return result, saved


def split_rows(values):
    return jnp.split(values, 4, axis=0)


def reduce_parts(parts):
    sent = jnp.stack([parts[1], parts[3]]).astype(BF16)
    received = swap(sent, "mp", 1).astype(F32)
    own = parts[0] + received[0]
    across = parts[2] + received[1]
    own = own + swap(across.astype(BF16), "mp", 2).astype(F32)
    place = lax.axis_index("seq")
    count = lax.axis_size("seq")
    bit = 1
    while bit < count:
        half = own.shape[0] // 2
        side = (place // bit) % 2
        kept = lax.dynamic_slice_in_dim(own, side * half, half, 0)
        given = lax.dynamic_slice_in_dim(own, (1 - side) * half, half, 0).astype(BF16)
        own = kept + swap(given, "seq", bit).astype(F32)
        bit *= 2
    whole = own.astype(BF16)
    while bit > 1:
        bit //= 2
        side = (place // bit) % 2
        other = swap(whole, "seq", bit)
        whole = jnp.where(
            side == 0,
            jnp.concatenate([whole, other], axis=0),
            jnp.concatenate([other, whole], axis=0),
        )
    return whole


def layer_backward(grad_out, masks, weights, saved):
    first, past, keep = masks
    qkv, qv, conv, conv_bias, out, up, up_bias, down, gains, biases = weights
    (
        entry_wide,
        queries,
        keys,
        values,
        pooled_k,
        pooled_v,
        mixed,
        lse,
        unit_one,
        inverse_one,
        normed_low,
        act,
        slope,
        unit_two,
        inverse_two,
    ) = saved
    total, width = queries.shape
    grad_middle, gain_two, shift_two = norm_backward(grad_out, unit_two, inverse_two, gains[1])
    bias_down = jnp.sum(grad_middle, axis=0)
    grad_middle_low = grad_middle.astype(BF16)
    grad_w_down = product_left_t(act, grad_middle_low)
    grad_pre = product_right_t(grad_middle_low, down) * slope.astype(F32)
    grad_b_up = jnp.sum(grad_pre, axis=0)
    grad_pre_low = grad_pre.astype(BF16)
    grad_w_up_t = product_left_t(grad_pre_low, normed_low)
    feed_parts = [
        jnp.concatenate(pair, axis=0)
        for pair in zip(split_rows(grad_w_down), split_rows(grad_w_up_t))
    ]
    feed = reduce_parts(feed_parts)
    grad_normed = product_right_t(grad_pre_low, up) + grad_middle
    grad_resid, gain_one, shift_one = norm_backward(grad_normed, unit_one, inverse_one, gains[0])
    bias_out = jnp.sum(grad_resid, axis=0)
    grad_resid_low = grad_resid.astype(BF16)
    grad_w_out = product_left_t(mixed, grad_resid_low)
    grad_mixed = product_right_t(grad_resid_low, out).astype(BF16)
    grad_q_low, grad_k_low, grad_v_low, small = attend_backward(
        queries, keys, values, pooled_k, pooled_v, grad_mixed, lse, first, past, keep, conv
    )
    entry = entry_wide[LEFT : LEFT + total]
    w_q = product_left_t(grad_q_low, entry)
    w_k = product_left_t(grad_k_low, entry_wide)
    w_v = product_left_t(grad_v_low, entry_wide)
    rest_parts = [
        jnp.concatenate(pieces, axis=0)
        for pieces in zip(*(split_rows(piece) for piece in (grad_w_out, w_q, w_k, w_v)))
    ]
    rest = reduce_parts(rest_parts)
    wide_grad = product_right_t(grad_k_low, qkv[1]) + product_right_t(grad_v_low, qkv[2])
    from_right = shift(wide_grad[LEFT - LEFT_SENT : LEFT].astype(BF16), -1).astype(F32)
    from_left = shift(wide_grad[LEFT + total :].astype(BF16), 1).astype(F32)
    grad_hidden = (
        product_right_t(grad_q_low, qkv[0])
        + wide_grad[LEFT : LEFT + total]
        + grad_resid
        + jnp.pad(from_right, ((total - LEFT_SENT, 0), (0, 0)))
        + jnp.pad(from_left, ((0, total - RIGHT), (0, 0)))
    )
    grad_b_up_rows = grad_b_up.reshape(4, -1, width // 4).transpose(1, 0, 2).reshape(-1, width)
    small_split = jnp.concatenate([small[:14], grad_b_up_rows], axis=0)
    small_whole = jnp.stack([gain_one, gain_two, bias_out, shift_one, bias_down, shift_two])
    return grad_hidden, feed, rest, small_split, small_whole


def to_absolute(rows):
    quarter = rows.shape[1] // 4
    parts = [rows[:, k * quarter : (k + 1) * quarter] for k in range(4)]
    place = lax.axis_index("mp")
    odd, high = place % 2 == 1, place // 2 == 1
    parts = [jnp.where(odd, parts[k ^ 1], parts[k]) for k in range(4)]
    parts = [jnp.where(high, parts[k ^ 2], parts[k]) for k in range(4)]
    return jnp.concatenate(parts, axis=1)


def shards(
    inputs,
    doc_bounds,
    qkv_weight,
    qv_bias,
    conv_weight,
    conv_bias,
    out_weight,
    up_weight,
    up_bias,
    down_weight,
    norm_gains,
    shared_biases,
    cotangent,
):
    total, width = inputs.shape
    place = lax.axis_index("mp")
    base_row = lax.axis_index("seq") * doc_bounds.shape[1] + place * total
    bounds = lax.dynamic_slice_in_dim(doc_bounds, place * total, total, 1)
    keep = jnp.pad(tap_mask(bounds[0], bounds[1], base_row).astype(F32), ((0, 0), (0, 3)))
    near_bounds = (bounds - base_row).reshape(2, total // TILE, 1, TILE)
    masks = (near_bounds[0], near_bounds[1], keep)
    quarter = width // 4
    small = jnp.concatenate(
        [
            qv_bias.reshape(-1, quarter),
            conv_weight.reshape(-1, quarter),
            conv_bias.reshape(-1, quarter),
            up_bias.reshape(-1, quarter),
        ],
        axis=0,
    )
    small = gather_small(small)
    layers = []
    for index in range(LAYERS):
        qkv = jnp.concatenate(gather_parts(qkv_weight[index]), axis=2)
        out = jnp.concatenate(gather_parts(out_weight[index]), axis=0)
        up = jnp.concatenate(gather_parts(up_weight[index]), axis=1)
        down = jnp.concatenate(gather_parts(down_weight[index]), axis=0)
        layers.append((qkv, out, up, down))
    wide_small = jnp.concatenate(small, axis=1)
    qv_all = wide_small[:4].reshape(2, 2, width)
    conv_all = wide_small[4:24].reshape(2, 2, 5, width)
    conv_bias_all = wide_small[24:28].reshape(2, 2, width)
    up_bias_all = jnp.stack([part[28:].reshape(2, -1) for part in small], axis=1).reshape(2, -1)
    hidden = inputs.astype(F32)
    stack = []
    for index in range(LAYERS):
        qkv, out, up, down = layers[index]
        weights = (
            qkv,
            qv_all[index],
            conv_all[index],
            conv_bias_all[index],
            out,
            up,
            up_bias_all[index],
            down,
            norm_gains[index],
            shared_biases[index],
        )
        hidden, saved = layer_forward(hidden, masks, weights)
        stack.append((weights, saved))
    gradient = cotangent.astype(F32)
    collected = [None] * LAYERS
    for index in reversed(range(LAYERS)):
        weights, saved = stack[index]
        gradient, feed, rest, split, whole = layer_backward(gradient, masks, weights, saved)
        collected[index] = (feed, rest, split, whole)
    feed = jnp.stack([part[0] for part in collected]).astype(F32)
    rest = jnp.stack([part[1] for part in collected]).astype(F32)
    small_split = jnp.stack([to_absolute(part[2]) for part in collected])
    small_whole = jnp.stack([part[3] for part in collected])
    small_total = lax.psum(jnp.concatenate([small_split, small_whole], axis=1), BOTH)
    own_small = lax.dynamic_slice_in_dim(small_total[:, :18], place * quarter, quarter, 2)
    units = down_weight.shape[1]
    return (
        hidden,
        gradient,
        rest[:, quarter:].reshape(2, 3, quarter, width).transpose(0, 1, 3, 2),
        own_small[:, :2],
        own_small[:, 2:12].reshape(2, 2, 5, quarter),
        own_small[:, 12:14],
        rest[:, :quarter],
        feed[:, units:].transpose(0, 2, 1),
        own_small[:, 14:18].reshape(2, -1),
        feed[:, :units],
        small_total[:, 18:20],
        small_total[:, 20:24],
    )


def solution(mesh):
    return jax.shard_map(
        shards,
        mesh=mesh,
        in_specs=(
            P(BOTH, None),
            P(None, "seq"),
            P(None, None, None, "mp"),
            P(None, None, "mp"),
            P(None, None, None, "mp"),
            P(None, None, "mp"),
            P(None, "mp", None),
            P(None, None, "mp"),
            P(None, "mp"),
            P(None, "mp", None),
            P(),
            P(),
            P(BOTH, None),
        ),
        out_specs=(
            P(BOTH, None),
            P(BOTH, None),
            P(None, None, None, "mp"),
            P(None, None, "mp"),
            P(None, None, None, "mp"),
            P(None, None, "mp"),
            P(None, "mp", None),
            P(None, None, "mp"),
            P(None, "mp"),
            P(None, "mp", None),
            P(),
            P(),
        ),
        check_vma=False,
    )
```

```python
import functools

import jax
import jax.numpy as jnp
from jax import lax
from jax.experimental import pallas as pl
from jax.experimental.pallas import tpu as pltpu
from jax.sharding import PartitionSpec as P

HEAD_DIM = 64
LAYERS = 2
WINDOW = 64
POOL_REACH = 64
NORM_EPSILON = 1e-05
LEFT = 320
LEFT_SENT = 272
RIGHT = 256
BOTH = ("seq", "mp")
BF16 = jnp.bfloat16
F32 = jnp.float32


def product(left, right):
    return jnp.dot(left, right, preferred_element_type=F32)


def product_left_t(left, right):
    return lax.dot_general(left, right, (((0,), (0,)), ((), ())), preferred_element_type=F32)


def product_right_t(left, right):
    return lax.dot_general(left, right, (((1,), (1,)), ((), ())), preferred_element_type=F32)


def swap(values, axis, bit):
    count = lax.axis_size(axis)
    return lax.ppermute(values, axis, [(i, i ^ bit) for i in range(count)])


def shift(values, step):
    count = lax.axis_size("seq") * lax.axis_size("mp")
    return lax.ppermute(
        values, BOTH, [(i, i + step) for i in range(count) if 0 <= i + step < count]
    )


def gather_parts(own):
    across = swap(own, "mp", 2)
    return [own, swap(own, "mp", 1), across, swap(across, "mp", 1)]


def gather_small(own):
    return gather_parts(own)


def norm_forward(values, gain, offset):
    average = jnp.mean(values, axis=-1, keepdims=True)
    centered = values - average
    spread = jnp.mean(centered * centered, axis=-1, keepdims=True)
    inverse = lax.rsqrt(spread + NORM_EPSILON)
    unit = centered * inverse
    return unit * gain + offset, unit, inverse


def norm_backward(grad, unit, inverse, gain):
    scaled = grad * gain
    result = (
        scaled
        - jnp.mean(scaled, axis=-1, keepdims=True)
        - unit * jnp.mean(scaled * unit, axis=-1, keepdims=True)
    ) * inverse
    return result, jnp.sum(grad * unit, axis=0), jnp.sum(grad, axis=0)


def with_halo(rows):
    left = shift(rows[rows.shape[0] - LEFT_SENT :], 1)
    right = shift(rows[:RIGHT], -1)
    empty = jnp.zeros((LEFT - LEFT_SENT, rows.shape[1]), rows.dtype)
    return jnp.concatenate([empty, left, rows, right], axis=0)


def tap_mask(starts, finish, base_row):
    count = starts.shape[0] // 4
    reach = (POOL_REACH,)
    first = jnp.concatenate(
        [
            jnp.broadcast_to(starts[:1], reach),
            starts.reshape(count, 4)[:, 0],
            jnp.broadcast_to(starts[-1:], reach),
        ]
    )
    past = jnp.concatenate(
        [
            jnp.broadcast_to(finish[:1], reach),
            finish.reshape(count, 4)[:, 0],
            jnp.broadcast_to(finish[-1:], reach),
        ]
    )
    places = (
        base_row
        + 4 * (jnp.arange(count + 2 * POOL_REACH, dtype=jnp.int32)[:, None] - POOL_REACH)
        + jnp.arange(5, dtype=jnp.int32)[None]
        - 2
    )
    return (places >= first[:, None]) & (places < past[:, None])


PAIR = 128
TILE = 128
SPAN = TILE + 2 * WINDOW
POOL_SPAN = TILE // 4 + 2 * POOL_REACH
FAR = -1e30


def tile_bias(tile, first, past):
    lane = lax.broadcasted_iota(jnp.int32, (1, TILE), 1) + tile * TILE
    near = lax.broadcasted_iota(jnp.int32, (SPAN, 1), 0) + (tile * TILE - WINDOW)
    far = 4 * (lax.broadcasted_iota(jnp.int32, (POOL_SPAN, 1), 0) + (tile * (TILE // 4) - POOL_REACH))

    def one(keys, reach):
        low = jnp.maximum(lane - reach, first)
        high = jnp.minimum(lane + reach + 1, past)
        return jnp.where((keys >= low) & (keys < high), 0.0, FAR)

    return jnp.concatenate([one(near, WINDOW), one(far, 4 * POOL_REACH)], axis=0)


def pair_mask():
    return lax.broadcasted_iota(jnp.int32, (1, PAIR), 1) < HEAD_DIM


def stacked(rows):
    left = pair_mask()
    zero = jnp.zeros_like(rows)
    return jnp.concatenate([jnp.where(left, rows, zero), jnp.where(left, zero, rows)], axis=0)


def keys_of(wide_ref, pooled_ref, tile, lanes):
    near = wide_ref[pl.ds(pl.multiple_of(LEFT - WINDOW + tile * TILE, TILE), SPAN), lanes]
    far = pooled_ref[pl.ds(pl.multiple_of(tile * (TILE // 4), TILE // 4), POOL_SPAN), lanes]
    return jnp.concatenate([near, far], axis=0)


def unstack(both):
    return jnp.concatenate([both[:HEAD_DIM, :TILE], both[HEAD_DIM:, TILE:]], axis=0)


def pool_into(wide_ref, wide_f32, keep_ref, conv_ref, conv_bias_ref, which, pooled_ref):
    count = pooled_ref.shape[0]
    begin = LEFT - 4 * POOL_REACH - 2
    for pair in range(pooled_ref.shape[1] // PAIR):
        lanes = slice(pair * PAIR, (pair + 1) * PAIR)
        wide_f32[...] = wide_ref[:, lanes].astype(F32)
        total = jnp.broadcast_to(conv_bias_ref[which : which + 1, lanes], (count, PAIR))
        for tap in range(5):
            rows = wide_f32[pl.ds(begin + tap, count, stride=4), :]
            kept = jnp.where(keep_ref[:, tap : tap + 1] > 0.0, rows, 0.0)
            total = total + kept * conv_ref[which, tap : tap + 1, lanes]
        pooled_ref[:, lanes] = total.astype(BF16)


def attend_forward_kernel(
    q_ref, k_ref, v_ref, first_ref, past_ref, keep_ref, conv_ref, conv_bias_ref,
    mixed_ref, lse_ref, pooled_k_ref, pooled_v_ref, wide_f32,
):
    pool_into(k_ref, wide_f32, keep_ref, conv_ref, conv_bias_ref, 0, pooled_k_ref)
    pool_into(v_ref, wide_f32, keep_ref, conv_ref, conv_bias_ref, 1, pooled_v_ref)
    pairs = q_ref.shape[1] // PAIR

    @pl.loop(0, q_ref.shape[0] // TILE)
    def _(tile):
        rows = pl.ds(pl.multiple_of(tile * TILE, TILE), TILE)
        bias = tile_bias(tile, first_ref[tile], past_ref[tile])
        bias = jnp.concatenate([bias, bias], axis=1)
        for pair in range(pairs):
            lanes = slice(pair * PAIR, (pair + 1) * PAIR)
            query = stacked(q_ref[rows, lanes] * BF16(HEAD_DIM**-0.5))
            key = keys_of(k_ref, pooled_k_ref, tile, lanes)
            value = keys_of(v_ref, pooled_v_ref, tile, lanes)
            scores = product_right_t(key, query) + bias
            most = jnp.max(scores, axis=0, keepdims=True)
            weight = jnp.exp(scores - most)
            total = jnp.sum(weight, axis=0, keepdims=True)
            both = product_left_t(value, weight.astype(BF16)) * (1.0 / total)
            mixed_ref[rows, lanes] = unstack(both).T.astype(BF16)
            lse_ref[tile, pair : pair + 1, :] = most + jnp.log(total)


def attend_backward_kernel(
    q_ref, k_ref, v_ref, pooled_k_ref, pooled_v_ref, grad_ref, lse_ref,
    first_ref, past_ref, keep_ref, conv_ref,
    grad_q_ref, grad_k_ref, grad_v_ref, small_ref,
    wide_k, wide_v, far_k, far_v, wide_f32,
):
    pairs = q_ref.shape[1] // PAIR
    wide_k[...] = jnp.zeros_like(wide_k)
    wide_v[...] = jnp.zeros_like(wide_v)
    far_k[...] = jnp.zeros_like(far_k)
    far_v[...] = jnp.zeros_like(far_v)
    small_ref[...] = jnp.zeros_like(small_ref)

    @pl.loop(0, q_ref.shape[0] // TILE)
    def _(tile):
        rows = pl.ds(pl.multiple_of(tile * TILE, TILE), TILE)
        near = pl.ds(pl.multiple_of(LEFT - WINDOW + tile * TILE, TILE), SPAN)
        far = pl.ds(pl.multiple_of(tile * (TILE // 4), TILE // 4), POOL_SPAN)
        bias = tile_bias(tile, first_ref[tile], past_ref[tile])
        bias = jnp.concatenate([bias, bias], axis=1)
        for pair in range(pairs):
            lanes = slice(pair * PAIR, (pair + 1) * PAIR)
            query = stacked(q_ref[rows, lanes] * BF16(HEAD_DIM**-0.5))
            grad = stacked(grad_ref[rows, lanes])
            key = keys_of(k_ref, pooled_k_ref, tile, lanes)
            value = keys_of(v_ref, pooled_v_ref, tile, lanes)
            scores = product_right_t(key, query) + bias
            probs = jnp.exp(scores - lse_ref[tile, pair : pair + 1, :])
            grad_probs = product_right_t(value, grad)
            delta = jnp.sum(probs * grad_probs, axis=0, keepdims=True)
            grad_scores = (probs * (grad_probs - delta)).astype(BF16)
            grad_value = product(probs.astype(BF16), grad)
            grad_key = product(grad_scores, query)
            wide_v[pair, near, :] += grad_value[:SPAN]
            far_v[far, lanes] += grad_value[SPAN:]
            wide_k[pair, near, :] += grad_key[:SPAN]
            far_k[far, lanes] += grad_key[SPAN:]
            grad_query = unstack(product_left_t(key, grad_scores)).T * (HEAD_DIM**-0.5)
            grad_q_ref[rows, lanes] = grad_query.astype(BF16)
            small_ref[0:1, lanes] += jnp.sum(grad_query, axis=0, keepdims=True)

    count = far_k.shape[0]
    begin = LEFT - 4 * POOL_REACH - 2
    for which, (source, wide, pooled, result) in enumerate(
        ((k_ref, wide_k, far_k, grad_k_ref), (v_ref, wide_v, far_v, grad_v_ref))
    ):
        for pair in range(pairs):
            lanes = slice(pair * PAIR, (pair + 1) * PAIR)
            wide_f32[...] = source[:, lanes].astype(F32)
            grad = pooled[:, lanes]
            at = 12 + which
            small_ref[at : at + 1, lanes] = jnp.sum(grad, axis=0, keepdims=True)
            for tap in range(5):
                places = pl.ds(begin + tap, count, stride=4)
                kept = jnp.where(keep_ref[:, tap : tap + 1] > 0.0, grad, 0.0)
                at = 2 + 5 * which + tap
                small_ref[at : at + 1, lanes] = jnp.sum(
                    kept * wide_f32[places, :], axis=0, keepdims=True
                )
                wide[pair, places, :] += kept * conv_ref[which, tap : tap + 1, lanes]
            if which == 1:
                small_ref[1:2, lanes] = jnp.sum(wide[pair], axis=0, keepdims=True)
            result[:, lanes] = wide[pair].astype(BF16)


def in_vmem(count):
    return [pl.BlockSpec(memory_space=pltpu.VMEM)] * count


VMEM_LIMIT = 56 * 1024 * 1024


def attend_forward(queries, keys, values, first, past, keep, conv, conv_bias):
    total, width = queries.shape
    count = total // 4 + 2 * POOL_REACH
    shape = jax.ShapeDtypeStruct
    return pl.pallas_call(
        attend_forward_kernel,
        out_shape=(
            shape((total, width), BF16),
            shape((total // TILE, width // PAIR, 2 * TILE), F32),
            shape((count, width), BF16),
            shape((count, width), BF16),
        ),
        in_specs=in_vmem(8),
        out_specs=tuple(in_vmem(4)),
        scratch_shapes=[pltpu.VMEM((keys.shape[0], PAIR), F32)],
        compiler_params=pltpu.CompilerParams(vmem_limit_bytes=VMEM_LIMIT),
        name="attend_forward",
    )(queries, keys, values, first, past, keep, conv, conv_bias)


def attend_backward(queries, keys, values, pooled_k, pooled_v, grad, lse, first, past, keep, conv):
    total, width = queries.shape
    shape = jax.ShapeDtypeStruct
    return pl.pallas_call(
        attend_backward_kernel,
        out_shape=(
            shape((total, width), BF16),
            shape(keys.shape, BF16),
            shape(keys.shape, BF16),
            shape((16, width), F32),
        ),
        in_specs=in_vmem(11),
        out_specs=tuple(in_vmem(4)),
        scratch_shapes=[
            pltpu.VMEM((width // PAIR, keys.shape[0], PAIR), F32),
            pltpu.VMEM((width // PAIR, keys.shape[0], PAIR), F32),
            pltpu.VMEM(pooled_k.shape, F32),
            pltpu.VMEM(pooled_k.shape, F32),
            pltpu.VMEM((keys.shape[0], PAIR), F32),
        ],
        compiler_params=pltpu.CompilerParams(vmem_limit_bytes=VMEM_LIMIT),
        name="attend_backward",
    )(queries, keys, values, pooled_k, pooled_v, grad, lse, first, past, keep, conv)


def gelu_parts(pre):
    size = jnp.abs(pre) * (0.5**0.5)
    t = 1.0 / (1.0 + 0.5 * size)
    series = 0.17087277
    for term in (-0.82215223, 1.48851587, -1.13520398, 0.27886807, -0.18628806, 0.09678418,
                 0.37409196, 1.00002368, -1.26551223):
        series = series * t + term
    tail = 0.5 * t * jnp.exp(series - size * size)
    cdf = jnp.where(pre < 0.0, tail, 1.0 - tail)
    density = jnp.exp(-0.5 * pre * pre) * (0.5 / jnp.pi) ** 0.5
    return pre * cdf, cdf + pre * density


def layer_forward(hidden, masks, weights):
    first, past, keep = masks
    qkv, qv, conv, conv_bias, out, up, up_bias, down, gains, biases = weights
    total = hidden.shape[0]
    entry_wide = with_halo(hidden.astype(BF16))
    entry = entry_wide[LEFT : LEFT + total]
    queries = (product(entry, qkv[0]) + qv[0]).astype(BF16)
    keys = product(entry_wide, qkv[1]).astype(BF16)
    values = (product(entry_wide, qkv[2]) + qv[1]).astype(BF16)

    mixed, lse, pooled_k, pooled_v = attend_forward(
        queries, keys, values, first, past, keep, conv, conv_bias
    )
    resid = hidden + (product(mixed, out) + biases[0])
    normed, unit_one, inverse_one = norm_forward(resid, gains[0], biases[1])
    normed_low = normed.astype(BF16)
    pre = product(normed_low, up) + up_bias
    act, slope = gelu_parts(pre)
    act, slope = act.astype(BF16), slope.astype(BF16)
    middle = normed + (product(act, down) + biases[2])
    result, unit_two, inverse_two = norm_forward(middle, gains[1], biases[3])
    saved = (
        entry_wide,
        queries,
        keys,
        values,
        pooled_k,
        pooled_v,
        mixed,
        lse,
        unit_one,
        inverse_one,
        normed_low,
        act,
        slope,
        unit_two,
        inverse_two,
    )
    return result, saved


CHUNK = 256
LAG = 2


def partner(seq=None, mp=None):
    return {"seq": lax.axis_index("seq") if seq is None else seq,
            "mp": lax.axis_index("mp") if mp is None else mp}


def peers_of(place, seat, group):
    low, high = place % 2, place // 2
    others = [partner(seq=((high + step) % group) * 2 + low) for step in range(1, group)]
    return (
        partner(mp=seat + 1 - 2 * (seat % 2)),
        partner(mp=(seat + 2) % 4),
        partner(seq=place + 1 - 2 * low),
        others,
    )


def reduce_kernel(
    group, count, parts_ref, out_ref,
    own_v, core_v, across_v, cross_v, first_v, give_v, half_v, keep_v, piece_v, slab_v, sum_v, done_v,
    local_sem, core_send, core_recv, x_send, x_recv, y_send, y_recv, z_send, z_recv,
    g_send, g_recv, f_send, f_recv, f_local,
):
    place, seat = lax.axis_index("seq"), lax.axis_index("mp")
    low, high = place % 2, place // 2
    core, across, beside, others = peers_of(place, seat, group)
    rows = CHUNK // group
    width = parts_ref.shape[-1]
    half = width // 2
    barrier = pltpu.get_barrier_semaphore()
    for device in [core, across, beside] + others:
        pl.semaphore_signal(barrier, inc=1, device_id=device, device_id_type=pl.DeviceIdType.MESH)
    pl.semaphore_wait(barrier, 3 + len(others))

    def remote(source, target, send, recv, device):
        return pltpu.make_async_remote_copy(
            src_ref=source, dst_ref=target, send_sem=send, recv_sem=recv,
            device_id=device, device_id_type=pl.DeviceIdType.MESH,
        )

    def local_copy(c):
        return pltpu.make_async_copy(parts_ref.at[c, pl.ds(0, 2)], own_v.at[c % 2], local_sem.at[c % 2])

    def core_copy(c):
        return remote(parts_ref.at[c, pl.ds(2, 2)], core_v.at[c], core_send.at[c], core_recv.at[c], core)

    def x_copy(c):
        return remote(across_v.at[c % 4], cross_v.at[c], x_send.at[c], x_recv.at[c], across)

    def y_copy(c):
        return remote(give_v.at[c % 4], half_v.at[c], y_send.at[c], y_recv.at[c], beside)

    def z_copy(c, step):
        to = (high + step) % group
        return remote(
            slab_v.at[c % 4, pl.ds(pl.multiple_of(to * rows, rows), rows)],
            piece_v.at[c, step - 1],
            z_send.at[c, step - 1], z_recv.at[c, step - 1], others[step - 1],
        )

    def own_rows():
        return pl.ds(pl.multiple_of(high * rows, rows), rows)

    def g_copy(c, step):
        mine = done_v.at[c, own_rows()]
        return remote(mine, mine, g_send.at[c, step - 1], g_recv.at[c, step - 1], others[step - 1])

    def lanes():
        return pl.ds(pl.multiple_of(low * half, 128), half)

    def f_copy(c):
        return remote(done_v.at[c], out_ref.at[c, :, lanes()], f_send.at[c], f_recv.at[c], beside)

    def f_own(c):
        return pltpu.make_async_copy(done_v.at[c], out_ref.at[c, :, lanes()], f_local.at[c])

    def step_zero(c):
        local_copy(c).start()
        core_copy(c).start()

    def step_core(c):
        local_copy(c).wait()
        core_copy(c).wait()
        first_v[c % 4] = own_v[c % 2, 0].astype(F32) + core_v[c, 0].astype(F32)
        across_v[c % 4] = (own_v[c % 2, 1].astype(F32) + core_v[c, 1].astype(F32)).astype(BF16)
        x_copy(c).start()

    def step_x(c):
        x_copy(c).wait()
        total = first_v[c % 4] + cross_v[c].astype(F32)
        left, right = total[:, :half], total[:, half:]
        keep_v[c % 4] = jnp.where(low == 0, left, right)
        give_v[c % 4] = jnp.where(low == 0, right, left).astype(BF16)
        y_copy(c).start()

    def step_y(c):
        y_copy(c).wait()
        total = keep_v[c % 4] + half_v[c].astype(F32)
        sum_v[c % 4] = total
        slab_v[c % 4] = total.astype(BF16)
        for step in range(1, group):
            z_copy(c, step).start()

    def step_z(c):
        total = sum_v[c % 4, own_rows(), :]
        for step in range(1, group):
            z_copy(c, step).wait()
            total = total + piece_v[c, step - 1].astype(F32)
        done_v[c, own_rows(), :] = total.astype(BF16)
        for step in range(1, group):
            g_copy(c, step).start()

    def step_gather(c):
        for step in range(1, group):
            g_copy(c, step).wait()
        f_copy(c).start()
        f_own(c).start()

    def step_end(c):
        local = f_own(c)
        local.wait()
        f_copy(c).wait()

    stages = [(step_zero, 0), (step_core, 1)]
    for k, stage in enumerate((step_x, step_y, step_z, step_gather, step_end)):
        stages.append((stage, 1 + LAG * (k + 1)))
    last = stages[-1][1]

    @pl.loop(0, count + last)
    def _(slot):
        for stage, delay in stages:
            at = slot - delay

            @pl.when((at >= 0) & (at < count))
            def _():
                stage(at)


def reduce_parts(parts):
    count, _, rows, width = parts.shape
    group = lax.axis_size("seq") // 2
    half = width // 2
    piece = rows // group
    vmem, dma = pltpu.VMEM, pltpu.SemaphoreType.DMA
    return pl.pallas_call(
        functools.partial(reduce_kernel, group, count),
        out_shape=jax.ShapeDtypeStruct((count, rows, width), BF16),
        in_specs=[pl.BlockSpec(memory_space=pl.ANY)],
        out_specs=pl.BlockSpec(memory_space=pl.ANY),
        scratch_shapes=[
            vmem((2, 2, rows, width), BF16),
            vmem((count, 2, rows, width), BF16),
            vmem((4, rows, width), BF16),
            vmem((count, rows, width), BF16),
            vmem((4, rows, width), F32),
            vmem((4, rows, half), BF16),
            vmem((count, rows, half), BF16),
            vmem((4, rows, half), F32),
            vmem((count, group - 1, piece, half), BF16),
            vmem((4, rows, half), BF16),
            vmem((4, rows, half), F32),
            vmem((count, rows, half), BF16),
            dma((2,)),
            dma((count,)),
            dma((count,)),
            dma((count,)),
            dma((count,)),
            dma((count,)),
            dma((count,)),
            dma((count, group - 1)),
            dma((count, group - 1)),
            dma((count, group - 1)),
            dma((count, group - 1)),
            dma((count,)),
            dma((count,)),
            dma((count,)),
        ],
        compiler_params=pltpu.CompilerParams(
            collective_id=0, has_side_effects=True, vmem_limit_bytes=VMEM_LIMIT
        ),
        name="reduce_parts",
    )(parts)


ORDER = (0, 2, 1, 3)


def layer_parts(down, up_t, *rest):
    rows = CHUNK // 4
    big = [piece.astype(BF16).reshape(4, 3, CHUNK, -1) for piece in (down, up_t)]
    small = [piece.astype(BF16).reshape(4, 3, rows, piece.shape[1]) for piece in rest]
    joined = jnp.concatenate(big + [jnp.concatenate(small, axis=2)], axis=1)
    return jnp.stack([joined[k] for k in ORDER], axis=1)


def layer_backward(grad_out, masks, weights, saved):
    first, past, keep = masks
    qkv, qv, conv, conv_bias, out, up, up_bias, down, gains, biases = weights
    (
        entry_wide,
        queries,
        keys,
        values,
        pooled_k,
        pooled_v,
        mixed,
        lse,
        unit_one,
        inverse_one,
        normed_low,
        act,
        slope,
        unit_two,
        inverse_two,
    ) = saved
    total, width = queries.shape
    grad_middle, gain_two, shift_two = norm_backward(grad_out, unit_two, inverse_two, gains[1])
    bias_down = jnp.sum(grad_middle, axis=0)
    grad_middle_low = grad_middle.astype(BF16)
    grad_w_down = product_left_t(act, grad_middle_low)
    grad_pre = product_right_t(grad_middle_low, down) * slope.astype(F32)
    grad_b_up = jnp.sum(grad_pre, axis=0)
    grad_pre_low = grad_pre.astype(BF16)
    grad_w_up_t = product_left_t(grad_pre_low, normed_low)
    grad_normed = product_right_t(grad_pre_low, up) + grad_middle
    grad_resid, gain_one, shift_one = norm_backward(grad_normed, unit_one, inverse_one, gains[0])
    bias_out = jnp.sum(grad_resid, axis=0)
    grad_resid_low = grad_resid.astype(BF16)
    grad_w_out = product_left_t(mixed, grad_resid_low)
    grad_mixed = product_right_t(grad_resid_low, out).astype(BF16)
    grad_q_low, grad_k_low, grad_v_low, small = attend_backward(
        queries, keys, values, pooled_k, pooled_v, grad_mixed, lse, first, past, keep, conv
    )
    entry = entry_wide[LEFT : LEFT + total]
    w_q = product_left_t(grad_q_low, entry)
    w_k = product_left_t(grad_k_low, entry_wide)
    w_v = product_left_t(grad_v_low, entry_wide)
    parts = layer_parts(grad_w_down, grad_w_up_t, grad_w_out, w_q, w_k, w_v)
    wide_grad = product_right_t(grad_k_low, qkv[1]) + product_right_t(grad_v_low, qkv[2])
    from_right = shift(wide_grad[LEFT - LEFT_SENT : LEFT].astype(BF16), -1).astype(F32)
    from_left = shift(wide_grad[LEFT + total :].astype(BF16), 1).astype(F32)
    grad_hidden = (
        product_right_t(grad_q_low, qkv[0])
        + wide_grad[LEFT : LEFT + total]
        + grad_resid
        + jnp.pad(from_right, ((total - LEFT_SENT, 0), (0, 0)))
        + jnp.pad(from_left, ((0, total - RIGHT), (0, 0)))
    )
    grad_b_up_rows = grad_b_up.reshape(4, -1, width // 4).transpose(1, 0, 2).reshape(-1, width)
    small_split = jnp.concatenate([small[:14], grad_b_up_rows], axis=0)
    small_whole = jnp.stack([gain_one, gain_two, bias_out, shift_one, bias_down, shift_two])
    return grad_hidden, parts, small_split, small_whole


def shards(
    inputs,
    doc_bounds,
    qkv_weight,
    qv_bias,
    conv_weight,
    conv_bias,
    out_weight,
    up_weight,
    up_bias,
    down_weight,
    norm_gains,
    shared_biases,
    cotangent,
):
    total, width = inputs.shape
    place = lax.axis_index("mp")
    base_row = lax.axis_index("seq") * doc_bounds.shape[1] + place * total
    bounds = lax.dynamic_slice_in_dim(doc_bounds, place * total, total, 1)
    keep = jnp.pad(tap_mask(bounds[0], bounds[1], base_row).astype(F32), ((0, 0), (0, 3)))
    near_bounds = (bounds - base_row).reshape(2, total // TILE, 1, TILE)
    masks = (near_bounds[0], near_bounds[1], keep)
    quarter = width // 4
    small = jnp.concatenate(
        [
            qv_bias.reshape(-1, quarter),
            conv_weight.reshape(-1, quarter),
            conv_bias.reshape(-1, quarter),
            up_bias.reshape(-1, quarter),
        ],
        axis=0,
    )
    small = gather_small(small)
    layers = []
    for index in range(LAYERS):
        qkv = jnp.concatenate(gather_parts(qkv_weight[index]), axis=2)
        out = jnp.concatenate(gather_parts(out_weight[index]), axis=0)
        up = jnp.concatenate(gather_parts(up_weight[index]), axis=1)
        down = jnp.concatenate(gather_parts(down_weight[index]), axis=0)
        layers.append((qkv, out, up, down))
    wide_small = jnp.concatenate(small, axis=1)
    qv_all = wide_small[:4].reshape(2, 2, width)
    conv_all = wide_small[4:24].reshape(2, 2, 5, width)
    conv_bias_all = wide_small[24:28].reshape(2, 2, width)
    up_bias_all = jnp.stack([part[28:].reshape(2, -1) for part in small], axis=1).reshape(2, -1)
    hidden = inputs.astype(F32)
    stack = []
    for index in range(LAYERS):
        qkv, out, up, down = layers[index]
        weights = (
            qkv,
            qv_all[index],
            conv_all[index],
            conv_bias_all[index],
            out,
            up,
            up_bias_all[index],
            down,
            norm_gains[index],
            shared_biases[index],
        )
        hidden, saved = layer_forward(hidden, masks, weights)
        stack.append((weights, saved))
    gradient = cotangent.astype(F32)
    collected = [None] * LAYERS
    for index in reversed(range(LAYERS)):
        weights, saved = stack[index]
        gradient, parts, split, whole = layer_backward(gradient, masks, weights, saved)
        collected[index] = (parts, split, whole)
    split = jnp.concatenate([part[1] for part in collected], axis=0).astype(BF16)
    whole = jnp.concatenate([part[2] for part in collected], axis=0).astype(BF16)
    extra = []
    for part in ORDER:
        own_split = jnp.pad(
            split[:, part * quarter : (part + 1) * quarter],
            ((0, 64 - split.shape[0]), (0, width - quarter)),
        )
        extra.append(
            jnp.pad(
                jnp.concatenate([own_split, whole], axis=0),
                ((0, CHUNK - 64 - whole.shape[0]), (0, 0)),
            )
        )
    total_parts = jnp.concatenate(
        [collected[1][0], collected[0][0], jnp.stack(extra)[None]], axis=0
    )
    sums = reduce_parts(total_parts).astype(F32)
    per_layer = sums[:18].reshape(2, 3, 3, 4, CHUNK // 4, width)
    per_layer = jnp.stack([per_layer[1], per_layer[0]])
    units = down_weight.shape[1]
    grad_down = per_layer[:, 0].reshape(2, units, width)
    grad_up = per_layer[:, 1].reshape(2, units, width).transpose(0, 2, 1)
    rest = per_layer[:, 2].transpose(0, 2, 1, 3, 4).reshape(2, 4, quarter, width)
    small_split = sums[18, :36, :quarter].reshape(2, 18, quarter)
    small_whole = sums[18, 64:76].reshape(2, 6, width)
    return (
        hidden,
        gradient,
        rest[:, 1:].transpose(0, 1, 3, 2),
        small_split[:, :2],
        small_split[:, 2:12].reshape(2, 2, 5, quarter),
        small_split[:, 12:14],
        rest[:, 0],
        grad_up,
        small_split[:, 14:18].reshape(2, -1),
        grad_down,
        small_whole[:, :2],
        small_whole[:, 2:],
    )


def solution(mesh):
    return jax.shard_map(
        shards,
        mesh=mesh,
        in_specs=(
            P(BOTH, None),
            P(None, "seq"),
            P(None, None, None, "mp"),
            P(None, None, "mp"),
            P(None, None, None, "mp"),
            P(None, None, "mp"),
            P(None, "mp", None),
            P(None, None, "mp"),
            P(None, "mp"),
            P(None, "mp", None),
            P(),
            P(),
            P(BOTH, None),
        ),
        out_specs=(
            P(BOTH, None),
            P(BOTH, None),
            P(None, None, None, "mp"),
            P(None, None, "mp"),
            P(None, None, None, "mp"),
            P(None, None, "mp"),
            P(None, "mp", None),
            P(None, None, "mp"),
            P(None, "mp"),
            P(None, "mp", None),
            P(),
            P(),
        ),
        check_vma=False,
    )
```

```python
import functools

import jax
import jax.numpy as jnp
from jax import lax
from jax.experimental import pallas as pl
from jax.experimental.pallas import tpu as pltpu
from jax.sharding import PartitionSpec as P

HEAD_DIM = 64
LAYERS = 2
WINDOW = 64
POOL_REACH = 64
NORM_EPSILON = 1e-05
LEFT = 320
LEFT_SENT = 272
RIGHT = 256
BOTH = ("seq", "mp")
BF16 = jnp.bfloat16
F32 = jnp.float32


def product(left, right):
    return jnp.dot(left, right, preferred_element_type=F32)


def product_left_t(left, right):
    return lax.dot_general(left, right, (((0,), (0,)), ((), ())), preferred_element_type=F32)


def product_right_t(left, right):
    return lax.dot_general(left, right, (((1,), (1,)), ((), ())), preferred_element_type=F32)


def swap(values, axis, bit):
    count = lax.axis_size(axis)
    return lax.ppermute(values, axis, [(i, i ^ bit) for i in range(count)])


def shift(values, step):
    count = lax.axis_size("seq") * lax.axis_size("mp")
    return lax.ppermute(
        values, BOTH, [(i, i + step) for i in range(count) if 0 <= i + step < count]
    )


def gather_parts(own):
    across = swap(own, "mp", 2)
    return [own, swap(own, "mp", 1), across, swap(across, "mp", 1)]


def gather_small(own):
    return gather_parts(own)


def norm_forward(values, gain, offset):
    average = jnp.mean(values, axis=-1, keepdims=True)
    centered = values - average
    spread = jnp.mean(centered * centered, axis=-1, keepdims=True)
    inverse = lax.rsqrt(spread + NORM_EPSILON)
    unit = centered * inverse
    return unit * gain + offset, unit, inverse


def with_halo(rows):
    left = shift(rows[rows.shape[0] - LEFT_SENT :], 1)
    right = shift(rows[:RIGHT], -1)
    empty = jnp.zeros((LEFT - LEFT_SENT, rows.shape[1]), rows.dtype)
    return jnp.concatenate([empty, left, rows, right], axis=0)


def tap_mask(starts, finish, base_row):
    count = starts.shape[0] // 4
    reach = (POOL_REACH,)
    first = jnp.concatenate(
        [
            jnp.broadcast_to(starts[:1], reach),
            starts.reshape(count, 4)[:, 0],
            jnp.broadcast_to(starts[-1:], reach),
        ]
    )
    past = jnp.concatenate(
        [
            jnp.broadcast_to(finish[:1], reach),
            finish.reshape(count, 4)[:, 0],
            jnp.broadcast_to(finish[-1:], reach),
        ]
    )
    places = (
        base_row
        + 4 * (jnp.arange(count + 2 * POOL_REACH, dtype=jnp.int32)[:, None] - POOL_REACH)
        + jnp.arange(5, dtype=jnp.int32)[None]
        - 2
    )
    return (places >= first[:, None]) & (places < past[:, None])


PAIR = 128
TILE = 128
SPAN = TILE + 2 * WINDOW
POOL_SPAN = TILE // 4 + 2 * POOL_REACH
FAR = -1e30


def tile_bias(tile, first, past):
    lane = lax.broadcasted_iota(jnp.int32, (1, TILE), 1) + tile * TILE
    near = lax.broadcasted_iota(jnp.int32, (SPAN, 1), 0) + (tile * TILE - WINDOW)
    far = 4 * (lax.broadcasted_iota(jnp.int32, (POOL_SPAN, 1), 0) + (tile * (TILE // 4) - POOL_REACH))

    def one(keys, reach):
        low = jnp.maximum(lane - reach, first)
        high = jnp.minimum(lane + reach + 1, past)
        return jnp.where((keys >= low) & (keys < high), 0.0, FAR)

    return jnp.concatenate([one(near, WINDOW), one(far, 4 * POOL_REACH)], axis=0)


def pair_mask():
    return lax.broadcasted_iota(jnp.int32, (1, PAIR), 1) < HEAD_DIM


def stacked(rows):
    left = pair_mask()
    zero = jnp.zeros_like(rows)
    return jnp.concatenate([jnp.where(left, rows, zero), jnp.where(left, zero, rows)], axis=0)


def keys_of(wide_ref, pooled_ref, tile, lanes):
    near = wide_ref[pl.ds(pl.multiple_of(LEFT - WINDOW + tile * TILE, TILE), SPAN), lanes]
    far = pooled_ref[pl.ds(pl.multiple_of(tile * (TILE // 4), TILE // 4), POOL_SPAN), lanes]
    return jnp.concatenate([near, far], axis=0)


def unstack(both):
    return jnp.concatenate([both[:HEAD_DIM, :TILE], both[HEAD_DIM:, TILE:]], axis=0)


def pool_into(wide_ref, wide_f32, keep_ref, conv_ref, conv_bias_ref, which, pooled_ref):
    count = pooled_ref.shape[0]
    begin = LEFT - 4 * POOL_REACH - 2
    for pair in range(pooled_ref.shape[1] // PAIR):
        lanes = slice(pair * PAIR, (pair + 1) * PAIR)
        wide_f32[...] = wide_ref[:, lanes].astype(F32)
        total = jnp.broadcast_to(conv_bias_ref[which : which + 1, lanes], (count, PAIR))
        for tap in range(5):
            rows = wide_f32[pl.ds(begin + tap, count, stride=4), :]
            kept = jnp.where(keep_ref[:, tap : tap + 1] > 0.0, rows, 0.0)
            total = total + kept * conv_ref[which, tap : tap + 1, lanes]
        pooled_ref[:, lanes] = total.astype(BF16)


def attend_forward_kernel(
    q_ref, k_ref, v_ref, first_ref, past_ref, keep_ref, conv_ref, conv_bias_ref,
    mixed_ref, lse_ref, pooled_k_ref, pooled_v_ref, wide_f32,
):
    pool_into(k_ref, wide_f32, keep_ref, conv_ref, conv_bias_ref, 0, pooled_k_ref)
    pool_into(v_ref, wide_f32, keep_ref, conv_ref, conv_bias_ref, 1, pooled_v_ref)
    pairs = q_ref.shape[1] // PAIR

    @pl.loop(0, q_ref.shape[0] // TILE)
    def _(tile):
        rows = pl.ds(pl.multiple_of(tile * TILE, TILE), TILE)
        bias = tile_bias(tile, first_ref[tile], past_ref[tile])
        bias = jnp.concatenate([bias, bias], axis=1)
        for pair in range(pairs):
            lanes = slice(pair * PAIR, (pair + 1) * PAIR)
            query = stacked(q_ref[rows, lanes] * BF16(HEAD_DIM**-0.5))
            key = keys_of(k_ref, pooled_k_ref, tile, lanes)
            value = keys_of(v_ref, pooled_v_ref, tile, lanes)
            scores = product_right_t(key, query) + bias
            most = jnp.max(scores, axis=0, keepdims=True)
            weight = jnp.exp(scores - most)
            total = jnp.sum(weight, axis=0, keepdims=True)
            both = product_left_t(value, weight.astype(BF16)) * (1.0 / total)
            mixed_ref[rows, lanes] = unstack(both).T.astype(BF16)
            lse_ref[tile, pair : pair + 1, :] = most + jnp.log(total)


def attend_backward_body(
    q_ref, k_ref, v_ref, pooled_k_ref, pooled_v_ref, grad_ref, lse_ref,
    first_ref, past_ref, keep_ref, conv_ref,
    grad_q_ref, grad_k_ref, grad_v_ref, small_ref,
    wide_k, wide_v, far_k, far_v, wide_f32, slot_of,
):
    pairs = q_ref.shape[1] // PAIR
    wide_k[...] = jnp.zeros_like(wide_k)
    wide_v[...] = jnp.zeros_like(wide_v)
    far_k[...] = jnp.zeros_like(far_k)
    far_v[...] = jnp.zeros_like(far_v)
    small_ref[...] = jnp.zeros_like(small_ref)

    @pl.loop(0, q_ref.shape[0] // TILE)
    def _(tile):
        rows = pl.ds(pl.multiple_of(tile * TILE, TILE), TILE)
        near = pl.ds(pl.multiple_of(LEFT - WINDOW + tile * TILE, TILE), SPAN)
        far = pl.ds(pl.multiple_of(tile * (TILE // 4), TILE // 4), POOL_SPAN)
        bias = tile_bias(tile, first_ref[tile], past_ref[tile])
        bias = jnp.concatenate([bias, bias], axis=1)
        for pair in range(pairs):
            lanes = slice(pair * PAIR, (pair + 1) * PAIR)
            query = stacked(q_ref[rows, lanes] * BF16(HEAD_DIM**-0.5))
            grad = stacked(grad_ref[rows, lanes])
            key = keys_of(k_ref, pooled_k_ref, tile, lanes)
            value = keys_of(v_ref, pooled_v_ref, tile, lanes)
            scores = product_right_t(key, query) + bias
            probs = jnp.exp(scores - lse_ref[tile, pair : pair + 1, :])
            grad_probs = product_right_t(value, grad)
            delta = jnp.sum(probs * grad_probs, axis=0, keepdims=True)
            grad_scores = (probs * (grad_probs - delta)).astype(BF16)
            grad_value = product(probs.astype(BF16), grad)
            grad_key = product(grad_scores, query)
            wide_v[pair, near, :] += grad_value[:SPAN]
            far_v[far, lanes] += grad_value[SPAN:]
            wide_k[pair, near, :] += grad_key[:SPAN]
            far_k[far, lanes] += grad_key[SPAN:]
            grad_query = unstack(product_left_t(key, grad_scores)).T * (HEAD_DIM**-0.5)
            grad_q_ref[rows, lanes] = grad_query.astype(BF16)
            small_ref[0:1, lanes] += jnp.sum(grad_query, axis=0, keepdims=True)
        slot_of(tile)

    count = far_k.shape[0]
    begin = LEFT - 4 * POOL_REACH - 2
    for which, (source, wide, pooled, result) in enumerate(
        ((k_ref, wide_k, far_k, grad_k_ref), (v_ref, wide_v, far_v, grad_v_ref))
    ):
        for pair in range(pairs):
            lanes = slice(pair * PAIR, (pair + 1) * PAIR)
            wide_f32[...] = source[:, lanes].astype(F32)
            grad = pooled[:, lanes]
            at = 12 + which
            small_ref[at : at + 1, lanes] = jnp.sum(grad, axis=0, keepdims=True)
            for tap in range(5):
                places = pl.ds(begin + tap, count, stride=4)
                kept = jnp.where(keep_ref[:, tap : tap + 1] > 0.0, grad, 0.0)
                at = 2 + 5 * which + tap
                small_ref[at : at + 1, lanes] = jnp.sum(
                    kept * wide_f32[places, :], axis=0, keepdims=True
                )
                wide[pair, places, :] += kept * conv_ref[which, tap : tap + 1, lanes]
            if which == 1:
                small_ref[1:2, lanes] = jnp.sum(wide[pair], axis=0, keepdims=True)
            result[:, lanes] = wide[pair].astype(BF16)


def in_vmem(count):
    return [pl.BlockSpec(memory_space=pltpu.VMEM)] * count


VMEM_LIMIT = 56 * 1024 * 1024


def attend_forward(queries, keys, values, first, past, keep, conv, conv_bias):
    total, width = queries.shape
    count = total // 4 + 2 * POOL_REACH
    shape = jax.ShapeDtypeStruct
    return pl.pallas_call(
        attend_forward_kernel,
        out_shape=(
            shape((total, width), BF16),
            shape((total // TILE, width // PAIR, 2 * TILE), F32),
            shape((count, width), BF16),
            shape((count, width), BF16),
        ),
        in_specs=in_vmem(8),
        out_specs=tuple(in_vmem(4)),
        scratch_shapes=[pltpu.VMEM((keys.shape[0], PAIR), F32)],
        compiler_params=pltpu.CompilerParams(vmem_limit_bytes=VMEM_LIMIT),
        name="attend_forward",
    )(queries, keys, values, first, past, keep, conv, conv_bias)


def gelu_parts(pre):
    size = jnp.abs(pre) * (0.5**0.5)
    t = 1.0 / (1.0 + 0.5 * size)
    series = 0.17087277
    for term in (-0.82215223, 1.48851587, -1.13520398, 0.27886807, -0.18628806, 0.09678418,
                 0.37409196, 1.00002368, -1.26551223):
        series = series * t + term
    tail = 0.5 * t * jnp.exp(series - size * size)
    cdf = jnp.where(pre < 0.0, tail, 1.0 - tail)
    density = jnp.exp(-0.5 * pre * pre) * (0.5 / jnp.pi) ** 0.5
    return pre * cdf, cdf + pre * density


def layer_forward(hidden, masks, weights):
    first, past, keep = masks
    qkv, qv, conv, conv_bias, out, up, up_bias, down, gains, biases = weights
    total = hidden.shape[0]
    entry_wide = with_halo(hidden.astype(BF16))
    entry = entry_wide[LEFT : LEFT + total]
    queries = (product(entry, qkv[0]) + qv[0]).astype(BF16)
    keys = product(entry_wide, qkv[1]).astype(BF16)
    values = (product(entry_wide, qkv[2]) + qv[1]).astype(BF16)

    mixed, lse, pooled_k, pooled_v = attend_forward(
        queries, keys, values, first, past, keep, conv, conv_bias
    )
    resid = hidden + (product(mixed, out) + biases[0])
    normed, unit_one, inverse_one = norm_forward(resid, gains[0], biases[1])
    normed_low = normed.astype(BF16)
    pre = product(normed_low, up) + up_bias
    act, slope = gelu_parts(pre)
    act, slope = act.astype(BF16), slope.astype(BF16)
    middle = normed + (product(act, down) + biases[2])
    result, unit_two, inverse_two = norm_forward(middle, gains[1], biases[3])
    saved = dict(
        act=act, slope=slope, normed=normed_low, unit_one=unit_one, unit_two=unit_two, mixed=mixed,
        q=queries, k=keys, v=values, pooled_k=pooled_k, pooled_v=pooled_v, entry=entry_wide,
        down=down, up=up, out=out, qkv=qkv, inverse_one=inverse_one, inverse_two=inverse_two, lse=lse,
    )
    return result, saved


CHUNK = 256
LAG = 2
MESH = pl.DeviceIdType.MESH
LAYER_ROWS = 2304
SMALL_ROWS = 256
NORM_ROWS = 64


def seat_of(seq=None, mp=None):
    return {
        "seq": lax.axis_index("seq") if seq is None else seq,
        "mp": lax.axis_index("mp") if mp is None else mp,
    }


class Reducer:
    def __init__(self, group, count, parts, out, bufs, sems):
        place, seat = lax.axis_index("seq"), lax.axis_index("mp")
        self.group, self.count, self.parts, self.out = group, count, parts, out
        self.low, self.high = place % 2, place // 2
        self.core = seat_of(mp=seat + 1 - 2 * (seat % 2))
        self.across = seat_of(mp=(seat + 2) % 4)
        self.beside = seat_of(seq=place + 1 - 2 * self.low)
        self.others = [
            seat_of(seq=((self.high + step) % group) * 2 + self.low) for step in range(1, group)
        ]
        (self.own_v, self.core_v, self.across_v, self.cross_v, self.first_v, self.give_v,
         self.half_v, self.keep_v, self.piece_v, self.slab_v, self.sum_v, self.done_v) = bufs
        (self.local_s, self.core_s, self.core_r, self.x_s, self.x_r, self.y_s, self.y_r,
         self.z_s, self.z_r, self.g_s, self.g_r, self.f_s, self.f_r, self.f_l) = sems
        self.rows = CHUNK // group
        self.half = parts.shape[-1] // 2
        stages = [(self.step_zero, 0), (self.step_core, 1)]
        for k, stage in enumerate(
            (self.step_x, self.step_y, self.step_z, self.step_gather, self.step_end)
        ):
            stages.append((stage, 1 + LAG * (k + 1)))
        self.stages = stages
        self.last = stages[-1][1]

    def remote(self, source, target, send, recv, device):
        return pltpu.make_async_remote_copy(
            src_ref=source, dst_ref=target, send_sem=send, recv_sem=recv,
            device_id=device, device_id_type=MESH,
        )

    def chunk_rows(self, c):
        return pl.ds(pl.multiple_of(c * CHUNK, CHUNK), CHUNK)

    def local_copy(self, c):
        return pltpu.make_async_copy(
            self.parts.at[pl.ds(0, 2), self.chunk_rows(c)], self.own_v.at[c % 2], self.local_s.at[c % 2]
        )

    def core_copy(self, c):
        return self.remote(
            self.parts.at[pl.ds(2, 2), self.chunk_rows(c)], self.core_v.at[c % 4],
            self.core_s.at[c], self.core_r.at[c], self.core,
        )

    def x_copy(self, c):
        return self.remote(
            self.across_v.at[c % 3], self.cross_v.at[c % 6], self.x_s.at[c], self.x_r.at[c], self.across
        )

    def y_copy(self, c):
        return self.remote(
            self.give_v.at[c % 3], self.half_v.at[c % 6], self.y_s.at[c], self.y_r.at[c], self.beside
        )

    def z_copy(self, c, step):
        to = (self.high + step) % self.group
        return self.remote(
            self.slab_v.at[c % 3, pl.ds(pl.multiple_of(to * self.rows, self.rows), self.rows)],
            self.piece_v.at[c % 6, step - 1],
            self.z_s.at[c, step - 1], self.z_r.at[c, step - 1], self.others[step - 1],
        )

    def own_rows(self):
        return pl.ds(pl.multiple_of(self.high * self.rows, self.rows), self.rows)

    def g_copy(self, c, step):
        mine = self.done_v.at[c % 8, self.own_rows()]
        return self.remote(
            mine, mine, self.g_s.at[c, step - 1], self.g_r.at[c, step - 1], self.others[step - 1]
        )

    def target(self, c):
        lanes = pl.ds(pl.multiple_of(self.low * self.half, 128), self.half)
        return self.out.at[self.chunk_rows(c), lanes]

    def f_copy(self, c):
        return self.remote(
            self.done_v.at[c % 8], self.target(c), self.f_s.at[c], self.f_r.at[c], self.beside
        )

    def f_own(self, c):
        return pltpu.make_async_copy(self.done_v.at[c % 8], self.target(c), self.f_l.at[c])

    def step_zero(self, c):
        self.local_copy(c).start()
        self.core_copy(c).start()

    def step_core(self, c):
        self.local_copy(c).wait()
        self.core_copy(c).wait()
        own, came = self.own_v.at[c % 2], self.core_v.at[c % 4]
        self.first_v[c % 3] = own[0].astype(F32) + came[0].astype(F32)
        self.across_v[c % 3] = (own[1].astype(F32) + came[1].astype(F32)).astype(BF16)
        self.x_copy(c).start()

    def step_x(self, c):
        self.x_copy(c).wait()
        total = self.first_v[c % 3] + self.cross_v[c % 6].astype(F32)
        left, right = total[:, : self.half], total[:, self.half :]
        self.keep_v[c % 3] = jnp.where(self.low == 0, left, right)
        self.give_v[c % 3] = jnp.where(self.low == 0, right, left).astype(BF16)
        self.y_copy(c).start()

    def step_y(self, c):
        self.y_copy(c).wait()
        total = self.keep_v[c % 3] + self.half_v[c % 6].astype(F32)
        self.sum_v[c % 3] = total
        self.slab_v[c % 3] = total.astype(BF16)
        for step in range(1, self.group):
            self.z_copy(c, step).start()

    def step_z(self, c):
        total = self.sum_v[c % 3, self.own_rows(), :]
        for step in range(1, self.group):
            self.z_copy(c, step).wait()
            total = total + self.piece_v[c % 6, step - 1].astype(F32)
        self.done_v[c % 8, self.own_rows(), :] = total.astype(BF16)
        for step in range(1, self.group):
            self.g_copy(c, step).start()

    def step_gather(self, c):
        for step in range(1, self.group):
            self.g_copy(c, step).wait()
        self.f_copy(c).start()
        self.f_own(c).start()

    def step_end(self, c):
        self.f_own(c).wait()
        self.f_copy(c).wait()

    def slot(self, at):
        for stage, delay in self.stages:
            c = at - delay
            if isinstance(c, int):
                if 0 <= c < self.count:
                    stage(c)
            else:
                pl.when((c >= 0) & (c < self.count))(functools.partial(stage, c))


def reducer_scratch(count, group, width):
    vmem, dma = pltpu.VMEM, pltpu.SemaphoreType.DMA
    half, piece, rows = width // 2, CHUNK // group, CHUNK
    bufs = [
        vmem((2, 2, rows, width), BF16),
        vmem((4, 2, rows, width), BF16),
        vmem((3, rows, width), BF16),
        vmem((6, rows, width), BF16),
        vmem((3, rows, width), F32),
        vmem((3, rows, half), BF16),
        vmem((6, rows, half), BF16),
        vmem((3, rows, half), F32),
        vmem((6, group - 1, piece, half), BF16),
        vmem((3, rows, half), BF16),
        vmem((3, rows, half), F32),
        vmem((8, rows, half), BF16),
    ]
    sems = [dma((2,))] + [dma((count,))] * 6 + [dma((count, group - 1))] * 4 + [dma((count,))] * 3
    return bufs, sems


LAYER_NAMES = (
    "act", "slope", "normed", "unit_one", "unit_two", "mixed", "q", "k", "v", "pooled_k",
    "pooled_v", "entry", "down", "up", "out", "qkv",
)
LOCAL_NAMES = ("inverse_one", "inverse_two", "lse")


def backward_kernel(group, count, *refs):
    refs = list(refs)
    take = lambda n: [refs.pop(0) for _ in range(n)]
    cot_ref, gains_ref, conv_ref, first_ref, past_ref, keep_ref = take(6)
    layers = []
    for _ in range(LAYERS):
        names = LAYER_NAMES + LOCAL_NAMES
        layers.append(dict(zip(names, take(len(names)))))
    sums_ref, grad_in_ref, parts_ref = take(3)
    bufs, sems = take(12), take(14)
    (g_ref, gm_ref, gr_low, gmix_ref, send_left, send_right, from_right, from_left,
     split_ref, up_ref, whole_ref, load_s, halo_s, store_s, out_s) = take(15)
    total, width = g_ref.shape
    place, seat = lax.axis_index("seq"), lax.axis_index("mp")
    seqs = lax.axis_size("seq")
    red = Reducer(group, count, parts_ref, sums_ref, bufs, sems)
    ahead = seat_of(seq=(place + (seat + 1) // 4) % seqs, mp=(seat + 1) % 4)
    behind = seat_of(seq=(place + seqs - (3 - seat + 1) // 4) % seqs, mp=(seat + 3) % 4)
    barrier = pltpu.get_barrier_semaphore()
    devices = [red.core, red.across, red.beside, ahead, behind] + red.others
    for device in devices:
        pl.semaphore_signal(barrier, inc=1, device_id=device, device_id_type=MESH)
    pl.semaphore_wait(barrier, len(devices))

    split_ref[...] = jnp.zeros_like(split_ref)
    up_ref[...] = jnp.zeros_like(up_ref)
    whole_ref[...] = jnp.zeros_like(whole_ref)
    quarter = width // 4
    feed = 4 * width

    def load(source, target, index):
        copy = pltpu.make_async_copy(source, target, load_s.at[index])
        copy.start()
        return copy

    def place_of(part):
        return (part % 2) * 2 + part // 2

    def norm_back(layer, grad, unit, inverse, gain, result, low_ref, rows_at):
        gain_row, shift_row, bias_row = rows_at

        @pl.loop(0, total // NORM_ROWS)
        def _(block):
            rows = pl.ds(pl.multiple_of(block * NORM_ROWS, NORM_ROWS), NORM_ROWS)
            g, n = grad[rows, :], unit[rows, :]
            a = g * gain
            mean = jnp.sum(a, axis=1, keepdims=True) * (1.0 / width)
            tilt = jnp.sum(a * n, axis=1, keepdims=True) * (1.0 / width)
            back = (a - mean - n * tilt) * inverse[rows, :]
            result[rows, :] = back
            low_ref[rows, :] = back.astype(BF16)
            for at, value in ((gain_row, g * n), (shift_row, g), (bias_row, back)):
                whole_ref[layer, at : at + 1, :] += jnp.sum(value, axis=0, keepdims=True)

    def feed_scope(layer, base, ticks, down, up, act, slope, normed, unit_one, unit_two, out, mixed,
                   gm_low, gn_ref, stage, wide_out):
        ref = layers[layer]
        pairs = ((ref["unit_two"], unit_two), (ref["down"], down), (ref["slope"], slope),
                 (ref["act"], act), (ref["normed"], normed), (ref["up"], up),
                 (ref["unit_one"], unit_one), (ref["out"], out), (ref["mixed"], mixed))
        copies = [load(a, b, i) for i, (a, b) in enumerate(pairs)]
        copies[0].wait()
        norm_back(layer, g_ref, unit_two, ref["inverse_two"], gains_ref[layer, 1:2, :], gm_ref,
                  gm_low, (1, 5, 4))
        gn_ref[...] = gm_ref[...]
        for copy in copies[1:6]:
            copy.wait()
        ticks()
        stores = []
        for j in range(3):
            for copy in stores:
                copy.wait()

            @pl.loop(0, 4)
            def _(part):
                at = pl.multiple_of(part * width + j * CHUNK, CHUNK)
                cols = pl.ds(at, CHUNK)
                pos = place_of(part)
                ga = product_right_t(gm_low[...], down[cols, :])
                gp = ga * slope[:, cols].astype(F32)
                up_ref[layer, pl.ds(part, 1), j * CHUNK : (j + 1) * CHUNK] = jnp.sum(
                    gp, axis=0, keepdims=True
                )
                gp_low = gp.astype(BF16)
                stage[0, pos] = product_left_t(act[:, cols], gm_low[...]).astype(BF16)
                stage[1, pos] = product_left_t(gp_low, normed[...]).astype(BF16)
                gn_ref[...] += product_right_t(gp_low, up[:, cols])

            stores = []
            for kind in range(2):
                at = base + kind * width + j * CHUNK
                copy = pltpu.make_async_copy(
                    stage.at[kind], parts_ref.at[:, pl.ds(at, CHUNK)], store_s.at[kind]
                )
                copy.start()
                stores.append(copy)
            ticks()
        for copy in copies[6:]:
            copy.wait()
        norm_back(layer, gn_ref, unit_one, ref["inverse_one"], gains_ref[layer, 0:1, :], gm_ref,
                  gr_low, (0, 3, 2))
        gmix_ref[...] = product_right_t(gr_low[...], out[...]).astype(BF16)
        wide_out[...] = product_left_t(mixed[...], gr_low[...]).astype(BF16)
        for copy in stores:
            copy.wait()
        store_parts(wide_out, base + 2 * width, 0)
        ticks()

    def part_copies(source, at, bank):
        return [
            pltpu.make_async_copy(
                source.at[pl.ds(part * quarter, quarter)],
                parts_ref.at[place_of(part), pl.ds(at, quarter)],
                out_s.at[bank, part],
            )
            for part in range(4)
        ]

    def store_parts(source, at, bank):
        copies = part_copies(source, at, bank)
        for copy in copies:
            copy.start()
        for copy in copies:
            copy.wait()

    def attend_scope(layer, slot_of, grad_q, grad_k, grad_v, q, k, v, pooled_k, pooled_v,
                     wide_k, wide_v, far_k, far_v, wide_f32):
        ref = layers[layer]
        names = ("q", "k", "v", "pooled_k", "pooled_v")
        copies = [load(ref[n], b, i) for i, (n, b) in enumerate(zip(names, (q, k, v, pooled_k, pooled_v)))]
        for copy in copies:
            copy.wait()
        attend_backward_body(
            q, k, v, pooled_k, pooled_v, gmix_ref, ref["lse"], first_ref, past_ref, keep_ref,
            conv_ref.at[layer], grad_q, grad_k, grad_v, split_ref.at[layer],
            wide_k, wide_v, far_k, far_v, wide_f32, slot_of,
        )

    def project_scope(layer, base, last, grad_q, grad_k, grad_v, qkv, entry, wide, full):
        ref = layers[layer]
        copies = [load(ref["qkv"], qkv, 0), load(ref["entry"], entry, 1)]
        for copy in copies:
            copy.wait()
        wide[...] = product_right_t(grad_k[...], qkv[1])
        wide[...] += product_right_t(grad_v[...], qkv[2])
        send_left[...] = wide[LEFT - LEFT_SENT : LEFT, :].astype(BF16)
        send_right[...] = wide[LEFT + total :, :].astype(BF16)
        halo = [
            red.remote(send_left, from_right, halo_s.at[layer, 0], halo_s.at[layer, 1], behind),
            red.remote(send_right, from_left, halo_s.at[layer, 2], halo_s.at[layer, 3], ahead),
        ]
        for copy in halo:
            copy.start()
        own = slice(LEFT, LEFT + total)
        gm_ref[...] += wide[own, :]
        gm_ref[...] += product_right_t(grad_q[...], qkv[0])
        banks = []
        for which, (grad, rows) in enumerate(((grad_q, own), (grad_k, slice(None)), (grad_v, slice(None)))):
            bank = which % 2
            if which >= 2:
                for copy in banks[which - 2]:
                    copy.wait()
            full[bank] = product_left_t(grad[...], entry[rows, :]).astype(BF16)
            copies = part_copies(full.at[bank], base + 2 * width + (which + 1) * quarter, bank)
            for copy in copies:
                copy.start()
            banks.append(copies)
        for copies in banks[1:]:
            for copy in copies:
                copy.wait()
        for copy in halo:
            copy.wait()
        index = place * 4 + seat
        right = jnp.where(index == 4 * seqs - 1, 0.0, 1.0)
        left = jnp.where(index == 0, 0.0, 1.0)
        gm_ref[total - LEFT_SENT :, :] += from_right[...].astype(F32) * right
        gm_ref[:RIGHT, :] += from_left[...].astype(F32) * left

    slots = [0]
    state = {"next": 0}

    def tick(limit):
        def run():
            if state["next"] < limit:
                red.slot(state["next"])
                state["next"] += 1
        return run

    def loop_ticks(number):
        begin = state["next"]
        state["next"] += number
        return lambda step: red.slot(begin + step)

    start = load(cot_ref, gr_low, 0)
    start.wait()
    g_ref[...] = gr_low[...].astype(F32)
    vmem = pltpu.VMEM
    block = (total, width)
    wide_rows = total + LEFT + RIGHT
    far_rows = total // 4 + 2 * POOL_REACH
    pairs = width // PAIR
    for turn, layer in enumerate(reversed(range(LAYERS))):
        base = turn * LAYER_ROWS
        state["calls"] = 0

        def ticks():
            state["calls"] += 1
            if turn > 0 or state["calls"] >= 4:
                tick(count)()

        pl.run_scoped(
            functools.partial(feed_scope, layer, base, ticks),
            vmem((feed, width), BF16), vmem((width, feed), BF16), vmem((total, feed), BF16),
            vmem((total, feed), BF16), vmem(block, BF16), vmem(block, F32), vmem(block, F32),
            vmem((width, width), BF16), vmem(block, BF16), vmem(block, BF16), vmem(block, F32),
            vmem((2, 4, CHUNK, width), BF16), vmem((width, width), BF16),
        )

        def attention(grad_q, grad_k, grad_v):
            pl.run_scoped(
                functools.partial(attend_scope, layer, loop_ticks(total // TILE), grad_q, grad_k, grad_v),
                vmem(block, BF16), vmem((wide_rows, width), BF16), vmem((wide_rows, width), BF16),
                vmem((far_rows, width), BF16), vmem((far_rows, width), BF16),
                vmem((pairs, wide_rows, PAIR), F32), vmem((pairs, wide_rows, PAIR), F32),
                vmem((far_rows, width), F32), vmem((far_rows, width), F32),
                vmem((wide_rows, PAIR), F32),
            )
            pl.run_scoped(
                functools.partial(project_scope, layer, base, turn == LAYERS - 1, grad_q, grad_k, grad_v),
                vmem((3, width, width), BF16), vmem((wide_rows, width), BF16),
                vmem((wide_rows, width), F32), vmem((2, width, width), BF16),
            )

        pl.run_scoped(
            attention, vmem(block, BF16), vmem((wide_rows, width), BF16), vmem((wide_rows, width), BF16)
        )
        g_ref[...] = gm_ref[...]

    final = pltpu.make_async_copy(g_ref, grad_in_ref, load_s.at[0])
    final.start()

    def small_scope(stage):
        stage[...] = jnp.zeros_like(stage)
        for layer in range(LAYERS):
            at = 32 * layer
            for part in range(4):
                pos = place_of(part)
                rolled = split_ref[layer]
                if part:
                    rolled = pltpu.roll(rolled, width - part * quarter, 1)
                stage[pos, at : at + 16, :] = rolled.astype(BF16)
                rest = jnp.concatenate([whole_ref[layer], up_ref[layer, part : part + 1, :]] + [jnp.zeros((7, width), F32)], axis=0)
                stage[pos, at + 16 : at + 32, :] = rest.astype(BF16)
        copy = pltpu.make_async_copy(
            stage, parts_ref.at[:, pl.ds(LAYERS * LAYER_ROWS, SMALL_ROWS)], store_s.at[0]
        )
        copy.start()
        copy.wait()

    pl.run_scoped(small_scope, vmem((4, SMALL_ROWS, width), BF16))

    @pl.loop(state["next"], count + red.last)
    def _(at):
        red.slot(at)

    final.wait()


def backward(cot, gains, conv, first, past, keep, saved):
    total, width = cot.shape
    group = lax.axis_size("seq") // 2
    rows = LAYERS * LAYER_ROWS + SMALL_ROWS
    count = rows // CHUNK
    vmem, dma = pltpu.VMEM, pltpu.SemaphoreType.DMA
    anywhere = pl.BlockSpec(memory_space=pl.ANY)
    local = pl.BlockSpec(memory_space=pltpu.VMEM)
    args = [cot, gains, conv, first, past, keep]
    specs = [anywhere] + [local] * 5
    for layer in saved:
        args += [layer[name] for name in LAYER_NAMES + LOCAL_NAMES]
        specs += [anywhere] * len(LAYER_NAMES) + [local] * len(LOCAL_NAMES)
    bufs, sems = reducer_scratch(count, group, width)
    shape = jax.ShapeDtypeStruct
    return pl.pallas_call(
        functools.partial(backward_kernel, group, count),
        out_shape=(
            shape((rows, width), BF16),
            shape((total, width), F32),
            shape((4, rows, width), BF16),
        ),
        in_specs=specs,
        out_specs=(anywhere,) * 3,
        scratch_shapes=bufs + sems + [
            vmem((total, width), F32),
            vmem((total, width), F32),
            vmem((total, width), BF16),
            vmem((total, width), BF16),
            vmem((LEFT_SENT, width), BF16),
            vmem((RIGHT, width), BF16),
            vmem((LEFT_SENT, width), BF16),
            vmem((RIGHT, width), BF16),
            vmem((LAYERS, 16, width), F32),
            vmem((LAYERS, 8, width), F32),
            vmem((LAYERS, 8, width), F32),
            dma((9,)),
            dma((LAYERS, 4)),
            dma((2,)),
            dma((2, 4)),
        ],
        compiler_params=pltpu.CompilerParams(
            collective_id=0, has_side_effects=True, vmem_limit_bytes=60 * 1024 * 1024
        ),
        name="backward",
    )(*args)


def shards(
    inputs,
    doc_bounds,
    qkv_weight,
    qv_bias,
    conv_weight,
    conv_bias,
    out_weight,
    up_weight,
    up_bias,
    down_weight,
    norm_gains,
    shared_biases,
    cotangent,
):
    total, width = inputs.shape
    place = lax.axis_index("mp")
    base_row = lax.axis_index("seq") * doc_bounds.shape[1] + place * total
    bounds = lax.dynamic_slice_in_dim(doc_bounds, place * total, total, 1)
    keep = jnp.pad(tap_mask(bounds[0], bounds[1], base_row).astype(F32), ((0, 0), (0, 3)))
    near_bounds = (bounds - base_row).reshape(2, total // TILE, 1, TILE)
    masks = (near_bounds[0], near_bounds[1], keep)
    quarter = width // 4
    small = jnp.concatenate(
        [
            qv_bias.reshape(-1, quarter),
            conv_weight.reshape(-1, quarter),
            conv_bias.reshape(-1, quarter),
            up_bias.reshape(-1, quarter),
        ],
        axis=0,
    )
    small = gather_small(small)
    layers = []
    for index in range(LAYERS):
        qkv = jnp.concatenate(gather_parts(qkv_weight[index]), axis=2)
        out = jnp.concatenate(gather_parts(out_weight[index]), axis=0)
        up = jnp.concatenate(gather_parts(up_weight[index]), axis=1)
        down = jnp.concatenate(gather_parts(down_weight[index]), axis=0)
        layers.append((qkv, out, up, down))
    wide_small = jnp.concatenate(small, axis=1)
    qv_all = wide_small[:4].reshape(2, 2, width)
    conv_all = wide_small[4:24].reshape(2, 2, 5, width)
    conv_bias_all = wide_small[24:28].reshape(2, 2, width)
    up_bias_all = jnp.stack([part[28:].reshape(2, -1) for part in small], axis=1).reshape(2, -1)
    hidden = inputs.astype(F32)
    stack = []
    for index in range(LAYERS):
        qkv, out, up, down = layers[index]
        weights = (
            qkv,
            qv_all[index],
            conv_all[index],
            conv_bias_all[index],
            out,
            up,
            up_bias_all[index],
            down,
            norm_gains[index],
            shared_biases[index],
        )
        hidden, saved = layer_forward(hidden, masks, weights)
        stack.append(saved)
    sums, gradient, _ = backward(
        cotangent, norm_gains, conv_all, near_bounds[0], near_bounds[1], keep, stack
    )
    sums = sums.astype(F32)
    per_layer = sums[: LAYERS * LAYER_ROWS].reshape(LAYERS, LAYER_ROWS, width)
    per_layer = jnp.stack([per_layer[1], per_layer[0]])
    small = sums[LAYERS * LAYER_ROWS :][: 32 * LAYERS].reshape(LAYERS, 32, width)
    units = down_weight.shape[1]
    grad_down = per_layer[:, :units]
    grad_up = per_layer[:, units : 2 * units].transpose(0, 2, 1)
    rest = per_layer[:, 2 * units :].reshape(LAYERS, 4, quarter, width)
    split = small[:, :14, :quarter]
    return (
        hidden,
        gradient,
        rest[:, 1:].transpose(0, 1, 3, 2),
        split[:, :2],
        split[:, 2:12].reshape(LAYERS, 2, 5, quarter),
        split[:, 12:14],
        rest[:, 0],
        grad_up,
        small[:, 24],
        grad_down,
        small[:, 16:18],
        small[:, 18:22],
    )


def solution(mesh):
    return jax.shard_map(
        shards,
        mesh=mesh,
        in_specs=(
            P(BOTH, None),
            P(None, "seq"),
            P(None, None, None, "mp"),
            P(None, None, "mp"),
            P(None, None, None, "mp"),
            P(None, None, "mp"),
            P(None, "mp", None),
            P(None, None, "mp"),
            P(None, "mp"),
            P(None, "mp", None),
            P(),
            P(),
            P(BOTH, None),
        ),
        out_specs=(
            P(BOTH, None),
            P(BOTH, None),
            P(None, None, None, "mp"),
            P(None, None, "mp"),
            P(None, None, None, "mp"),
            P(None, None, "mp"),
            P(None, "mp", None),
            P(None, None, "mp"),
            P(None, "mp"),
            P(None, "mp", None),
            P(),
            P(),
        ),
        check_vma=False,
    )
```

```python
import functools

import jax
import jax.numpy as jnp
from jax import lax
from jax.experimental import pallas as pl
from jax.experimental.pallas import tpu as pltpu
from jax.sharding import PartitionSpec as P

HEAD_DIM = 64
LAYERS = 2
WINDOW = 64
POOL_REACH = 64
NORM_EPSILON = 1e-05
LEFT = 320
LEFT_SENT = 272
RIGHT = 256
BOTH = ("seq", "mp")
BF16 = jnp.bfloat16
F32 = jnp.float32


def product(left, right):
    return jnp.dot(left, right, preferred_element_type=F32)


def product_left_t(left, right):
    return lax.dot_general(left, right, (((0,), (0,)), ((), ())), preferred_element_type=F32)


def product_right_t(left, right):
    return lax.dot_general(left, right, (((1,), (1,)), ((), ())), preferred_element_type=F32)


def tap_mask(starts, finish, base_row):
    count = starts.shape[0] // 4
    reach = (POOL_REACH,)
    first = jnp.concatenate(
        [
            jnp.broadcast_to(starts[:1], reach),
            starts.reshape(count, 4)[:, 0],
            jnp.broadcast_to(starts[-1:], reach),
        ]
    )
    past = jnp.concatenate(
        [
            jnp.broadcast_to(finish[:1], reach),
            finish.reshape(count, 4)[:, 0],
            jnp.broadcast_to(finish[-1:], reach),
        ]
    )
    places = (
        base_row
        + 4 * (jnp.arange(count + 2 * POOL_REACH, dtype=jnp.int32)[:, None] - POOL_REACH)
        + jnp.arange(5, dtype=jnp.int32)[None]
        - 2
    )
    return (places >= first[:, None]) & (places < past[:, None])


PAIR = 128
TILE = 128
SPAN = TILE + 2 * WINDOW
POOL_SPAN = TILE // 4 + 2 * POOL_REACH
FAR = -1e30


def tile_bias(tile, first, past):
    lane = lax.broadcasted_iota(jnp.int32, (1, TILE), 1) + tile * TILE
    near = lax.broadcasted_iota(jnp.int32, (SPAN, 1), 0) + (tile * TILE - WINDOW)
    far = 4 * (lax.broadcasted_iota(jnp.int32, (POOL_SPAN, 1), 0) + (tile * (TILE // 4) - POOL_REACH))

    def one(keys, reach):
        low = jnp.maximum(lane - reach, first)
        high = jnp.minimum(lane + reach + 1, past)
        return jnp.where((keys >= low) & (keys < high), 0.0, FAR)

    return jnp.concatenate([one(near, WINDOW), one(far, 4 * POOL_REACH)], axis=0)


def pair_mask():
    return lax.broadcasted_iota(jnp.int32, (1, PAIR), 1) < HEAD_DIM


def stacked(rows):
    left = pair_mask()
    zero = jnp.zeros_like(rows)
    return jnp.concatenate([jnp.where(left, rows, zero), jnp.where(left, zero, rows)], axis=0)


def keys_of(wide_ref, pooled_ref, tile, lanes):
    near = wide_ref[pl.ds(pl.multiple_of(LEFT - WINDOW + tile * TILE, TILE), SPAN), lanes]
    far = pooled_ref[pl.ds(pl.multiple_of(tile * (TILE // 4), TILE // 4), POOL_SPAN), lanes]
    return jnp.concatenate([near, far], axis=0)


def unstack(both):
    return jnp.concatenate([both[:HEAD_DIM, :TILE], both[HEAD_DIM:, TILE:]], axis=0)


def pool_into(wide_ref, wide_f32, keep_ref, taps, shift_row, pooled_ref, pairs):
    count = pooled_ref.shape[0]
    begin = LEFT - 4 * POOL_REACH - 2
    for pair in pairs:
        lanes = slice(pair * PAIR, (pair + 1) * PAIR)
        wide_f32[...] = wide_ref[:, lanes].astype(F32)
        total = jnp.broadcast_to(shift_row[:, lanes], (count, PAIR))
        for tap in range(5):
            rows = wide_f32[pl.ds(begin + tap, count, stride=4), :]
            kept = jnp.where(keep_ref[:, tap : tap + 1] > 0.0, rows, 0.0)
            total = total + kept * taps(tap)[:, lanes]
        pooled_ref[:, lanes] = total.astype(BF16)


def attend_backward_body(
    q_ref, k_ref, v_ref, pooled_k_ref, pooled_v_ref, grad_ref, lse_ref,
    first_ref, past_ref, keep_ref, conv_ref,
    grad_q_ref, grad_k_ref, grad_v_ref, small_ref,
    wide_k, wide_v, far_k, far_v, wide_f32, slot_of,
):
    pairs = q_ref.shape[1] // PAIR
    wide_k[...] = jnp.zeros_like(wide_k)
    wide_v[...] = jnp.zeros_like(wide_v)
    far_k[...] = jnp.zeros_like(far_k)
    far_v[...] = jnp.zeros_like(far_v)
    small_ref[...] = jnp.zeros_like(small_ref)

    @pl.loop(0, q_ref.shape[0] // TILE)
    def _(tile):
        rows = pl.ds(pl.multiple_of(tile * TILE, TILE), TILE)
        near = pl.ds(pl.multiple_of(LEFT - WINDOW + tile * TILE, TILE), SPAN)
        far = pl.ds(pl.multiple_of(tile * (TILE // 4), TILE // 4), POOL_SPAN)
        bias = tile_bias(tile, first_ref[tile], past_ref[tile])
        bias = jnp.concatenate([bias, bias], axis=1)
        for pair in range(pairs):
            lanes = slice(pair * PAIR, (pair + 1) * PAIR)
            query = stacked(q_ref[rows, lanes] * BF16(HEAD_DIM**-0.5))
            grad = stacked(grad_ref[rows, lanes])
            key = keys_of(k_ref, pooled_k_ref, tile, lanes)
            value = keys_of(v_ref, pooled_v_ref, tile, lanes)
            scores = product_right_t(key, query) + bias
            probs = jnp.exp(scores - lse_ref[tile, pair : pair + 1, :])
            grad_probs = product_right_t(value, grad)
            delta = jnp.sum(probs * grad_probs, axis=0, keepdims=True)
            grad_scores = (probs * (grad_probs - delta)).astype(BF16)
            grad_value = product(probs.astype(BF16), grad)
            grad_key = product(grad_scores, query)
            wide_v[pair, near, :] += grad_value[:SPAN]
            far_v[far, lanes] += grad_value[SPAN:]
            wide_k[pair, near, :] += grad_key[:SPAN]
            far_k[far, lanes] += grad_key[SPAN:]
            grad_query = unstack(product_left_t(key, grad_scores)).T * (HEAD_DIM**-0.5)
            grad_q_ref[rows, lanes] = grad_query.astype(BF16)
            small_ref[0:1, lanes] += jnp.sum(grad_query, axis=0, keepdims=True)
        slot_of(tile)

    count = far_k.shape[0]
    begin = LEFT - 4 * POOL_REACH - 2
    for which, (source, wide, pooled, result) in enumerate(
        ((k_ref, wide_k, far_k, grad_k_ref), (v_ref, wide_v, far_v, grad_v_ref))
    ):
        for pair in range(pairs):
            lanes = slice(pair * PAIR, (pair + 1) * PAIR)
            wide_f32[...] = source[:, lanes].astype(F32)
            grad = pooled[:, lanes]
            at = 12 + which
            small_ref[at : at + 1, lanes] = jnp.sum(grad, axis=0, keepdims=True)
            for tap in range(5):
                places = pl.ds(begin + tap, count, stride=4)
                kept = jnp.where(keep_ref[:, tap : tap + 1] > 0.0, grad, 0.0)
                at = 2 + 5 * which + tap
                small_ref[at : at + 1, lanes] = jnp.sum(
                    kept * wide_f32[places, :], axis=0, keepdims=True
                )
                wide[pair, places, :] += kept * conv_ref[which, tap : tap + 1, lanes]
            if which == 1:
                small_ref[1:2, lanes] = jnp.sum(wide[pair], axis=0, keepdims=True)
            result[:, lanes] = wide[pair].astype(BF16)


def gelu_parts(pre):
    size = jnp.abs(pre) * (0.5**0.5)
    t = 1.0 / (1.0 + 0.5 * size)
    series = 0.17087277
    for term in (-0.82215223, 1.48851587, -1.13520398, 0.27886807, -0.18628806, 0.09678418,
                 0.37409196, 1.00002368, -1.26551223):
        series = series * t + term
    tail = 0.5 * t * jnp.exp(series - size * size)
    cdf = jnp.where(pre < 0.0, tail, 1.0 - tail)
    density = jnp.exp(-0.5 * pre * pre) * (0.5 / jnp.pi) ** 0.5
    return pre * cdf, cdf + pre * density


CHUNK = 256
LAG = 2
MESH = pl.DeviceIdType.MESH
LAYER_ROWS = 2304
SMALL_ROWS = 256
NORM_ROWS = 64


def seat_of(seq=None, mp=None):
    return {
        "seq": lax.axis_index("seq") if seq is None else seq,
        "mp": lax.axis_index("mp") if mp is None else mp,
    }


class Reducer:
    def __init__(self, group, count, parts, out, bufs, sems):
        place, seat = lax.axis_index("seq"), lax.axis_index("mp")
        self.group, self.count, self.parts, self.out = group, count, parts, out
        self.low, self.high = place % 2, place // 2
        self.core = seat_of(mp=seat + 1 - 2 * (seat % 2))
        self.across = seat_of(mp=(seat + 2) % 4)
        self.beside = seat_of(seq=place + 1 - 2 * self.low)
        self.others = [
            seat_of(seq=((self.high + step) % group) * 2 + self.low) for step in range(1, group)
        ]
        (self.own_v, self.core_v, self.across_v, self.cross_v, self.first_v, self.give_v,
         self.half_v, self.keep_v, self.piece_v, self.slab_v, self.sum_v, self.done_v) = bufs
        (self.local_s, self.core_s, self.core_r, self.x_s, self.x_r, self.y_s, self.y_r,
         self.z_s, self.z_r, self.g_s, self.g_r, self.f_s, self.f_r, self.f_l) = sems
        self.rows = CHUNK // group
        self.half = parts.shape[-1] // 2
        stages = [(self.step_zero, 0), (self.step_core, 1)]
        for k, stage in enumerate(
            (self.step_x, self.step_y, self.step_z, self.step_gather, self.step_end)
        ):
            stages.append((stage, 1 + LAG * (k + 1)))
        self.stages = stages
        self.last = stages[-1][1]

    def remote(self, source, target, send, recv, device):
        return pltpu.make_async_remote_copy(
            src_ref=source, dst_ref=target, send_sem=send, recv_sem=recv,
            device_id=device, device_id_type=MESH,
        )

    def chunk_rows(self, c):
        return pl.ds(pl.multiple_of(c * CHUNK, CHUNK), CHUNK)

    def local_copy(self, c):
        return pltpu.make_async_copy(
            self.parts.at[pl.ds(0, 2), self.chunk_rows(c)], self.own_v.at[c % 2], self.local_s.at[c % 2]
        )

    def core_copy(self, c):
        return self.remote(
            self.parts.at[pl.ds(2, 2), self.chunk_rows(c)], self.core_v.at[c % 4],
            self.core_s.at[c], self.core_r.at[c], self.core,
        )

    def x_copy(self, c):
        return self.remote(
            self.across_v.at[c % 3], self.cross_v.at[c % 6], self.x_s.at[c], self.x_r.at[c], self.across
        )

    def y_copy(self, c):
        return self.remote(
            self.give_v.at[c % 3], self.half_v.at[c % 6], self.y_s.at[c], self.y_r.at[c], self.beside
        )

    def z_copy(self, c, step):
        to = (self.high + step) % self.group
        return self.remote(
            self.slab_v.at[c % 3, pl.ds(pl.multiple_of(to * self.rows, self.rows), self.rows)],
            self.piece_v.at[c % 6, step - 1],
            self.z_s.at[c, step - 1], self.z_r.at[c, step - 1], self.others[step - 1],
        )

    def own_rows(self):
        return pl.ds(pl.multiple_of(self.high * self.rows, self.rows), self.rows)

    def g_copy(self, c, step):
        mine = self.done_v.at[c % 8, self.own_rows()]
        return self.remote(
            mine, mine, self.g_s.at[c, step - 1], self.g_r.at[c, step - 1], self.others[step - 1]
        )

    def target(self, c):
        lanes = pl.ds(pl.multiple_of(self.low * self.half, 128), self.half)
        layer_chunks = LAYER_ROWS // CHUNK
        turned = (c + (LAYERS - 1) * layer_chunks) % (LAYERS * layer_chunks)
        at = turned if isinstance(c, int) else jnp.where(c < LAYERS * layer_chunks, turned, c)
        if isinstance(c, int) and c >= LAYERS * layer_chunks:
            at = c
        return self.out.at[self.chunk_rows(at), lanes]

    def f_copy(self, c):
        return self.remote(
            self.done_v.at[c % 8], self.target(c), self.f_s.at[c], self.f_r.at[c], self.beside
        )

    def f_own(self, c):
        return pltpu.make_async_copy(self.done_v.at[c % 8], self.target(c), self.f_l.at[c])

    def step_zero(self, c):
        self.local_copy(c).start()
        self.core_copy(c).start()

    def step_core(self, c):
        self.local_copy(c).wait()
        self.core_copy(c).wait()
        own, came = self.own_v.at[c % 2], self.core_v.at[c % 4]
        self.first_v[c % 3] = own[0].astype(F32) + came[0].astype(F32)
        self.across_v[c % 3] = (own[1].astype(F32) + came[1].astype(F32)).astype(BF16)
        self.x_copy(c).start()

    def step_x(self, c):
        self.x_copy(c).wait()
        total = self.first_v[c % 3] + self.cross_v[c % 6].astype(F32)
        left, right = total[:, : self.half], total[:, self.half :]
        self.keep_v[c % 3] = jnp.where(self.low == 0, left, right)
        self.give_v[c % 3] = jnp.where(self.low == 0, right, left).astype(BF16)
        self.y_copy(c).start()

    def step_y(self, c):
        self.y_copy(c).wait()
        total = self.keep_v[c % 3] + self.half_v[c % 6].astype(F32)
        self.sum_v[c % 3] = total
        self.slab_v[c % 3] = total.astype(BF16)
        for step in range(1, self.group):
            self.z_copy(c, step).start()

    def step_z(self, c):
        total = self.sum_v[c % 3, self.own_rows(), :]
        for step in range(1, self.group):
            self.z_copy(c, step).wait()
            total = total + self.piece_v[c % 6, step - 1].astype(F32)
        self.done_v[c % 8, self.own_rows(), :] = total.astype(BF16)
        for step in range(1, self.group):
            self.g_copy(c, step).start()

    def step_gather(self, c):
        for step in range(1, self.group):
            self.g_copy(c, step).wait()
        self.f_copy(c).start()
        self.f_own(c).start()

    def step_end(self, c):
        self.f_own(c).wait()
        self.f_copy(c).wait()

    def slot(self, at):
        for stage, delay in self.stages:
            c = at - delay
            if isinstance(c, int):
                if 0 <= c < self.count:
                    stage(c)
            else:
                pl.when((c >= 0) & (c < self.count))(functools.partial(stage, c))


def reducer_scratch(count, group, width):
    vmem, dma = pltpu.VMEM, pltpu.SemaphoreType.DMA
    half, piece, rows = width // 2, CHUNK // group, CHUNK
    bufs = [
        vmem((2, 2, rows, width), BF16),
        vmem((4, 2, rows, width), BF16),
        vmem((3, rows, width), BF16),
        vmem((6, rows, width), BF16),
        vmem((3, rows, width), F32),
        vmem((3, rows, half), BF16),
        vmem((6, rows, half), BF16),
        vmem((3, rows, half), F32),
        vmem((6, group - 1, piece, half), BF16),
        vmem((3, rows, half), BF16),
        vmem((3, rows, half), F32),
        vmem((8, rows, half), BF16),
    ]
    sems = [dma((2,))] + [dma((count,))] * 6 + [dma((count, group - 1))] * 4 + [dma((count,))] * 3
    return bufs, sems


LAYER_NAMES = (
    "act", "slope", "normed", "unit_one", "unit_two", "mixed", "q", "k", "v", "pooled_k",
    "pooled_v", "entry", "down", "up", "out", "qkv",
)
LOCAL_NAMES = ("inverse_one", "inverse_two", "lse")


def backward_kernel(group, count, *refs):
    refs = list(refs)
    take = lambda n: [refs.pop(0) for _ in range(n)]
    cot_ref, gains_ref, conv_ref, first_ref, past_ref, keep_ref = take(6)
    layers = []
    for _ in range(LAYERS):
        names = LAYER_NAMES + LOCAL_NAMES
        layers.append(dict(zip(names, take(len(names)))))
    sums_ref, grad_in_ref, parts_ref = take(3)
    bufs, sems = take(12), take(14)
    (g_ref, gm_ref, gr_low, gmix_ref, send_left, send_right, from_right, from_left,
     split_ref, up_ref, whole_ref, load_s, halo_s, store_s, out_s) = take(15)
    total, width = g_ref.shape
    place, seat = lax.axis_index("seq"), lax.axis_index("mp")
    seqs = lax.axis_size("seq")
    red = Reducer(group, count, parts_ref, sums_ref, bufs, sems)
    ahead = seat_of(seq=(place + (seat + 1) // 4) % seqs, mp=(seat + 1) % 4)
    behind = seat_of(seq=(place + seqs - (3 - seat + 1) // 4) % seqs, mp=(seat + 3) % 4)
    barrier = pltpu.get_barrier_semaphore()
    devices = [red.core, red.across, red.beside, ahead, behind] + red.others
    for device in devices:
        pl.semaphore_signal(barrier, inc=1, device_id=device, device_id_type=MESH)
    pl.semaphore_wait(barrier, len(devices))

    split_ref[...] = jnp.zeros_like(split_ref)
    up_ref[...] = jnp.zeros_like(up_ref)
    whole_ref[...] = jnp.zeros_like(whole_ref)
    quarter = width // 4
    feed = 4 * width

    def load(source, target, index):
        copy = pltpu.make_async_copy(source, target, load_s.at[index])
        copy.start()
        return copy

    def place_of(part):
        return (part % 2) * 2 + part // 2

    def norm_back(layer, grad, unit, inverse, gain, result, low_ref, rows_at):
        gain_row, shift_row, bias_row = rows_at

        @pl.loop(0, total // NORM_ROWS)
        def _(block):
            rows = pl.ds(pl.multiple_of(block * NORM_ROWS, NORM_ROWS), NORM_ROWS)
            g, n = grad[rows, :], unit[rows, :]
            a = g * gain
            mean = jnp.sum(a, axis=1, keepdims=True) * (1.0 / width)
            tilt = jnp.sum(a * n, axis=1, keepdims=True) * (1.0 / width)
            back = (a - mean - n * tilt) * inverse[rows, :]
            result[rows, :] = back
            low_ref[rows, :] = back.astype(BF16)
            for at, value in ((gain_row, g * n), (shift_row, g), (bias_row, back)):
                whole_ref[layer, at : at + 1, :] += jnp.sum(value, axis=0, keepdims=True)

    def feed_scope(layer, base, ticks, down, up, act, slope, normed, unit_one, unit_two, out, mixed,
                   gm_low, gn_ref, stage_down, stage_up, wide_out, normed_t):
        ref = layers[layer]
        pairs = ((ref["unit_two"], unit_two), (ref["down"], down), (ref["slope"], slope),
                 (ref["act"], act), (ref["normed"], normed), (ref["up"], up),
                 (ref["unit_one"], unit_one), (ref["out"], out), (ref["mixed"], mixed))
        copies = [load(a, b, i) for i, (a, b) in enumerate(pairs)]
        copies[0].wait()
        norm_back(layer, g_ref, unit_two, ref["inverse_two"], gains_ref[layer, 1:2, :], gm_ref,
                  gm_low, (1, 5, 4))
        gn_ref[...] = gm_ref[...]
        for copy in copies[1:6]:
            copy.wait()
        normed_t[...] = normed[...].T
        ticks()
        stores = []
        for j in range(3):
            for copy in stores:
                copy.wait()

            @pl.loop(0, 4)
            def _(part):
                at = pl.multiple_of(part * width + j * CHUNK, CHUNK)
                cols = pl.ds(at, CHUNK)
                pos = place_of(part)
                ga = product_right_t(gm_low[...], down[cols, :])
                gp = ga * slope[:, cols].astype(F32)
                up_ref[layer, pl.ds(part, 1), j * CHUNK : (j + 1) * CHUNK] = jnp.sum(
                    gp, axis=0, keepdims=True
                )
                gp_low = gp.astype(BF16)
                stage_down[pos] = product_left_t(act[:, cols], gm_low[...]).astype(BF16)
                stage_up[pos] = product(normed_t[...], gp_low).astype(BF16)
                gn_ref[...] += product_right_t(gp_low, up[:, cols])

            stores = []
            for kind, (source, target) in enumerate((
                (stage_down, parts_ref.at[:, pl.ds(base + j * CHUNK, CHUNK)]),
                (stage_up, parts_ref.at[:, pl.ds(base + width, width), pl.ds(j * CHUNK, CHUNK)]),
            )):
                copy = pltpu.make_async_copy(source, target, store_s.at[kind])
                copy.start()
                stores.append(copy)
            ticks()
        for copy in copies[6:]:
            copy.wait()
        norm_back(layer, gn_ref, unit_one, ref["inverse_one"], gains_ref[layer, 0:1, :], gm_ref,
                  gr_low, (0, 3, 2))
        gmix_ref[...] = product_right_t(gr_low[...], out[...]).astype(BF16)
        wide_out[...] = product_left_t(mixed[...], gr_low[...]).astype(BF16)
        for copy in stores:
            copy.wait()
        store_parts(wide_out, base + 2 * width, 0)
        ticks()

    def part_copies(source, at, bank):
        return [
            pltpu.make_async_copy(
                source.at[pl.ds(part * quarter, quarter)],
                parts_ref.at[place_of(part), pl.ds(at, quarter)],
                out_s.at[bank, part],
            )
            for part in range(4)
        ]

    def store_parts(source, at, bank):
        copies = part_copies(source, at, bank)
        for copy in copies:
            copy.start()
        for copy in copies:
            copy.wait()

    def attend_scope(layer, slot_of, grad_q, grad_k, grad_v, q, k, v, pooled_k, pooled_v,
                     wide_k, wide_v, far_k, far_v, wide_f32):
        ref = layers[layer]
        names = ("q", "k", "v", "pooled_k", "pooled_v")
        copies = [load(ref[n], b, i) for i, (n, b) in enumerate(zip(names, (q, k, v, pooled_k, pooled_v)))]
        for copy in copies:
            copy.wait()
        attend_backward_body(
            q, k, v, pooled_k, pooled_v, gmix_ref, ref["lse"], first_ref, past_ref, keep_ref,
            conv_ref.at[layer], grad_q, grad_k, grad_v, split_ref.at[layer],
            wide_k, wide_v, far_k, far_v, wide_f32, slot_of,
        )

    def project_scope(layer, base, last, grad_q, grad_k, grad_v, qkv, entry, wide, full):
        ref = layers[layer]
        copies = [load(ref["qkv"], qkv, 0), load(ref["entry"], entry, 1)]
        for copy in copies:
            copy.wait()
        wide[...] = product(grad_k[...], qkv[1])
        wide[...] += product(grad_v[...], qkv[2])
        send_left[...] = wide[LEFT - LEFT_SENT : LEFT, :].astype(BF16)
        send_right[...] = wide[LEFT + total :, :].astype(BF16)
        halo = [
            red.remote(send_left, from_right, halo_s.at[layer, 0], halo_s.at[layer, 1], behind),
            red.remote(send_right, from_left, halo_s.at[layer, 2], halo_s.at[layer, 3], ahead),
        ]
        for copy in halo:
            copy.start()
        own = slice(LEFT, LEFT + total)
        gm_ref[...] += wide[own, :]
        gm_ref[...] += product(grad_q[...], qkv[0])
        banks = []
        for which, (grad, rows) in enumerate(((grad_q, own), (grad_k, slice(None)), (grad_v, slice(None)))):
            bank = which % 2
            if which >= 2:
                for copy in banks[which - 2]:
                    copy.wait()
            full[bank] = product_left_t(grad[...], entry[rows, :]).astype(BF16)
            copies = part_copies(full.at[bank], base + 2 * width + (which + 1) * quarter, bank)
            for copy in copies:
                copy.start()
            banks.append(copies)
        for copies in banks[1:]:
            for copy in copies:
                copy.wait()
        for copy in halo:
            copy.wait()
        index = place * 4 + seat
        right = jnp.where(index == 4 * seqs - 1, 0.0, 1.0)
        left = jnp.where(index == 0, 0.0, 1.0)
        gm_ref[total - LEFT_SENT :, :] += from_right[...].astype(F32) * right
        gm_ref[:RIGHT, :] += from_left[...].astype(F32) * left

    slots = [0]
    state = {"next": 0}

    def tick(limit):
        def run():
            if state["next"] < limit:
                red.slot(state["next"])
                state["next"] += 1
        return run

    def loop_ticks(number):
        begin = state["next"]
        state["next"] += number
        return lambda step: red.slot(begin + step)

    start = load(cot_ref, gr_low, 0)
    start.wait()
    g_ref[...] = gr_low[...].astype(F32)
    vmem = pltpu.VMEM
    block = (total, width)
    wide_rows = total + LEFT + RIGHT
    far_rows = total // 4 + 2 * POOL_REACH
    pairs = width // PAIR
    for turn, layer in enumerate(reversed(range(LAYERS))):
        base = turn * LAYER_ROWS
        state["calls"] = 0

        def ticks():
            state["calls"] += 1
            if turn > 0 or state["calls"] >= 4:
                tick(count)()

        pl.run_scoped(
            functools.partial(feed_scope, layer, base, ticks),
            vmem((feed, width), BF16), vmem((width, feed), BF16), vmem((total, feed), BF16),
            vmem((total, feed), BF16), vmem(block, BF16), vmem(block, F32), vmem(block, F32),
            vmem((width, width), BF16), vmem(block, BF16), vmem(block, BF16), vmem(block, F32),
            vmem((4, CHUNK, width), BF16), vmem((4, width, CHUNK), BF16), vmem((width, width), BF16),
            vmem((width, total), BF16),
        )

        def attention(grad_q, grad_k, grad_v):
            pl.run_scoped(
                functools.partial(attend_scope, layer, loop_ticks(total // TILE), grad_q, grad_k, grad_v),
                vmem(block, BF16), vmem((wide_rows, width), BF16), vmem((wide_rows, width), BF16),
                vmem((far_rows, width), BF16), vmem((far_rows, width), BF16),
                vmem((pairs, wide_rows, PAIR), F32), vmem((pairs, wide_rows, PAIR), F32),
                vmem((far_rows, width), F32), vmem((far_rows, width), F32),
                vmem((wide_rows, PAIR), F32),
            )
            pl.run_scoped(
                functools.partial(project_scope, layer, base, turn == LAYERS - 1, grad_q, grad_k, grad_v),
                vmem((3, width, width), BF16), vmem((wide_rows, width), BF16),
                vmem((wide_rows, width), F32), vmem((2, width, width), BF16),
            )

        pl.run_scoped(
            attention, vmem(block, BF16), vmem((wide_rows, width), BF16), vmem((wide_rows, width), BF16)
        )
        g_ref[...] = gm_ref[...]

    final = pltpu.make_async_copy(g_ref, grad_in_ref, load_s.at[0])
    final.start()

    def small_scope(stage):
        stage[...] = jnp.zeros_like(stage)
        for layer in range(LAYERS):
            at = 32 * layer
            for part in range(4):
                pos = place_of(part)
                rolled = split_ref[layer]
                if part:
                    rolled = pltpu.roll(rolled, width - part * quarter, 1)
                stage[pos, at : at + 16, :] = rolled.astype(BF16)
                rest = jnp.concatenate([whole_ref[layer], up_ref[layer, part : part + 1, :]] + [jnp.zeros((7, width), F32)], axis=0)
                stage[pos, at + 16 : at + 32, :] = rest.astype(BF16)
        copy = pltpu.make_async_copy(
            stage, parts_ref.at[:, pl.ds(LAYERS * LAYER_ROWS, SMALL_ROWS)], store_s.at[0]
        )
        copy.start()
        copy.wait()

    pl.run_scoped(small_scope, vmem((4, SMALL_ROWS, width), BF16))

    @pl.loop(state["next"], count + red.last)
    def _(at):
        red.slot(at)

    final.wait()


def backward(cot, gains, conv, first, past, keep, saved):
    total, width = cot.shape
    group = lax.axis_size("seq") // 2
    rows = LAYERS * LAYER_ROWS + SMALL_ROWS
    count = rows // CHUNK
    vmem, dma = pltpu.VMEM, pltpu.SemaphoreType.DMA
    anywhere = pl.BlockSpec(memory_space=pl.ANY)
    local = pl.BlockSpec(memory_space=pltpu.VMEM)
    args = [cot, gains, conv, first, past, keep]
    specs = [anywhere] + [local] * 5
    for layer in saved:
        args += [layer[name] for name in LAYER_NAMES + LOCAL_NAMES]
        specs += [anywhere] * len(LAYER_NAMES) + [local] * len(LOCAL_NAMES)
    bufs, sems = reducer_scratch(count, group, width)
    shape = jax.ShapeDtypeStruct
    return pl.pallas_call(
        functools.partial(backward_kernel, group, count),
        out_shape=(
            shape((rows, width), BF16),
            shape((total, width), F32),
            shape((4, rows, width), BF16),
        ),
        in_specs=specs,
        out_specs=(anywhere,) * 3,
        scratch_shapes=bufs + sems + [
            vmem((total, width), F32),
            vmem((total, width), F32),
            vmem((total, width), BF16),
            vmem((total, width), BF16),
            vmem((LEFT_SENT, width), BF16),
            vmem((RIGHT, width), BF16),
            vmem((LEFT_SENT, width), BF16),
            vmem((RIGHT, width), BF16),
            vmem((LAYERS, 16, width), F32),
            vmem((LAYERS, 8, width), F32),
            vmem((LAYERS, 8, width), F32),
            dma((9,)),
            dma((LAYERS, 4)),
            dma((2,)),
            dma((2, 4)),
        ],
        compiler_params=pltpu.CompilerParams(
            collective_id=0, has_side_effects=True, vmem_limit_bytes=60 * 1024 * 1024
        ),
        name="backward",
    )(*args)


def row_blocks(total, size, body):
    @pl.loop(0, total // size)
    def _(block):
        body(pl.ds(pl.multiple_of(block * size, size), size))


def attend_forward_body(
    q_ref, k_ref, v_ref, first_ref, past_ref, keep_ref, taps, shifts,
    mixed_ref, lse_ref, pooled_k_ref, pooled_v_ref, wide_f32, pairs,
):
    for which, (source, pooled) in enumerate(((k_ref, pooled_k_ref), (v_ref, pooled_v_ref))):
        pool_into(source, wide_f32, keep_ref, taps[which], shifts[which], pooled, pairs)

    @pl.loop(0, q_ref.shape[0] // TILE)
    def _(tile):
        rows = pl.ds(pl.multiple_of(tile * TILE, TILE), TILE)
        bias = tile_bias(tile, first_ref[tile], past_ref[tile])
        bias = jnp.concatenate([bias, bias], axis=1)
        for pair in pairs:
            lanes = slice(pair * PAIR, (pair + 1) * PAIR)
            query = stacked(q_ref[rows, lanes] * BF16(HEAD_DIM**-0.5))
            key = keys_of(k_ref, pooled_k_ref, tile, lanes)
            value = keys_of(v_ref, pooled_v_ref, tile, lanes)
            scores = product_right_t(key, query) + bias
            most = jnp.max(scores, axis=0, keepdims=True)
            weight = jnp.exp(scores - most)
            total = jnp.sum(weight, axis=0, keepdims=True)
            both = product_left_t(value, weight.astype(BF16)) * (1.0 / total)
            mixed_ref[rows, lanes] = unstack(both).T.astype(BF16)
            lse_ref[tile, pair : pair + 1, :] = most + jnp.log(total)


SAVED_NAMES = LAYER_NAMES
TENSORS = 4 * LAYERS


def forward_kernel(*refs):
    refs = list(refs)
    take = lambda n: [refs.pop(0) for _ in range(n)]
    (x_ref, qkv_ref, out_ref, up_ref, down_ref, small_ref, gains_ref, biases_ref, first_ref, past_ref,
     keep_ref) = take(11)
    hidden_ref, conv_ref = take(2)
    results = [dict(zip(SAVED_NAMES + LOCAL_NAMES, take(len(SAVED_NAMES + LOCAL_NAMES)))) for _ in range(LAYERS)]
    (qkv_v, out_v, up_v, down_v, entry_v, q_v, k_v, v_v, far_k, far_v, mixed_v, hidden_v, acc_v,
     unit_one, unit_two, low_v, act_v, slope_v, pre_v, wide_f32, small_v, full_v,
     own_s, x_s, x_r, y_s, y_r, c_s, c_r, d_s, d_r, halo_s, save_s, load_s) = take(34)
    total, width = hidden_v.shape
    quarter, half = width // 4, width // 2
    place, seat, seqs = lax.axis_index("seq"), lax.axis_index("mp"), lax.axis_size("seq")
    low = place % 2
    core = seat_of(mp=seat + 1 - 2 * (seat % 2))
    across = seat_of(mp=(seat + 2) % 4)
    beside = seat_of(seq=place + 1 - 2 * low)
    ahead = seat_of(seq=(place + (seat + 1) // 4) % seqs, mp=(seat + 1) % 4)
    behind = seat_of(seq=(place + seqs - (4 - seat) // 4) % seqs, mp=(seat + 3) % 4)
    barrier = pltpu.get_barrier_semaphore()
    devices = [core, across, beside, ahead, behind]
    for device in devices:
        pl.semaphore_signal(barrier, inc=1, device_id=device, device_id_type=MESH)
    entry_own = pl.ds(LEFT, total)
    first_load = pltpu.make_async_copy(x_ref, entry_v.at[0, entry_own], load_s.at[0])
    first_load.start()
    small_load = pltpu.make_async_copy(small_ref, small_v.at[0], load_s.at[1])
    small_load.start()
    for layer in range(LAYERS):
        entry_v[layer, : LEFT - LEFT_SENT, :] = jnp.zeros((LEFT - LEFT_SENT, width), BF16)
    pl.semaphore_wait(barrier, len(devices))

    def remote(source, target, send, recv, device):
        return pltpu.make_async_remote_copy(
            src_ref=source, dst_ref=target, send_sem=send, recv_sem=recv,
            device_id=device, device_id_type=MESH,
        )

    def span(size, side):
        if side is None:
            return 0, size
        return pl.multiple_of(side * (size // 2), size // 2), size // 2

    def shard(tensor, side=None):
        layer, kind = tensor // 4, tensor % 4
        if kind == 0:
            return qkv_ref.at[layer, :, pl.ds(*span(quarter, side))]
        if kind == 1:
            return out_ref.at[layer, pl.ds(*span(quarter, side))]
        return (up_ref if kind == 2 else down_ref).at[layer, pl.ds(*span(width, side))]

    def landed(tensor, part, side=None):
        layer, kind = tensor // 4, tensor % 4
        if kind == 2:
            return up_v.at[layer, pl.ds(*span(width, side)), pl.ds(part * width, width)]
        size = width if kind == 3 else quarter
        at, count = span(size, side)
        rows = pl.ds(part * size + at, count)
        if kind == 0:
            return qkv_v.at[layer, :, rows]
        return (out_v if kind == 1 else down_v).at[layer, rows]

    def own_copy(t):
        return pltpu.make_async_copy(shard(t), landed(t, 0), own_s.at[t])

    def x_copy(t):
        return remote(shard(t, low), landed(t, 2, low), x_s.at[t], x_r.at[t], across)

    def y_copy(t):
        return remote(landed(t, 2, low), landed(t, 2, low), y_s.at[t], y_r.at[t], beside)

    def c_copy(t):
        return remote(shard(t), landed(t, 1), c_s.at[t], c_r.at[t], core)

    def d_copy(t):
        return remote(landed(t, 2), landed(t, 3), d_s.at[t], d_r.at[t], core)

    def gather(step):
        if step < TENSORS:
            own_copy(step).start()
            c_copy(step).start()
            x_copy(step).start()
        if 0 <= step - 2 < TENSORS:
            x_copy(step - 2).wait_recv()
            y_copy(step - 2).start()
        if 0 <= step - 4 < TENSORS:
            y_copy(step - 4).wait_recv()
            d_copy(step - 4).start()

    small_index = TENSORS
    small_x = remote(small_ref, small_v.at[2], x_s.at[small_index], x_r.at[small_index], across)
    small_c = remote(small_ref, small_v.at[1], c_s.at[small_index], c_r.at[small_index], core)
    small_d = remote(small_v.at[2], small_v.at[3], d_s.at[small_index], d_r.at[small_index], core)

    def halo(layer):
        entry = entry_v.at[layer]
        return (
            remote(
                entry.at[pl.ds(LEFT + total - LEFT_SENT, LEFT_SENT)],
                entry.at[pl.ds(LEFT - LEFT_SENT, LEFT_SENT)],
                halo_s.at[layer, 0], halo_s.at[layer, 1], ahead,
            ),
            remote(
                entry.at[pl.ds(LEFT, RIGHT)], entry.at[pl.ds(LEFT + total, RIGHT)],
                halo_s.at[layer, 2], halo_s.at[layer, 3], behind,
            ),
        )

    saves = {}

    def save(layer, name, source):
        index = SAVED_NAMES.index(name)
        copy = pltpu.make_async_copy(source, results[layer][name], save_s.at[layer, index])
        copy.start()
        saves[layer, name] = copy

    def settle(layer, *names):
        for name in names:
            if (layer, name) in saves:
                saves.pop((layer, name)).wait()

    def norm(layer, which, extra, result, low_ref, unit, inverse):
        gain = gains_ref[layer, which : which + 1, :]
        offset = biases_ref[layer, 2 * which + 1 : 2 * which + 2, :]
        shift_row = biases_ref[layer, 2 * which : 2 * which + 1, :]

        def body(rows):
            value = hidden_v[rows, :] + (extra[rows, :] + shift_row)
            average = jnp.sum(value, axis=1, keepdims=True) * (1.0 / width)
            centered = value - average
            spread = jnp.sum(centered * centered, axis=1, keepdims=True) * (1.0 / width)
            scale = lax.rsqrt(spread + NORM_EPSILON)
            one = centered * scale
            out = one * gain + offset
            unit[rows, :] = one
            inverse[rows, :] = scale
            result[rows, :] = out
            if low_ref is not None:
                low_ref[rows, :] = out.astype(BF16)

        row_blocks(total, NORM_ROWS, body)

    first_load.wait()
    for copy in halo(0):
        copy.start()
    small_x.start()
    small_c.start()
    gather(0)
    gather(1)
    row_blocks(total, NORM_ROWS, lambda rows: hidden_v.__setitem__(
        (rows, slice(None)), entry_v[0, pl.ds(rows.start + LEFT, NORM_ROWS), :].astype(F32)))

    for layer in range(LAYERS):
        entry = entry_v.at[layer]
        tensor = 4 * layer
        steps = iter(((2, 3, 4, 5, 6, 7, 8, 9), (10, 11))[layer])

        def advance():
            step = next(steps, None)
            if step is not None:
                gather(step)

        settle(layer - 1, "q", "k", "v", "pooled_k", "pooled_v", "mixed", "normed")

        def project(which, target, side, rows):
            lanes = slice(side * half, (side + 1) * half)
            made = product_right_t(entry[rows, :], qkv_v[layer, which, lanes, :])
            if which != 1:
                row = 2 * layer + which // 2
                made = made + full_v[row : row + 1, lanes]
            target[:, lanes] = made.astype(BF16)

        own_copy(tensor).wait()
        c_copy(tensor).wait_recv()
        if layer == 0:
            small_load.wait()
            small_c.wait_recv()
            small_x.wait_recv()
            small_d.start()
            small_d.wait_recv()
            rows = [small_v[0, :32, :]] + [
                pltpu.roll(small_v[part, :32, :], part * quarter, 1) for part in range(1, 4)
            ]
            full_v[...] = rows[0] + rows[1] + rows[2] + rows[3]
            for one in range(LAYERS):
                for which in range(2):
                    at = 4 + 10 * one + 5 * which
                    conv_ref[one, which] = full_v[at : at + 5, :]
        project(0, q_v, 0, entry_own)
        advance()
        for copy in halo(layer):
            copy.wait_recv()
        everything = slice(None)
        project(1, k_v, 0, everything)
        project(2, v_v, 0, everything)
        save(layer, "entry", entry)
        taps = [
            lambda tap, at=4 + 10 * layer + 5 * which: full_v[at + tap : at + tap + 1, :]
            for which in range(2)
        ]
        shifts = [full_v[24 + 2 * layer + which : 25 + 2 * layer + which, :] for which in range(2)]

        def attend(pairs):
            attend_forward_body(
                q_v, k_v, v_v, first_ref, past_ref, keep_ref, taps, shifts,
                mixed_v, results[layer]["lse"], far_k, far_v, wide_f32, pairs,
            )

        pairs = width // PAIR
        attend(range(pairs // 2))
        advance()
        advance()
        d_copy(tensor).wait_recv()
        project(0, q_v, 1, entry_own)
        project(1, k_v, 1, everything)
        project(2, v_v, 1, everything)
        for name, source in (("q", q_v), ("k", k_v), ("v", v_v)):
            save(layer, name, source)
        advance()
        attend(range(pairs // 2, pairs))
        save(layer, "pooled_k", far_k)
        save(layer, "pooled_v", far_v)
        save(layer, "mixed", mixed_v)
        advance()
        tensor += 1
        own_copy(tensor).wait()
        c_copy(tensor).wait_recv()
        d_copy(tensor).wait_recv()
        acc_v[...] = product(mixed_v[...], out_v[layer])
        settle(layer - 1, "unit_one", "unit_two", "act", "slope")
        norm(layer, 0, acc_v, hidden_v, low_v, unit_one, results[layer]["inverse_one"])
        save(layer, "unit_one", unit_one)
        save(layer, "normed", low_v)
        advance()
        for part in range(4):
            if part == 0:
                own_copy(tensor + 1).wait()
                own_copy(tensor + 2).wait()
            elif part == 1:
                c_copy(tensor + 1).wait_recv()
                c_copy(tensor + 2).wait_recv()
            elif part == 3:
                d_copy(tensor + 1).wait_recv()
                d_copy(tensor + 2).wait_recv()

            @pl.loop(0, 3)
            def _(j):
                at = pl.multiple_of(part * width + j * CHUNK, CHUNK)
                cols = pl.ds(at, CHUNK)
                lanes = pl.ds(pl.multiple_of(j * CHUNK, CHUNK), CHUNK)
                pre_v[...] = product(low_v[...], up_v[layer, :, cols])
                up_row = small_v[part, 32 + layer : 33 + layer, lanes]

                def body(rows):
                    act, slope = gelu_parts(pre_v[rows, :] + up_row)
                    act_v[rows, cols] = act.astype(BF16)
                    slope_v[rows, cols] = slope.astype(BF16)

                row_blocks(total, NORM_ROWS, body)
                made = product(act_v[:, cols], down_v[layer, cols, :])
                if part == 0:
                    @pl.when(j == 0)
                    def _():
                        acc_v[...] = made

                    @pl.when(j > 0)
                    def _():
                        acc_v[...] += made
                else:
                    acc_v[...] += made

            if part in (0, 2):
                advance()
        save(layer, "act", act_v)
        save(layer, "slope", slope_v)
        save(layer, "qkv", qkv_v.at[layer])
        save(layer, "out", out_v.at[layer])
        save(layer, "up", up_v.at[layer])
        save(layer, "down", down_v.at[layer])
        norm(layer, 1, acc_v, hidden_v, low_v if False else None, unit_two, results[layer]["inverse_two"])
        save(layer, "unit_two", unit_two)
        if layer + 1 < LAYERS:
            later = entry_v.at[layer + 1]
            row_blocks(total, NORM_ROWS, lambda rows: later.__setitem__(
                (pl.ds(rows.start + LEFT, NORM_ROWS), slice(None)), hidden_v[rows, :].astype(BF16)))
            for copy in halo(layer + 1):
                copy.start()
    last = pltpu.make_async_copy(hidden_v, hidden_ref, load_s.at[0])
    last.start()
    for key in list(saves):
        settle(*key)
    small_x.wait_send()
    small_c.wait_send()
    small_d.wait_send()
    for t in range(TENSORS):
        for copy in (x_copy(t), y_copy(t), c_copy(t), d_copy(t)):
            copy.wait_send()
    for layer in range(LAYERS):
        for copy in halo(layer):
            copy.wait_send()
    last.wait()


def forward(x, qkv_t, out, up, down, small, gains, biases, first, past, keep):
    total, width = x.shape
    vmem, dma, shape = pltpu.VMEM, pltpu.SemaphoreType.DMA, jax.ShapeDtypeStruct
    anywhere = pl.BlockSpec(memory_space=pl.ANY)
    local = pl.BlockSpec(memory_space=pltpu.VMEM)
    feed, wide_rows, far_rows = 4 * width, total + LEFT + RIGHT, total // 4 + 2 * POOL_REACH
    block, wide, far, square = (total, width), (wide_rows, width), (far_rows, width), (width, width)
    saved = dict(
        act=((total, feed), BF16), slope=((total, feed), BF16), normed=(block, BF16),
        unit_one=(block, F32), unit_two=(block, F32), mixed=(block, BF16), q=(block, BF16),
        k=(wide, BF16), v=(wide, BF16), pooled_k=(far, BF16), pooled_v=(far, BF16), entry=(wide, BF16),
        down=((feed, width), BF16), up=((width, feed), BF16), out=(square, BF16),
        qkv=((3, width, width), BF16), inverse_one=((total, 1), F32), inverse_two=((total, 1), F32),
        lse=((total // TILE, width // PAIR, 2 * TILE), F32),
    )
    names = SAVED_NAMES + LOCAL_NAMES
    shapes = [shape(block, F32), shape((LAYERS, 2, 5, width), F32)]
    specs = [anywhere, local]
    for _ in range(LAYERS):
        shapes += [shape(*saved[name]) for name in names]
        specs += [anywhere] * len(SAVED_NAMES) + [local] * len(LOCAL_NAMES)
    tensors = dma((TENSORS + 1,))
    outs = pl.pallas_call(
        forward_kernel,
        out_shape=tuple(shapes),
        in_specs=[anywhere] * 6 + [local] * 5,
        out_specs=tuple(specs),
        scratch_shapes=[
            vmem((LAYERS, 3, width, width), BF16), vmem((LAYERS, width, width), BF16),
            vmem((LAYERS, width, feed), BF16), vmem((LAYERS, feed, width), BF16),
            vmem((LAYERS, wide_rows, width), BF16),
            vmem(block, BF16), vmem(wide, BF16), vmem(wide, BF16), vmem(far, BF16), vmem(far, BF16),
            vmem(block, BF16), vmem(block, F32), vmem(block, F32), vmem(block, F32), vmem(block, F32),
            vmem(block, BF16), vmem((total, feed), BF16), vmem((total, feed), BF16),
            vmem((total, CHUNK), F32), vmem((wide_rows, PAIR), F32), vmem((4, 40, width), F32),
            vmem((32, width), F32),
            tensors, tensors, tensors, tensors, tensors, tensors, tensors, tensors, tensors,
            dma((LAYERS, 4)), dma((LAYERS, len(SAVED_NAMES))), dma((2,)),
        ],
        compiler_params=pltpu.CompilerParams(
            collective_id=1, has_side_effects=True, vmem_limit_bytes=60 * 1024 * 1024
        ),
        name="forward",
    )(x, qkv_t, out, up, down, small, gains, biases, first, past, keep)
    size = len(names)
    stack = [dict(zip(names, outs[2 + size * one : 2 + size * (one + 1)])) for one in range(LAYERS)]
    return outs[0], outs[1], stack


def shards(
    inputs,
    doc_bounds,
    qkv_weight,
    qv_bias,
    conv_weight,
    conv_bias,
    out_weight,
    up_weight,
    up_bias,
    down_weight,
    norm_gains,
    shared_biases,
    cotangent,
):
    total, width = inputs.shape
    place = lax.axis_index("mp")
    base_row = lax.axis_index("seq") * doc_bounds.shape[1] + place * total
    bounds = lax.dynamic_slice_in_dim(doc_bounds, place * total, total, 1)
    keep = jnp.pad(tap_mask(bounds[0], bounds[1], base_row).astype(F32), ((0, 0), (0, 3)))
    near_bounds = (bounds - base_row).reshape(2, total // TILE, 1, TILE)
    quarter = width // 4
    small = jnp.concatenate(
        [
            qv_bias.reshape(-1, quarter),
            conv_weight.reshape(-1, quarter),
            conv_bias.reshape(-1, quarter),
        ],
        axis=0,
    )
    small = jnp.concatenate(
        [jnp.pad(small, ((0, 32 - small.shape[0]), (0, width - quarter))), jnp.pad(up_bias, ((0, 6), (0, 0)))],
        axis=0,
    )
    hidden, conv_all, stack = forward(
        inputs, qkv_weight.transpose(0, 1, 3, 2), out_weight, up_weight, down_weight, small, norm_gains,
        shared_biases, near_bounds[0], near_bounds[1], keep,
    )
    sums, gradient, _ = backward(
        cotangent, norm_gains, conv_all, near_bounds[0], near_bounds[1], keep, stack
    )
    per_layer = sums[: LAYERS * LAYER_ROWS].reshape(LAYERS, LAYER_ROWS, width)
    small = sums[LAYERS * LAYER_ROWS :][: 32 * LAYERS].reshape(LAYERS, 32, width).astype(F32)
    units = down_weight.shape[1]
    grad_down = per_layer[:, :units].astype(F32)
    grad_up = per_layer[:, units : 2 * units].astype(F32)
    rest = per_layer[:, 2 * units :].reshape(LAYERS, 4, quarter, width)
    split = small[:, :14, :quarter]
    return (
        hidden,
        gradient,
        rest[:, 1:].transpose(0, 1, 3, 2).astype(F32),
        split[:, :2],
        split[:, 2:12].reshape(LAYERS, 2, 5, quarter),
        split[:, 12:14],
        rest[:, 0].astype(F32),
        grad_up,
        small[:, 24],
        grad_down,
        small[:, 16:18],
        small[:, 18:22],
    )


def solution(mesh):
    return jax.shard_map(
        shards,
        mesh=mesh,
        in_specs=(
            P(BOTH, None),
            P(None, "seq"),
            P(None, None, None, "mp"),
            P(None, None, "mp"),
            P(None, None, None, "mp"),
            P(None, None, "mp"),
            P(None, "mp", None),
            P(None, None, "mp"),
            P(None, "mp"),
            P(None, "mp", None),
            P(),
            P(),
            P(BOTH, None),
        ),
        out_specs=(
            P(BOTH, None),
            P(BOTH, None),
            P(None, None, None, "mp"),
            P(None, None, "mp"),
            P(None, None, None, "mp"),
            P(None, None, "mp"),
            P(None, "mp", None),
            P(None, None, "mp"),
            P(None, "mp"),
            P(None, "mp", None),
            P(),
            P(),
        ),
        check_vma=False,
    )
```

```python
import functools

import jax
import jax.numpy as jnp
from jax import lax
from jax.experimental import pallas as pl
from jax.experimental.pallas import tpu as pltpu
from jax.sharding import PartitionSpec as P

HEAD_DIM = 64
LAYERS = 2
WINDOW = 64
POOL_REACH = 64
NORM_EPSILON = 1e-05
LEFT = 320
LEFT_SENT = 272
RIGHT = 256
BOTH = ("seq", "mp")
BF16 = jnp.bfloat16
F32 = jnp.float32


def product(left, right):
    return jnp.dot(left, right, preferred_element_type=F32)


def product_left_t(left, right):
    return lax.dot_general(left, right, (((0,), (0,)), ((), ())), preferred_element_type=F32)


def product_right_t(left, right):
    return lax.dot_general(left, right, (((1,), (1,)), ((), ())), preferred_element_type=F32)


PAIR = 128
TILE = 128
SPAN = TILE + 2 * WINDOW
POOL_SPAN = TILE // 4 + 2 * POOL_REACH
FAR = -1e30


def tile_bias(tile, first, past):
    lane = lax.broadcasted_iota(jnp.int32, (1, TILE), 1) + tile * TILE
    near = lax.broadcasted_iota(jnp.int32, (SPAN, 1), 0) + (tile * TILE - WINDOW)
    far = 4 * (lax.broadcasted_iota(jnp.int32, (POOL_SPAN, 1), 0) + (tile * (TILE // 4) - POOL_REACH))

    def one(keys, reach):
        low = jnp.maximum(lane - reach, first)
        high = jnp.minimum(lane + reach + 1, past)
        return jnp.where((keys >= low) & (keys < high), 0.0, FAR)

    return jnp.concatenate([one(near, WINDOW), one(far, 4 * POOL_REACH)], axis=0)


def pair_mask():
    return lax.broadcasted_iota(jnp.int32, (1, PAIR), 1) < HEAD_DIM


def stacked(rows):
    left = pair_mask()
    zero = jnp.zeros_like(rows)
    return jnp.concatenate([jnp.where(left, rows, zero), jnp.where(left, zero, rows)], axis=0)


def rows_from(at, unit, size):
    return pl.ds(at if isinstance(at, int) else pl.multiple_of(at, unit), size)


def keys_of(wide_ref, pooled_ref, tile, lanes):
    near = wide_ref[rows_from(LEFT - WINDOW + tile * TILE, TILE, SPAN), lanes]
    far = pooled_ref[rows_from(tile * (TILE // 4), TILE // 4, POOL_SPAN), lanes]
    return jnp.concatenate([near, far], axis=0)


def unstack(both):
    return jnp.concatenate([both[:HEAD_DIM, :TILE], both[HEAD_DIM:, TILE:]], axis=0)


def pool_into(wide_ref, wide_f32, keep_ref, taps, shift_row, pooled_ref, pairs):
    count = pooled_ref.shape[0]
    begin = LEFT - 4 * POOL_REACH - 2
    for pair in pairs:
        lanes = slice(pair * PAIR, (pair + 1) * PAIR)
        wide_f32[...] = wide_ref[:, lanes].astype(F32)
        total = jnp.broadcast_to(shift_row[:, lanes], (count, PAIR))
        for tap in range(5):
            rows = wide_f32[pl.ds(begin + tap, count, stride=4), :]
            kept = rows * keep_ref[tap]
            total = total + kept * taps(tap)[:, lanes]
        pooled_ref[:, lanes] = total.astype(BF16)


def attend_backward_body(
    q_ref, k_ref, v_ref, pooled_k_ref, pooled_v_ref, grad_ref, lse_ref,
    bounds_of, keep_ref, conv_ref,
    grad_q_ref, grad_k_ref, grad_v_ref, small_ref,
    wide_k, wide_v, far_k, far_v, wide_f32, tick,
):
    pairs = q_ref.shape[1] // PAIR
    wide_k[...] = jnp.zeros_like(wide_k)
    wide_v[...] = jnp.zeros_like(wide_v)
    far_k[...] = jnp.zeros_like(far_k)
    far_v[...] = jnp.zeros_like(far_v)
    small_ref[...] = jnp.zeros_like(small_ref)

    for tile in range(q_ref.shape[0] // TILE):
        rows = rows_from(tile * TILE, TILE, TILE)
        near = rows_from(LEFT - WINDOW + tile * TILE, TILE, SPAN)
        far = rows_from(tile * (TILE // 4), TILE // 4, POOL_SPAN)
        bias = tile_bias(tile, *bounds_of(tile))
        bias = jnp.concatenate([bias, bias], axis=1)
        for pair in range(pairs):
            lanes = slice(pair * PAIR, (pair + 1) * PAIR)
            query = stacked(q_ref[rows, lanes] * BF16(HEAD_DIM**-0.5))
            grad = stacked(grad_ref[rows, lanes])
            key = keys_of(k_ref, pooled_k_ref, tile, lanes)
            value = keys_of(v_ref, pooled_v_ref, tile, lanes)
            scores = product_right_t(key, query) + bias
            probs = jnp.exp(scores - lse_ref[tile, pair : pair + 1, :])
            grad_probs = product_right_t(value, grad)
            delta = jnp.sum(probs * grad_probs, axis=0, keepdims=True)
            grad_scores = (probs * (grad_probs - delta)).astype(BF16)
            grad_value = product(probs.astype(BF16), grad)
            grad_key = product(grad_scores, query)
            wide_v[pair, near, :] += grad_value[:SPAN]
            far_v[far, lanes] += grad_value[SPAN:]
            wide_k[pair, near, :] += grad_key[:SPAN]
            far_k[far, lanes] += grad_key[SPAN:]
            grad_query = unstack(product_left_t(key, grad_scores)).T * (HEAD_DIM**-0.5)
            grad_q_ref[rows, lanes] = grad_query.astype(BF16)
            small_ref[0:1, lanes] += jnp.sum(grad_query, axis=0, keepdims=True)
        tick(4.0)

    count = far_k.shape[0]
    begin = LEFT - 4 * POOL_REACH - 2
    for which, (source, wide, pooled, result) in enumerate(
        ((k_ref, wide_k, far_k, grad_k_ref), (v_ref, wide_v, far_v, grad_v_ref))
    ):
        for pair in range(pairs):
            lanes = slice(pair * PAIR, (pair + 1) * PAIR)
            wide_f32[...] = source[:, lanes].astype(F32)
            grad = pooled[:, lanes]
            at = 12 + which
            small_ref[at : at + 1, lanes] = jnp.sum(grad, axis=0, keepdims=True)
            for tap in range(5):
                places = pl.ds(begin + tap, count, stride=4)
                kept = grad * keep_ref[tap]
                at = 2 + 5 * which + tap
                small_ref[at : at + 1, lanes] = jnp.sum(
                    kept * wide_f32[places, :], axis=0, keepdims=True
                )
                wide[pair, places, :] += kept * conv_ref[which, tap : tap + 1, lanes]
            if which == 1:
                small_ref[1:2, lanes] = jnp.sum(wide[pair], axis=0, keepdims=True)
            result[:, lanes] = wide[pair].astype(BF16)


def gelu_parts(pre):
    size = jnp.abs(pre) * (0.5**0.5)
    t = 1.0 / (1.0 + 0.5 * size)
    series = 0.17087277
    for term in (-0.82215223, 1.48851587, -1.13520398, 0.27886807, -0.18628806, 0.09678418,
                 0.37409196, 1.00002368, -1.26551223):
        series = series * t + term
    tail = 0.5 * t * jnp.exp(series - size * size)
    cdf = jnp.where(pre < 0.0, tail, 1.0 - tail)
    density = jnp.exp(-0.5 * pre * pre) * (0.5 / jnp.pi) ** 0.5
    return pre * cdf, cdf + pre * density


CHUNK = 256
SENT_RING, LAND_RING, CORE_RING, DONE_RING = 3, 6, 4, 8
LINKS = (("core", 2.2), ("x", 8.9), ("y", 4.45), ("z", 4.45), ("z", 4.45), ("y", 4.45))
LATENCY, AHEAD, PACE = 3.0, 12.0, 1.0
MESH = pl.DeviceIdType.MESH
LAYER_ROWS = 2304
NORM_ROWS = 64


def bounds_reader(bounds_ref, total):
    base = lax.axis_index("seq") * bounds_ref.shape[1] + lax.axis_index("mp") * total

    def read(at, count):
        start = lax.axis_index("mp") * total + at
        lanes = pl.ds(start if isinstance(start, int) else pl.multiple_of(start, TILE), count)
        return bounds_ref[0:1, lanes] - base, bounds_ref[1:2, lanes] - base

    return read


def seat_of(seq=None, mp=None):
    return {
        "seq": lax.axis_index("seq") if seq is None else seq,
        "mp": lax.axis_index("mp") if mp is None else mp,
    }


class Reducer:
    def __init__(self, group, table, parts, out, small_out, bufs, sems):
        place, seat = lax.axis_index("seq"), lax.axis_index("mp")
        self.group, self.table, self.count = group, table, len(table)
        self.parts, self.out, self.small_out = parts, out, small_out
        self.low, self.high = place % 2, place // 2
        self.core = seat_of(mp=seat + 1 - 2 * (seat % 2))
        self.across = seat_of(mp=(seat + 2) % 4)
        self.beside = seat_of(seq=place + 1 - 2 * self.low)
        self.others = [
            seat_of(seq=((self.high + step) % group) * 2 + self.low) for step in range(1, group)
        ]
        (self.own_v, self.core_v, self.across_v, self.cross_v, self.first_v, self.give_v,
         self.half_v, self.keep_v, self.piece_v, self.slab_v, self.sum_v, self.done_v) = bufs
        (self.local_s, self.core_s, self.core_r, self.x_s, self.x_r, self.y_s, self.y_r,
         self.z_s, self.z_r, self.g_s, self.g_r, self.f_s, self.f_r, self.f_l) = sems
        self.half = parts.shape[-1] // 2
        self.stages = (
            self.step_zero, self.step_core, self.step_x, self.step_y, self.step_z, self.step_gather,
            self.step_end,
        )
        self.order, self.done, self.ready, self.free = [], {}, {}, {}
        self.clock, self.made = 0.0, 0

    def remote(self, source, target, send, recv, device):
        return pltpu.make_async_remote_copy(
            src_ref=source, dst_ref=target, send_sem=send, recv_sem=recv,
            device_id=device, device_id_type=MESH,
        )

    def size(self, c):
        return self.table[c][1]

    def chunk_rows(self, c):
        return pl.ds(*self.table[c])

    def used(self, c):
        return pl.ds(0, self.size(c))

    def piece(self, c, index):
        rows = self.size(c) // self.group
        return pl.ds(pl.multiple_of(index * rows, rows), rows)

    def local_copy(self, c):
        return pltpu.make_async_copy(
            self.parts.at[pl.ds(0, 2), self.chunk_rows(c)], self.own_v.at[c % 2, :, self.used(c)],
            self.local_s.at[c % 2]
        )

    def core_copy(self, c):
        return self.remote(
            self.parts.at[pl.ds(2, 2), self.chunk_rows(c)], self.core_v.at[c % CORE_RING, :, self.used(c)],
            self.core_s.at[c], self.core_r.at[c], self.core,
        )

    def x_copy(self, c):
        return self.remote(
            self.across_v.at[c % SENT_RING, self.used(c)], self.cross_v.at[c % LAND_RING, self.used(c)],
            self.x_s.at[c], self.x_r.at[c], self.across,
        )

    def y_copy(self, c):
        return self.remote(
            self.give_v.at[c % SENT_RING, self.used(c)], self.half_v.at[c % LAND_RING, self.used(c)],
            self.y_s.at[c], self.y_r.at[c], self.beside,
        )

    def z_copy(self, c, step):
        to = (self.high + step) % self.group
        return self.remote(
            self.slab_v.at[c % SENT_RING, self.piece(c, to)],
            self.piece_v.at[c % LAND_RING, step - 1, pl.ds(0, self.size(c) // self.group)],
            self.z_s.at[c, step - 1], self.z_r.at[c, step - 1], self.others[step - 1],
        )

    def own_rows(self, c):
        return self.piece(c, self.high)

    def g_copy(self, c, step):
        mine = self.done_v.at[c % DONE_RING, self.own_rows(c)]
        return self.remote(
            mine, mine, self.g_s.at[c, step - 1], self.g_r.at[c, step - 1], self.others[step - 1]
        )

    def target(self, c):
        lanes = pl.ds(pl.multiple_of(self.low * self.half, 128), self.half)
        start, rows = self.table[c]
        if start >= LAYERS * LAYER_ROWS:
            return self.small_out.at[pl.ds(0, rows), lanes]
        turned = (start + (LAYERS - 1) * LAYER_ROWS) % (LAYERS * LAYER_ROWS)
        return self.out.at[pl.ds(turned, rows), lanes]

    def f_copy(self, c):
        return self.remote(
            self.done_v.at[c % DONE_RING, self.used(c)], self.target(c), self.f_s.at[c], self.f_r.at[c], self.beside
        )

    def f_own(self, c):
        return pltpu.make_async_copy(
            self.done_v.at[c % DONE_RING, self.used(c)], self.target(c), self.f_l.at[c]
        )

    def step_zero(self, c):
        self.local_copy(c).start()
        self.core_copy(c).start()

    def step_core(self, c):
        self.local_copy(c).wait()
        self.core_copy(c).wait()
        used = self.used(c)
        own, came = self.own_v.at[c % 2], self.core_v.at[c % CORE_RING]
        self.first_v[c % SENT_RING, used, :] = own[0, used, :].astype(F32) + came[0, used, :].astype(F32)
        self.across_v[c % SENT_RING, used, :] = (
            own[1, used, :].astype(F32) + came[1, used, :].astype(F32)
        ).astype(BF16)
        self.x_copy(c).start()

    def step_x(self, c):
        self.x_copy(c).wait()
        used = self.used(c)
        total = self.first_v[c % SENT_RING, used, :] + self.cross_v[c % LAND_RING, used, :].astype(F32)
        left, right = total[:, : self.half], total[:, self.half :]
        self.keep_v[c % SENT_RING, used, :] = jnp.where(self.low == 0, left, right)
        self.give_v[c % SENT_RING, used, :] = jnp.where(self.low == 0, right, left).astype(BF16)
        self.y_copy(c).start()

    def step_y(self, c):
        self.y_copy(c).wait()
        used = self.used(c)
        total = self.keep_v[c % SENT_RING, used, :] + self.half_v[c % LAND_RING, used, :].astype(F32)
        self.sum_v[c % SENT_RING, used, :] = total
        self.slab_v[c % SENT_RING, used, :] = total.astype(BF16)
        for step in range(1, self.group):
            self.z_copy(c, step).start()

    def step_z(self, c):
        total = self.sum_v[c % SENT_RING, self.own_rows(c), :]
        for step in range(1, self.group):
            self.z_copy(c, step).wait()
            total = total + self.piece_v[c % LAND_RING, step - 1, : self.size(c) // self.group, :].astype(F32)
        self.done_v[c % DONE_RING, self.own_rows(c), :] = total.astype(BF16)
        for step in range(1, self.group):
            self.g_copy(c, step).start()

    def step_gather(self, c):
        for step in range(1, self.group):
            self.g_copy(c, step).wait()
        self.f_copy(c).start()
        self.f_own(c).start()

    def step_end(self, c):
        self.f_own(c).wait()
        self.f_copy(c).wait()

    def passed(self, k, c, sent_after, pairs):
        for send, receive in pairs:
            for other in range(self.count):
                at = self.done.get((other, send))
                if at is not None and at > sent_after and (other, receive) in self.done:
                    return True
        return False

    def may(self, c, k):
        done = self.done
        if k and (c, k - 1) not in done:
            return False
        if c and (c - 1, k) not in done:
            return False
        kept = {0: (2, 1), 1: (SENT_RING, 2), 2: (SENT_RING, 3), 3: (SENT_RING, 4), 4: (DONE_RING, 6)}
        if k in kept:
            ring, use = kept[k]
            if c >= ring and (c - ring, use) not in done:
                return False
        landing = {
            0: (CORE_RING, 1, ((0, 1),)),
            1: (LAND_RING, 2, ((1, 2),)),
            2: (LAND_RING, 3, ((2, 3), (5, 6))),
            3: (LAND_RING, 4, ((3, 4), (4, 5))),
            4: (DONE_RING, 6, ((3, 4), (4, 5))),
        }
        if k in landing:
            ring, use, pairs = landing[k]
            if c >= ring:
                read = done.get((c - ring, use))
                if read is None or not self.passed(k, c, read, pairs):
                    return False
        return k > 0 or c < self.made

    def issue(self, c, k):
        self.stages[k](c)
        self.done[c, k] = len(self.done)
        part = self.size(c) / CHUNK
        self.clock = max(self.clock, self.ready.get((c, k), 0.0)) + 0.15 + 0.2 * part
        if k < 6:
            link, rate = LINKS[k]
            begin = max(self.clock, self.free.get(link, 0.0))
            self.free[link] = begin + rate * part
            self.ready[c, k + 1] = self.free[link] + LATENCY

    def waiting(self):
        for c in range(self.count):
            for k in range(7):
                if (c, k) not in self.done:
                    if self.may(c, k):
                        yield self.ready.get((c, k), 0.0), -k, c
                    break

    def tick(self, spent, made=0):
        self.clock += PACE * spent
        self.made = max(self.made, made)
        while True:
            now = [op for op in self.waiting() if op[0] <= self.clock]
            now = [op for op in now if op[1] or self.free.get("x", 0.0) < self.clock + AHEAD]
            if not now:
                return
            _, k, c = min(now)
            self.issue(c, -k)

    def drain(self):
        self.made = self.count
        while len(self.done) < 7 * self.count:
            ready, k, c = min((max(at, self.clock), k, c) for at, k, c in self.waiting())
            self.issue(c, -k)


def reducer_scratch(count, group, width):
    vmem, dma = pltpu.VMEM, pltpu.SemaphoreType.DMA
    half, piece, rows = width // 2, CHUNK // group, CHUNK
    bufs = [
        vmem((2, 2, rows, width), BF16),
        vmem((CORE_RING, 2, rows, width), BF16),
        vmem((SENT_RING, rows, width), BF16),
        vmem((LAND_RING, rows, width), BF16),
        vmem((SENT_RING, rows, width), F32),
        vmem((SENT_RING, rows, half), BF16),
        vmem((LAND_RING, rows, half), BF16),
        vmem((SENT_RING, rows, half), F32),
        vmem((LAND_RING, group - 1, piece, half), BF16),
        vmem((SENT_RING, rows, half), BF16),
        vmem((SENT_RING, rows, half), F32),
        vmem((DONE_RING, rows, half), BF16),
    ]
    sems = [dma((2,))] + [dma((count,))] * 6 + [dma((count, group - 1))] * 4 + [dma((count,))] * 3
    return bufs, sems


LAYER_NAMES = (
    "act", "slope", "normed", "unit_one", "unit_two", "mixed", "q", "k", "v", "pooled_k",
    "pooled_v", "entry", "down", "up", "out", "qkv",
)
LOCAL_NAMES = ("inverse_one", "inverse_two", "lse")


def backward_kernel(group, table, *refs):
    count = len(table)
    refs = list(refs)
    take = lambda n: [refs.pop(0) for _ in range(n)]
    cot_ref, gains_ref, conv_ref, bounds_ref, keep_ref = take(5)
    layers = []
    for _ in range(LAYERS):
        names = LAYER_NAMES + LOCAL_NAMES
        layers.append(dict(zip(names, take(len(names)))))
    sums_ref, small_out_ref, grad_in_ref, parts_ref = take(4)
    bufs, sems = take(12), take(14)
    (g_ref, gm_ref, gr_low, gmix_ref, send_left, send_right, from_right, from_left,
     split_ref, up_ref, whole_ref, load_s, halo_s, store_s, out_s) = take(15)
    total, width = g_ref.shape
    read = bounds_reader(bounds_ref, total)
    place, seat = lax.axis_index("seq"), lax.axis_index("mp")
    seqs = lax.axis_size("seq")
    red = Reducer(group, table, parts_ref, sums_ref, small_out_ref, bufs, sems)
    ahead = seat_of(seq=(place + (seat + 1) // 4) % seqs, mp=(seat + 1) % 4)
    behind = seat_of(seq=(place + seqs - (3 - seat + 1) // 4) % seqs, mp=(seat + 3) % 4)
    barrier = pltpu.get_barrier_semaphore()
    devices = [red.core, red.across, red.beside, ahead, behind] + red.others
    for device in devices:
        pl.semaphore_signal(barrier, inc=1, device_id=device, device_id_type=MESH)
    pl.semaphore_wait(barrier, len(devices))

    split_ref[...] = jnp.zeros_like(split_ref)
    up_ref[...] = jnp.zeros_like(up_ref)
    whole_ref[...] = jnp.zeros_like(whole_ref)
    quarter = width // 4
    feed = 4 * width

    def load(source, target, index):
        copy = pltpu.make_async_copy(source, target, load_s.at[index])
        copy.start()
        return copy

    def place_of(part):
        return (part % 2) * 2 + part // 2

    def norm_back(layer, grad, unit, inverse, gain, result, low_ref, rows_at):
        gain_row, shift_row, bias_row = rows_at

        @pl.loop(0, total // NORM_ROWS)
        def _(block):
            rows = pl.ds(pl.multiple_of(block * NORM_ROWS, NORM_ROWS), NORM_ROWS)
            g, n = grad[rows, :], unit[rows, :]
            a = g * gain
            mean = jnp.sum(a, axis=1, keepdims=True) * (1.0 / width)
            tilt = jnp.sum(a * n, axis=1, keepdims=True) * (1.0 / width)
            back = (a - mean - n * tilt) * inverse[rows, :]
            result[rows, :] = back
            low_ref[rows, :] = back.astype(BF16)
            for at, value in ((gain_row, g * n), (shift_row, g), (bias_row, back)):
                whole_ref[layer, at : at + 1, :] += jnp.sum(value, axis=0, keepdims=True)

    def feed_scope(layer, base, ready, down, up, act, slope, normed, unit_one, unit_two, out, mixed,
                   gm_low, gn_ref, ga_ref, gp_low, stage, normed_t):
        ref = layers[layer]
        pairs = ((ref["unit_two"], unit_two), (ref["act"], act), (ref["down"], down),
                 (ref["slope"], slope), (ref["normed"], normed), (ref["up"], up),
                 (ref["unit_one"], unit_one), (ref["out"], out), (ref["mixed"], mixed))
        copies = [load(a, b, i) for i, (a, b) in enumerate(pairs)]
        copies[0].wait()
        norm_back(layer, g_ref, unit_two, ref["inverse_two"], gains_ref[layer, 1:2, :], gm_ref,
                  gm_low, (1, 5, 4))
        red.tick(4.0)
        stores = []

        def store(part, at):
            copy = pltpu.make_async_copy(
                stage.at[part % 2], parts_ref.at[place_of(part), pl.ds(at, width)], store_s.at[part % 2]
            )
            copy.start()
            stores.append(copy)

        def settle(keep):
            while len(stores) > keep:
                stores.pop(0).wait()

        copies[1].wait()
        for j in range(3):
            for part in range(4):
                slot = (4 * j + part) % 6
                settle(5)
                at = part * width + j * CHUNK
                piece = stage.at[slot // 3, pl.ds(slot % 3 * CHUNK, CHUNK)]
                piece[...] = product_left_t(act[:, at : at + CHUNK], gm_low[...]).astype(BF16)
                copy = pltpu.make_async_copy(
                    piece, parts_ref.at[place_of(part), pl.ds(base + j * CHUNK, CHUNK)], store_s.at[slot]
                )
                copy.start()
                stores.append(copy)
            settle(0)
            red.tick(2.2, ready + j + 1)
        for copy in copies[2:6]:
            copy.wait()
        normed_t[...] = normed[...].T
        for part in range(4):
            cols = slice(part * width, (part + 1) * width)
            ga_ref[...] = product_right_t(gm_low[...], down[cols, :])
            up_ref[layer, part : part + 1, :] = jnp.zeros((1, width), F32)

            @pl.loop(0, total // NORM_ROWS)
            def _(block):
                rows = pl.ds(pl.multiple_of(block * NORM_ROWS, NORM_ROWS), NORM_ROWS)
                gp = ga_ref[rows, :] * slope[rows, cols].astype(F32)
                gp_low[rows, :] = gp.astype(BF16)
                up_ref[layer, part : part + 1, :] += jnp.sum(gp, axis=0, keepdims=True)

            made = product_right_t(gp_low[...], up[:, cols])
            if part == 0:
                gn_ref[...] = gm_ref[...] + made
            else:
                gn_ref[...] += made
            red.tick(3.0)
            settle(1)
            stage[part % 2] = product(normed_t[...], gp_low[...]).astype(BF16)
            store(part, base + width)
            red.tick(1.5)
        for copy in copies[6:]:
            copy.wait()
        norm_back(layer, gn_ref, unit_one, ref["inverse_one"], gains_ref[layer, 0:1, :], gm_ref,
                  gr_low, (0, 3, 2))
        settle(0)
        red.tick(3.0, ready + 6)
        gmix_ref[...] = product_right_t(gr_low[...], out[...]).astype(BF16)
        stage[0] = product_left_t(mixed[...], gr_low[...]).astype(BF16)
        store_parts(stage.at[0], base + 2 * width, 0)
        red.tick(3.0)

    def part_copies(source, at, bank):
        return [
            pltpu.make_async_copy(
                source.at[pl.ds(part * quarter, quarter)],
                parts_ref.at[place_of(part), pl.ds(at, quarter)],
                out_s.at[bank, part],
            )
            for part in range(4)
        ]

    def store_parts(source, at, bank):
        copies = part_copies(source, at, bank)
        for copy in copies:
            copy.start()
        for copy in copies:
            copy.wait()

    def attend_scope(layer, grad_q, grad_k, grad_v, q, k, v, pooled_k, pooled_v,
                     wide_k, wide_v, far_k, far_v, wide_f32):
        ref = layers[layer]
        names = ("q", "k", "v", "pooled_k", "pooled_v")
        copies = [load(ref[n], b, i) for i, (n, b) in enumerate(zip(names, (q, k, v, pooled_k, pooled_v)))]
        for copy in copies:
            copy.wait()
        attend_backward_body(
            q, k, v, pooled_k, pooled_v, gmix_ref, ref["lse"],
            lambda tile: read(tile * TILE, TILE), keep_ref,
            conv_ref.at[layer], grad_q, grad_k, grad_v, split_ref.at[layer],
            wide_k, wide_v, far_k, far_v, wide_f32, red.tick,
        )

    def project_scope(layer, base, ready, grad_q, grad_k, grad_v, qkv, entry, wide, full):
        ref = layers[layer]
        copies = [load(ref["qkv"], qkv, 0), load(ref["entry"], entry, 1)]
        red.tick(3.0)
        for copy in copies:
            copy.wait()
        wide[...] = product(grad_k[...], qkv[1])
        wide[...] += product(grad_v[...], qkv[2])
        send_left[...] = wide[LEFT - LEFT_SENT : LEFT, :].astype(BF16)
        send_right[...] = wide[LEFT + total :, :].astype(BF16)
        for copy in halo(layer):
            copy.start()
        red.tick(4.0)
        own = slice(LEFT, LEFT + total)
        gm_ref[...] += wide[own, :]
        gm_ref[...] += product(grad_q[...], qkv[0])
        banks = []
        for which, (grad, rows) in enumerate(((grad_q, own), (grad_k, slice(None)), (grad_v, slice(None)))):
            bank = which % 2
            if which >= 2:
                for copy in banks[which - 2]:
                    copy.wait()
            full[bank] = product_left_t(grad[...], entry[rows, :]).astype(BF16)
            copies = part_copies(full.at[bank], base + 2 * width + (which + 1) * quarter, bank)
            for copy in copies:
                copy.start()
            banks.append(copies)
            red.tick(2.5)
        for copies in banks[1:]:
            for copy in copies:
                copy.wait()
        red.tick(0.5, ready + 9 if layer else count - 1)

    def halo(layer):
        return [
            red.remote(send_left, from_right, halo_s.at[layer, 0], halo_s.at[layer, 1], behind),
            red.remote(send_right, from_left, halo_s.at[layer, 2], halo_s.at[layer, 3], ahead),
        ]

    def add_halo(layer):
        for copy in halo(layer):
            copy.wait()
        index = place * 4 + seat
        right = jnp.where(index == 4 * seqs - 1, 0.0, 1.0)
        left = jnp.where(index == 0, 0.0, 1.0)
        gm_ref[total - LEFT_SENT :, :] += from_right[...].astype(F32) * right
        gm_ref[:RIGHT, :] += from_left[...].astype(F32) * left

    start = load(cot_ref, gr_low, 0)
    start.wait()
    g_ref[...] = gr_low[...].astype(F32)
    vmem = pltpu.VMEM
    block = (total, width)
    wide_rows = total + LEFT + RIGHT
    far_rows = total // 4 + 2 * POOL_REACH
    pairs = width // PAIR
    for turn, layer in enumerate(reversed(range(LAYERS))):
        base = turn * LAYER_ROWS
        ready = turn * (LAYER_ROWS // CHUNK)

        pl.run_scoped(
            functools.partial(feed_scope, layer, base, ready),
            vmem((feed, width), BF16), vmem((width, feed), BF16), vmem((total, feed), BF16),
            vmem((total, feed), BF16), vmem(block, BF16), vmem(block, F32), vmem(block, F32),
            vmem((width, width), BF16), vmem(block, BF16), vmem(block, BF16), vmem(block, F32),
            vmem(block, F32), vmem(block, BF16), vmem((2, width, width), BF16), vmem((width, total), BF16),
        )

        def attention(grad_q, grad_k, grad_v):
            pl.run_scoped(
                functools.partial(attend_scope, layer, grad_q, grad_k, grad_v),
                vmem(block, BF16), vmem((wide_rows, width), BF16), vmem((wide_rows, width), BF16),
                vmem((far_rows, width), BF16), vmem((far_rows, width), BF16),
                vmem((pairs, wide_rows, PAIR), F32), vmem((pairs, wide_rows, PAIR), F32),
                vmem((far_rows, width), F32), vmem((far_rows, width), F32),
                vmem((wide_rows, PAIR), F32),
            )
            pl.run_scoped(
                functools.partial(project_scope, layer, base, ready, grad_q, grad_k, grad_v),
                vmem((3, width, width), BF16), vmem((wide_rows, width), BF16),
                vmem((wide_rows, width), F32), vmem((2, width, width), BF16),
            )

        pl.run_scoped(
            attention, vmem(block, BF16), vmem((wide_rows, width), BF16), vmem((wide_rows, width), BF16)
        )
        if turn < LAYERS - 1:
            add_halo(layer)
            red.tick(3.0)
            g_ref[...] = gm_ref[...]

    def small_scope(stage):
        stage[...] = jnp.zeros_like(stage)
        for layer in range(LAYERS):
            at = 32 * layer
            for part in range(4):
                pos = place_of(part)
                rolled = split_ref[layer]
                if part:
                    rolled = pltpu.roll(rolled, width - part * quarter, 1)
                stage[pos, at : at + 16, :] = rolled.astype(BF16)
                rest = jnp.concatenate([whole_ref[layer], up_ref[layer, part : part + 1, :]] + [jnp.zeros((7, width), F32)], axis=0)
                stage[pos, at + 16 : at + 32, :] = rest.astype(BF16)
        copy = pltpu.make_async_copy(
            stage, parts_ref.at[:, pl.ds(LAYERS * LAYER_ROWS, table[-1][1])], store_s.at[0]
        )
        copy.start()
        copy.wait()

    pl.run_scoped(small_scope, vmem((4, table[-1][1], width), BF16))

    red.tick(1.0, count)
    add_halo(0)
    final = pltpu.make_async_copy(gm_ref, grad_in_ref, load_s.at[0])
    final.start()
    red.drain()
    final.wait()


def backward(cot, gains, conv, bounds, keep, saved):
    total, width = cot.shape
    group = lax.axis_size("seq") // 2
    last = max(CHUNK // 2, 16 * group)
    small_rows = max(64, 16 * group)
    rows = LAYERS * LAYER_ROWS
    cut = rows - width
    table = [(at, CHUNK) for at in range(0, cut, CHUNK)]
    table += [(at, last) for at in range(cut, rows, last)]
    table.append((rows, small_rows))
    rows += small_rows
    count = len(table)
    vmem, dma = pltpu.VMEM, pltpu.SemaphoreType.DMA
    anywhere = pl.BlockSpec(memory_space=pl.ANY)
    local = pl.BlockSpec(memory_space=pltpu.VMEM)
    args = [cot, gains, conv, bounds, keep]
    specs = [anywhere] + [local] * 4
    for layer in saved:
        args += [layer[name] for name in LAYER_NAMES + LOCAL_NAMES]
        specs += [anywhere] * len(LAYER_NAMES) + [local] * len(LOCAL_NAMES)
    bufs, sems = reducer_scratch(count, group, width)
    shape = jax.ShapeDtypeStruct
    return pl.pallas_call(
        functools.partial(backward_kernel, group, tuple(table)),
        out_shape=(
            shape((LAYERS * LAYER_ROWS, width), BF16),
            shape((small_rows, width), BF16),
            shape((total, width), F32),
            shape((4, rows, width), BF16),
        ),
        in_specs=specs,
        out_specs=(anywhere,) * 4,
        scratch_shapes=bufs + sems + [
            vmem((total, width), F32),
            vmem((total, width), F32),
            vmem((total, width), BF16),
            vmem((total, width), BF16),
            vmem((LEFT_SENT, width), BF16),
            vmem((RIGHT, width), BF16),
            vmem((LEFT_SENT, width), BF16),
            vmem((RIGHT, width), BF16),
            vmem((LAYERS, 16, width), F32),
            vmem((LAYERS, 8, width), F32),
            vmem((LAYERS, 8, width), F32),
            dma((9,)),
            dma((LAYERS, 4)),
            dma((6,)),
            dma((2, 4)),
        ],
        compiler_params=pltpu.CompilerParams(
            collective_id=0, has_side_effects=True, vmem_limit_bytes=60 * 1024 * 1024
        ),
        name="backward",
    )(*args)


def row_blocks(total, size, body):
    @pl.loop(0, total // size)
    def _(block):
        body(pl.ds(pl.multiple_of(block * size, size), size))


def attend_forward_body(
    q_ref, k_ref, v_ref, bounds_of, keep_ref, taps, shifts,
    mixed_ref, lse_ref, pooled_k_ref, pooled_v_ref, wide_f32, pairs,
):
    for which, (source, pooled) in enumerate(((k_ref, pooled_k_ref), (v_ref, pooled_v_ref))):
        pool_into(source, wide_f32, keep_ref, taps[which], shifts[which], pooled, pairs)

    @pl.loop(0, q_ref.shape[0] // TILE)
    def _(tile):
        rows = pl.ds(pl.multiple_of(tile * TILE, TILE), TILE)
        bias = tile_bias(tile, *bounds_of(tile))
        bias = jnp.concatenate([bias, bias], axis=1)
        for pair in pairs:
            lanes = slice(pair * PAIR, (pair + 1) * PAIR)
            query = stacked(q_ref[rows, lanes] * BF16(HEAD_DIM**-0.5))
            key = keys_of(k_ref, pooled_k_ref, tile, lanes)
            value = keys_of(v_ref, pooled_v_ref, tile, lanes)
            scores = product_right_t(key, query) + bias
            most = jnp.max(scores, axis=0, keepdims=True)
            weight = jnp.exp(scores - most)
            total = jnp.sum(weight, axis=0, keepdims=True)
            both = product_left_t(value, weight.astype(BF16)) * (1.0 / total)
            mixed_ref[rows, lanes] = unstack(both).T.astype(BF16)
            lse_ref[tile, pair : pair + 1, :] = most + jnp.log(total)


SAVED_NAMES = LAYER_NAMES
KINDS = 8
TENSORS = KINDS * LAYERS


def forward_kernel(*refs):
    refs = list(refs)
    take = lambda n: [refs.pop(0) for _ in range(n)]
    (x_ref, qkv_ref, out_ref, up_ref, down_ref, qv_ref, taps_ref, pool_ref, feed_ref, gains_ref,
     biases_ref, bounds_ref) = take(12)
    hidden_ref, conv_ref, keep_ref = take(3)
    results = [dict(zip(SAVED_NAMES + LOCAL_NAMES, take(len(SAVED_NAMES + LOCAL_NAMES)))) for _ in range(LAYERS)]
    (qkv_v, out_v, up_v, down_v, entry_v, q_v, k_v, v_v, far_k, far_v, mixed_v, hidden_v, acc_v,
     unit_one, low_v, act_v, slope_v, pre_v, wide_f32, small_v, full_v,
     own_s, x_s, x_r, y_s, y_r, c_s, c_r, d_s, d_r, halo_s, save_s, load_s) = take(33)
    total, width = hidden_v.shape
    quarter, half = width // 4, width // 2
    place, seat, seqs = lax.axis_index("seq"), lax.axis_index("mp"), lax.axis_size("seq")
    low = place % 2
    core = seat_of(mp=seat + 1 - 2 * (seat % 2))
    across = seat_of(mp=(seat + 2) % 4)
    beside = seat_of(seq=place + 1 - 2 * low)
    ahead = seat_of(seq=(place + (seat + 1) // 4) % seqs, mp=(seat + 1) % 4)
    behind = seat_of(seq=(place + seqs - (4 - seat) // 4) % seqs, mp=(seat + 3) % 4)
    barrier = pltpu.get_barrier_semaphore()
    devices = [core, across, beside, ahead, behind]
    for device in devices:
        pl.semaphore_signal(barrier, inc=1, device_id=device, device_id_type=MESH)
    entry_own = pl.ds(LEFT, total)
    first_load = pltpu.make_async_copy(x_ref, entry_v.at[0, entry_own], load_s.at[0])
    first_load.start()
    small_v[0] = jnp.zeros(small_v.shape[1:], F32)
    for layer in range(LAYERS):
        for which in range(2):
            at = 2 * layer + which
            small_v[0, at : at + 1, :quarter] = qv_ref[layer, which : which + 1, :]
            small_v[0, 24 + at : 25 + at, :quarter] = pool_ref[layer, which : which + 1, :]
            at = 4 + 10 * layer + 5 * which
            small_v[0, at : at + 5, :quarter] = taps_ref[layer, which]
        small_v[0, 32 + layer : 33 + layer, :] = feed_ref[layer : layer + 1, :]
    read = bounds_reader(bounds_ref, total)
    far = 4 * POOL_REACH
    edges = []
    for one in read(0, total):
        wide_f32[:total, :] = jnp.broadcast_to(one.astype(F32), (PAIR, total)).T
        edges.append(jnp.concatenate(
            [
                jnp.broadcast_to(wide_f32[0:1, :], (POOL_REACH, PAIR)),
                wide_f32[pl.ds(0, total // 4, stride=4), :],
                jnp.broadcast_to(wide_f32[total - 1 : total, :], (POOL_REACH, PAIR)),
            ],
            axis=0,
        ))
    token = 4 * lax.broadcasted_iota(jnp.int32, edges[0].shape, 0) - far - 2
    for tap in range(5):
        at = (token + tap).astype(F32)
        keep_ref[tap] = jnp.where((at >= edges[0]) & (at < edges[1]), 1.0, 0.0)
    for layer in range(LAYERS):
        entry_v[layer, : LEFT - LEFT_SENT, :] = jnp.zeros((LEFT - LEFT_SENT, width), BF16)
    pl.semaphore_wait(barrier, len(devices))

    def remote(source, target, send, recv, device):
        return pltpu.make_async_remote_copy(
            src_ref=source, dst_ref=target, send_sem=send, recv_sem=recv,
            device_id=device, device_id_type=MESH,
        )

    def span(size, side):
        if side is None:
            return 0, size
        return pl.multiple_of(side * (size // 2), size // 2), size // 2

    def shard(tensor, side=None):
        layer, kind = tensor // KINDS, tensor % KINDS
        if kind < 3:
            return qkv_ref.at[layer, (1, 2, 0)[kind], pl.ds(*span(quarter, side))]
        if kind == 3:
            return out_ref.at[layer, pl.ds(*span(quarter, side))]
        piece = (kind - 4) // 2 * half
        at, count = span(half, side)
        if kind % 2 == 0:
            at, count = span(width, side)
            return up_ref.at[layer, pl.ds(at, count), pl.ds(piece, half)]
        return down_ref.at[layer, pl.ds(piece + at, count)]

    def landed(tensor, part, side=None):
        layer, kind = tensor // KINDS, tensor % KINDS
        if kind < 4:
            at, count = span(quarter, side)
            rows = pl.ds(part * quarter + at, count)
            if kind < 3:
                return qkv_v.at[layer, (1, 2, 0)[kind], rows]
            return out_v.at[layer, rows]
        piece = part * width + (kind - 4) // 2 * half
        if kind % 2 == 0:
            return up_v.at[layer, pl.ds(*span(width, side)), pl.ds(piece, half)]
        at, count = span(half, side)
        return down_v.at[layer, pl.ds(piece + at, count)]

    def own_copy(t):
        return pltpu.make_async_copy(shard(t), landed(t, 0), own_s.at[t])

    def x_copy(t):
        return remote(shard(t, low), landed(t, 2, low), x_s.at[t], x_r.at[t], across)

    def y_copy(t):
        return remote(landed(t, 2, low), landed(t, 2, low), y_s.at[t], y_r.at[t], beside)

    def c_copy(t):
        return remote(shard(t), landed(t, 1), c_s.at[t], c_r.at[t], core)

    def d_copy(t):
        return remote(landed(t, 2), landed(t, 3), d_s.at[t], d_r.at[t], core)

    model = {"clock": 0.0, "x": 5.0, "y": 5.0, "next": [0, 0, 0], "at": {}}

    def issue(k):
        t = model["next"][k]
        model["next"][k] += 1
        cost = 3.3 if t % KINDS < 4 else 6.6
        model["clock"] = max(model["clock"], model["at"].get((t, k), 0.0)) + 0.15
        if k == 0:
            own_copy(t).start()
            c_copy(t).start()
            x_copy(t).start()
        elif k == 1:
            x_copy(t).wait_recv()
            y_copy(t).start()
        else:
            y_copy(t).wait_recv()
            d_copy(t).start()
        if k < 2:
            link = "xy"[k]
            model[link] = max(model[link], model["clock"]) + cost
            model["at"][t, k + 1] = model[link] + LATENCY

    def tick(spent):
        model["clock"] += spent
        while True:
            clock = model["clock"]
            for k in (2, 1, 0):
                t = model["next"][k]
                if t >= TENSORS or (k and t >= model["next"][k - 1]):
                    continue
                if model["at"].get((t, k), 0.0) <= clock if k else model["x"] < clock + 2 * AHEAD:
                    issue(k)
                    break
            else:
                return

    arrived = set()

    def need(t, part):
        if (t, part) in arrived:
            return
        arrived.add((t, part))
        for k in range(1 if part < 2 else 3):
            while model["next"][k] <= t:
                issue(k)
        if part == 0:
            own_copy(t).wait()
        elif part == 1:
            c_copy(t).wait_recv()
        elif part == 3:
            d_copy(t).wait_recv()

    small_index = TENSORS
    small_x = remote(small_v.at[0], small_v.at[2], x_s.at[small_index], x_r.at[small_index], across)
    small_c = remote(small_v.at[0], small_v.at[1], c_s.at[small_index], c_r.at[small_index], core)
    small_d = remote(small_v.at[2], small_v.at[3], d_s.at[small_index], d_r.at[small_index], core)

    def halo(layer):
        entry = entry_v.at[layer]
        return (
            remote(
                entry.at[pl.ds(LEFT + total - LEFT_SENT, LEFT_SENT)],
                entry.at[pl.ds(LEFT - LEFT_SENT, LEFT_SENT)],
                halo_s.at[layer, 0], halo_s.at[layer, 1], ahead,
            ),
            remote(
                entry.at[pl.ds(LEFT, RIGHT)], entry.at[pl.ds(LEFT + total, RIGHT)],
                halo_s.at[layer, 2], halo_s.at[layer, 3], behind,
            ),
        )

    saves = {}

    def save(layer, name, source):
        index = SAVED_NAMES.index(name)
        copy = pltpu.make_async_copy(source, results[layer][name], save_s.at[layer, index])
        copy.start()
        saves[layer, name] = copy

    def settle(layer, *names):
        for name in names:
            if (layer, name) in saves:
                saves.pop((layer, name)).wait()

    def norm(layer, which, extra, result, low_ref, unit, inverse):
        gain = gains_ref[layer, which : which + 1, :]
        offset = biases_ref[layer, 2 * which + 1 : 2 * which + 2, :]
        shift_row = biases_ref[layer, 2 * which : 2 * which + 1, :]

        def body(rows):
            value = hidden_v[rows, :] + (extra[rows, :] + shift_row)
            average = jnp.sum(value, axis=1, keepdims=True) * (1.0 / width)
            centered = value - average
            spread = jnp.sum(centered * centered, axis=1, keepdims=True) * (1.0 / width)
            scale = lax.rsqrt(spread + NORM_EPSILON)
            one = centered * scale
            out = one * gain + offset
            unit[rows, :] = one
            inverse[rows, :] = scale
            result[rows, :] = out
            if low_ref is not None:
                low_ref[rows, :] = out.astype(BF16)

        row_blocks(total, NORM_ROWS, body)

    first_load.wait()
    for copy in halo(0):
        copy.start()
    small_x.start()
    small_c.start()
    tick(3.0)
    row_blocks(total, NORM_ROWS, lambda rows: hidden_v.__setitem__(
        (rows, slice(None)), entry_v[0, pl.ds(rows.start + LEFT, NORM_ROWS), :].astype(F32)))

    for layer in range(LAYERS):
        entry = entry_v.at[layer]
        tensor = KINDS * layer
        settle(layer - 1, "q", "k", "v", "pooled_k", "pooled_v", "mixed", "normed")

        def project(which, target, side, rows):
            lanes = slice(side * half, (side + 1) * half)
            kind = (2, 0, 1)[which]
            for part in (2 * side, 2 * side + 1):
                need(tensor + kind, part)
            into = rows if which else slice(0, total)
            made = product_right_t(entry[rows, :], qkv_v[layer, which, lanes, :])
            if which != 1:
                row = 2 * layer + which // 2
                made = made + full_v[row : row + 1, lanes]
            target[into, lanes] = made.astype(BF16)

        own = slice(LEFT, LEFT + total)
        outer = (slice(0, LEFT), slice(LEFT + total, LEFT + total + RIGHT))

        def project_own(side):
            project(1, k_v, side, own)
            if layer == 0 and side == 0:
                small_params()
            project(2, v_v, side, own)
            project(0, q_v, side, own)
            tick(3.0)

        def project_outer(side):
            for rows in outer:
                project(1, k_v, side, rows)
                project(2, v_v, side, rows)
            tick(2.0)

        def small_params():
            small_c.wait_recv()
            small_x.wait_recv()
            small_d.start()
            small_d.wait_recv()
            rows = [small_v[0, :32, :]] + [
                pltpu.roll(small_v[part, :32, :], part * quarter, 1) for part in range(1, 4)
            ]
            full_v[...] = rows[0] + rows[1] + rows[2] + rows[3]
            for one in range(LAYERS):
                for which in range(2):
                    at = 4 + 10 * one + 5 * which
                    conv_ref[one, which] = full_v[at : at + 5, :]

        def attend(pairs):
            taps = [
                lambda tap, at=4 + 10 * layer + 5 * which: full_v[at + tap : at + tap + 1, :]
                for which in range(2)
            ]
            shifts = [full_v[24 + 2 * layer + which : 25 + 2 * layer + which, :] for which in range(2)]
            attend_forward_body(
                q_v, k_v, v_v, lambda tile: read(tile * TILE, TILE), keep_ref, taps, shifts,
                mixed_v, results[layer]["lse"], far_k, far_v, wide_f32, pairs,
            )
            tick(2.6 * len(pairs))

        pairs = width // PAIR
        if layer == 0:
            project_own(0)
            for copy in halo(layer):
                copy.wait_recv()
            tick(4.0)
            project_outer(0)
            attend(range(pairs // 2))
            project_own(1)
            project_outer(1)
            attend(range(pairs // 2, pairs))
        else:
            project_own(0)
            project_own(1)
            for copy in halo(layer):
                copy.wait_recv()
            tick(4.0)
            project_outer(0)
            project_outer(1)
            attend(range(pairs))
        for name, source in (("entry", entry), ("q", q_v), ("k", k_v), ("v", v_v),
                             ("pooled_k", far_k), ("pooled_v", far_v), ("mixed", mixed_v)):
            save(layer, name, source)
        for part in range(4):
            need(tensor + 3, part)
        acc_v[...] = product(mixed_v[...], out_v[layer])
        settle(layer - 1, "unit_one", "unit_two", "act", "slope")
        norm(layer, 0, acc_v, hidden_v, low_v, unit_one, results[layer]["inverse_one"])
        save(layer, "unit_one", unit_one)
        save(layer, "normed", low_v)
        tick(4.0)
        begun = False
        for part, piece in ((0, 0), (0, 1), (1, 0), (1, 1), (2, 0), (3, 0), (2, 1), (3, 1)):
            need(tensor + 4 + 2 * piece, part)
            need(tensor + 5 + 2 * piece, part)
            at = part * width + piece * half
            cols = slice(at, at + half)
            pre_v[...] = product(low_v[...], up_v[layer, :, cols])
            up_row = small_v[part, 32 + layer : 33 + layer, piece * half : (piece + 1) * half]

            def body(rows, cols=cols, up_row=up_row):
                act, slope = gelu_parts(pre_v[rows, :] + up_row)
                act_v[rows, cols] = act.astype(BF16)
                slope_v[rows, cols] = slope.astype(BF16)

            row_blocks(total, NORM_ROWS, body)
            made = product(act_v[:, cols], down_v[layer, cols, :])
            if begun:
                acc_v[...] += made
            else:
                acc_v[...] = made
            begun = True
            tick(3.0)
        save(layer, "act", act_v)
        save(layer, "slope", slope_v)
        save(layer, "qkv", qkv_v.at[layer])
        save(layer, "out", out_v.at[layer])
        save(layer, "up", up_v.at[layer])
        save(layer, "down", down_v.at[layer])
        settle(layer, "unit_one")
        norm(layer, 1, acc_v, hidden_v, None, unit_one, results[layer]["inverse_two"])
        save(layer, "unit_two", unit_one)
        if layer + 1 < LAYERS:
            later = entry_v.at[layer + 1]
            row_blocks(total, NORM_ROWS, lambda rows: later.__setitem__(
                (pl.ds(rows.start + LEFT, NORM_ROWS), slice(None)), hidden_v[rows, :].astype(BF16)))
            for copy in halo(layer + 1):
                copy.start()
            tick(4.0)
    last = pltpu.make_async_copy(hidden_v, hidden_ref, load_s.at[0])
    last.start()
    for key in list(saves):
        settle(*key)
    small_x.wait_send()
    small_c.wait_send()
    small_d.wait_send()
    for t in range(TENSORS):
        for copy in (x_copy(t), y_copy(t), c_copy(t), d_copy(t)):
            copy.wait_send()
    for layer in range(LAYERS):
        for copy in halo(layer):
            copy.wait_send()
    last.wait()


def forward(x, qkv_t, out, up, down, *rest):
    total, width = x.shape
    vmem, dma, shape = pltpu.VMEM, pltpu.SemaphoreType.DMA, jax.ShapeDtypeStruct
    anywhere = pl.BlockSpec(memory_space=pl.ANY)
    local = pl.BlockSpec(memory_space=pltpu.VMEM)
    feed, wide_rows, far_rows = 4 * width, total + LEFT + RIGHT, total // 4 + 2 * POOL_REACH
    block, wide, far, square = (total, width), (wide_rows, width), (far_rows, width), (width, width)
    saved = dict(
        act=((total, feed), BF16), slope=((total, feed), BF16), normed=(block, BF16),
        unit_one=(block, F32), unit_two=(block, F32), mixed=(block, BF16), q=(block, BF16),
        k=(wide, BF16), v=(wide, BF16), pooled_k=(far, BF16), pooled_v=(far, BF16), entry=(wide, BF16),
        down=((feed, width), BF16), up=((width, feed), BF16), out=(square, BF16),
        qkv=((3, width, width), BF16), inverse_one=((total, 1), F32), inverse_two=((total, 1), F32),
        lse=((total // TILE, width // PAIR, 2 * TILE), F32),
    )
    names = SAVED_NAMES + LOCAL_NAMES
    shapes = [shape(block, F32), shape((LAYERS, 2, 5, width), F32), shape((5, far_rows, PAIR), F32)]
    specs = [anywhere, local, local]
    for _ in range(LAYERS):
        shapes += [shape(*saved[name]) for name in names]
        specs += [anywhere] * len(SAVED_NAMES) + [local] * len(LOCAL_NAMES)
    tensors = dma((TENSORS + 1,))
    outs = pl.pallas_call(
        forward_kernel,
        out_shape=tuple(shapes),
        in_specs=[anywhere] * 5 + [local] * len(rest),
        out_specs=tuple(specs),
        scratch_shapes=[
            vmem((LAYERS, 3, width, width), BF16), vmem((LAYERS, width, width), BF16),
            vmem((LAYERS, width, feed), BF16), vmem((LAYERS, feed, width), BF16),
            vmem((LAYERS, wide_rows, width), BF16),
            vmem(block, BF16), vmem(wide, BF16), vmem(wide, BF16), vmem(far, BF16), vmem(far, BF16),
            vmem(block, BF16), vmem(block, F32), vmem(block, F32), vmem(block, F32),
            vmem(block, BF16), vmem((total, feed), BF16), vmem((total, feed), BF16),
            vmem((total, width // 2), F32), vmem((wide_rows, PAIR), F32), vmem((4, 40, width), F32),
            vmem((32, width), F32),
            tensors, tensors, tensors, tensors, tensors, tensors, tensors, tensors, tensors,
            dma((LAYERS, 4)), dma((LAYERS, len(SAVED_NAMES))), dma((2,)),
        ],
        compiler_params=pltpu.CompilerParams(
            collective_id=1, has_side_effects=True, vmem_limit_bytes=60 * 1024 * 1024
        ),
        name="forward",
    )(x, qkv_t, out, up, down, *rest)
    size = len(names)
    stack = [dict(zip(names, outs[3 + size * one : 3 + size * (one + 1)])) for one in range(LAYERS)]
    return outs[0], outs[1], outs[2], stack


def unpack_kernel(
    down_in, up_in, out_in, qkv_in, small_in,
    down_ref, up_ref, out_ref, qkv_ref, qv_ref, taps_ref, pool_ref, feed_ref, gains_ref, biases_ref,
):
    down_ref[0] = down_in[0].astype(F32)
    up_ref[0] = up_in[0].astype(F32)
    out_ref[0] = out_in[0].astype(F32)
    qkv_ref[0, 0] = qkv_in[0].astype(F32)
    quarter = qv_ref.shape[-1]

    @pl.when((pl.program_id(0) == 0) & (pl.program_id(1) == 0))
    def _():
        for layer in range(LAYERS):
            rows = small_in[32 * layer : 32 * layer + 32, :].astype(F32)
            qv_ref[layer] = rows[0:2, :quarter]
            for which in range(2):
                at = 2 + 5 * which
                taps_ref[layer, which] = rows[at : at + 5, :quarter]
            pool_ref[layer] = rows[12:14, :quarter]
            gains_ref[layer] = rows[16:18]
            biases_ref[layer] = rows[18:22]
            feed_ref[layer : layer + 1, :] = rows[24:25]


def unpack(sums, small):
    width = sums.shape[1]
    quarter = width // 4
    shape = jax.ShapeDtypeStruct
    by_layer = sums.reshape(LAYERS, LAYER_ROWS, width)
    third = width // 3

    def view(rows, first):
        return pl.BlockSpec((1, rows, width), lambda layer, j: (layer, first // rows + j, 0))

    def whole(*dims):
        return pl.BlockSpec(dims, lambda layer, j: (0,) * len(dims))

    rest = ((LAYERS, 2, quarter), (LAYERS, 2, 5, quarter), (LAYERS, 2, quarter), (LAYERS, width),
            (LAYERS, 2, width), (LAYERS, 4, width))
    return pl.pallas_call(
        unpack_kernel,
        grid=(LAYERS, 3),
        out_shape=(
            shape((LAYERS, width, width), F32), shape((LAYERS, width, width), F32),
            shape((LAYERS, quarter, width), F32), shape((LAYERS, 3, quarter, width), F32),
        ) + tuple(shape(dims, F32) for dims in rest),
        in_specs=[
            view(third, 0), view(third, width), view(quarter // 3, 2 * width),
            view(quarter, 2 * width + quarter), whole(*small.shape),
        ],
        out_specs=[
            view(third, 0), view(third, 0), view(quarter // 3, 0),
            pl.BlockSpec((1, 1, quarter, width), lambda layer, j: (layer, j, 0, 0)),
        ] + [whole(*dims) for dims in rest],
        compiler_params=pltpu.CompilerParams(vmem_limit_bytes=32 * 1024 * 1024),
        name="unpack",
    )(by_layer, by_layer, by_layer, by_layer, small)


def shards(
    inputs,
    doc_bounds,
    qkv_weight,
    qv_bias,
    conv_weight,
    conv_bias,
    out_weight,
    up_weight,
    up_bias,
    down_weight,
    norm_gains,
    shared_biases,
    cotangent,
):
    hidden, conv_all, keep, stack = forward(
        inputs, qkv_weight.transpose(0, 1, 3, 2), out_weight, up_weight, down_weight, qv_bias, conv_weight,
        conv_bias, up_bias, norm_gains, shared_biases, doc_bounds,
    )
    sums, small, gradient, _ = backward(cotangent, norm_gains, conv_all, doc_bounds, keep, stack)
    down, up, out, qkv, qv, taps, pool, feed, gains, biases = unpack(sums, small)
    return (hidden, gradient, qkv.transpose(0, 1, 3, 2), qv, taps, pool, out, up, feed, down, gains, biases)


def solution(mesh):
    return jax.shard_map(
        shards,
        mesh=mesh,
        in_specs=(
            P(BOTH, None),
            P(None, "seq"),
            P(None, None, None, "mp"),
            P(None, None, "mp"),
            P(None, None, None, "mp"),
            P(None, None, "mp"),
            P(None, "mp", None),
            P(None, None, "mp"),
            P(None, "mp"),
            P(None, "mp", None),
            P(),
            P(),
            P(BOTH, None),
        ),
        out_specs=(
            P(BOTH, None),
            P(BOTH, None),
            P(None, None, None, "mp"),
            P(None, None, "mp"),
            P(None, None, None, "mp"),
            P(None, None, "mp"),
            P(None, "mp", None),
            P(None, None, "mp"),
            P(None, "mp"),
            P(None, "mp", None),
            P(),
            P(),
        ),
        check_vma=False,
    )
```

```python
import functools

import jax
import jax.numpy as jnp
from jax import lax
from jax.experimental import pallas as pl
from jax.experimental.pallas import tpu as pltpu
from jax.sharding import PartitionSpec as P

HEAD_DIM = 64
LAYERS = 2
WINDOW = 64
POOL_REACH = 64
NORM_EPSILON = 1e-05
LEFT = 320
LEFT_SENT = 272
RIGHT = 256
BOTH = ("seq", "mp")
BF16 = jnp.bfloat16
F32 = jnp.float32


def product(left, right):
    return jnp.dot(left, right, preferred_element_type=F32)


def product_left_t(left, right):
    return lax.dot_general(left, right, (((0,), (0,)), ((), ())), preferred_element_type=F32)


def product_right_t(left, right):
    return lax.dot_general(left, right, (((1,), (1,)), ((), ())), preferred_element_type=F32)


PAIR = 128
TILE = 128
SPAN = TILE + 2 * WINDOW
POOL_SPAN = TILE // 4 + 2 * POOL_REACH
FAR = -1e30


def tile_bias(tile, first, past):
    lane = lax.broadcasted_iota(jnp.int32, (1, TILE), 1) + tile * TILE
    near = lax.broadcasted_iota(jnp.int32, (SPAN, 1), 0) + (tile * TILE - WINDOW)
    far = 4 * (lax.broadcasted_iota(jnp.int32, (POOL_SPAN, 1), 0) + (tile * (TILE // 4) - POOL_REACH))

    def one(keys, reach):
        low = jnp.maximum(lane - reach, first)
        high = jnp.minimum(lane + reach + 1, past)
        return jnp.where((keys >= low) & (keys < high), 0.0, FAR)

    return jnp.concatenate([one(near, WINDOW), one(far, 4 * POOL_REACH)], axis=0)


def pair_mask():
    return lax.broadcasted_iota(jnp.int32, (1, PAIR), 1) < HEAD_DIM


def stacked(rows):
    left = pair_mask()
    zero = jnp.zeros_like(rows)
    return jnp.concatenate([jnp.where(left, rows, zero), jnp.where(left, zero, rows)], axis=0)


def rows_from(at, unit, size):
    return pl.ds(at if isinstance(at, int) else pl.multiple_of(at, unit), size)


def keys_of(wide_ref, pooled_ref, tile, lanes):
    near = wide_ref[rows_from(LEFT - WINDOW + tile * TILE, TILE, SPAN), lanes]
    far = pooled_ref[rows_from(tile * (TILE // 4), TILE // 4, POOL_SPAN), lanes]
    return jnp.concatenate([near, far], axis=0)


def unstack(both):
    return jnp.concatenate([both[:HEAD_DIM, :TILE], both[HEAD_DIM:, TILE:]], axis=0)


def pool_into(wide_ref, wide_f32, keep_ref, taps, shift_row, pooled_ref, pairs):
    count = pooled_ref.shape[0]
    begin = LEFT - 4 * POOL_REACH - 2
    for pair in pairs:
        lanes = slice(pair * PAIR, (pair + 1) * PAIR)
        wide_f32[...] = wide_ref[:, lanes].astype(F32)
        total = jnp.broadcast_to(shift_row[:, lanes], (count, PAIR))
        for tap in range(5):
            rows = wide_f32[pl.ds(begin + tap, count, stride=4), :]
            kept = rows * keep_ref[tap]
            total = total + kept * taps(tap)[:, lanes]
        pooled_ref[:, lanes] = total.astype(BF16)


def attend_backward_body(
    q_ref, k_ref, v_ref, pooled_k_ref, pooled_v_ref, grad_ref, lse_ref,
    bounds_of, keep_ref, conv_ref,
    grad_q_ref, grad_k_ref, grad_v_ref, small_ref,
    wide_k, wide_v, far_k, far_v, wide_f32, tick,
):
    pairs = q_ref.shape[1] // PAIR
    wide_k[...] = jnp.zeros_like(wide_k)
    wide_v[...] = jnp.zeros_like(wide_v)
    far_k[...] = jnp.zeros_like(far_k)
    far_v[...] = jnp.zeros_like(far_v)
    small_ref[...] = jnp.zeros_like(small_ref)

    for tile in range(q_ref.shape[0] // TILE):
        rows = rows_from(tile * TILE, TILE, TILE)
        near = rows_from(LEFT - WINDOW + tile * TILE, TILE, SPAN)
        far = rows_from(tile * (TILE // 4), TILE // 4, POOL_SPAN)
        bias = tile_bias(tile, *bounds_of(tile))
        bias = jnp.concatenate([bias, bias], axis=1)
        for pair in range(pairs):
            lanes = slice(pair * PAIR, (pair + 1) * PAIR)
            query = stacked(q_ref[rows, lanes] * BF16(HEAD_DIM**-0.5))
            grad = stacked(grad_ref[rows, lanes])
            key = keys_of(k_ref, pooled_k_ref, tile, lanes)
            value = keys_of(v_ref, pooled_v_ref, tile, lanes)
            scores = product_right_t(key, query) + bias
            probs = jnp.exp(scores - lse_ref[tile, pair : pair + 1, :])
            grad_probs = product_right_t(value, grad)
            delta = jnp.sum(probs * grad_probs, axis=0, keepdims=True)
            grad_scores = (probs * (grad_probs - delta)).astype(BF16)
            grad_value = product(probs.astype(BF16), grad)
            grad_key = product(grad_scores, query)
            wide_v[pair, near, :] += grad_value[:SPAN]
            far_v[far, lanes] += grad_value[SPAN:]
            wide_k[pair, near, :] += grad_key[:SPAN]
            far_k[far, lanes] += grad_key[SPAN:]
            grad_query = unstack(product_left_t(key, grad_scores)).T * (HEAD_DIM**-0.5)
            grad_q_ref[rows, lanes] = grad_query.astype(BF16)
            small_ref[0:1, lanes] += jnp.sum(grad_query, axis=0, keepdims=True)
        tick(4.0)

    count = far_k.shape[0]
    begin = LEFT - 4 * POOL_REACH - 2
    for which, (source, wide, pooled, result) in enumerate(
        ((k_ref, wide_k, far_k, grad_k_ref), (v_ref, wide_v, far_v, grad_v_ref))
    ):
        for pair in range(pairs):
            lanes = slice(pair * PAIR, (pair + 1) * PAIR)
            wide_f32[...] = source[:, lanes].astype(F32)
            grad = pooled[:, lanes]
            at = 12 + which
            small_ref[at : at + 1, lanes] = jnp.sum(grad, axis=0, keepdims=True)
            for tap in range(5):
                places = pl.ds(begin + tap, count, stride=4)
                kept = grad * keep_ref[tap]
                at = 2 + 5 * which + tap
                small_ref[at : at + 1, lanes] = jnp.sum(
                    kept * wide_f32[places, :], axis=0, keepdims=True
                )
                wide[pair, places, :] += kept * conv_ref[which, tap : tap + 1, lanes]
            if which == 1:
                small_ref[1:2, lanes] = jnp.sum(wide[pair], axis=0, keepdims=True)
            result[:, lanes] = wide[pair].astype(BF16)


def gelu_parts(pre):
    size = jnp.abs(pre) * (0.5**0.5)
    t = 1.0 / (1.0 + 0.5 * size)
    series = 0.17087277
    for term in (-0.82215223, 1.48851587, -1.13520398, 0.27886807, -0.18628806, 0.09678418,
                 0.37409196, 1.00002368, -1.26551223):
        series = series * t + term
    tail = 0.5 * t * jnp.exp(series - size * size)
    cdf = jnp.where(pre < 0.0, tail, 1.0 - tail)
    density = jnp.exp(-0.5 * pre * pre) * (0.5 / jnp.pi) ** 0.5
    return pre * cdf, cdf + pre * density


CHUNK = 256
SENT_RING, LAND_RING, CORE_RING, DONE_RING = 3, 6, 4, 8
LINKS = (("core", 2.2), ("x", 8.9), ("y", 4.45), ("z", 4.45), ("z", 4.45), ("y", 4.45))
LATENCY, AHEAD, PACE = 3.0, 12.0, 1.0
MESH = pl.DeviceIdType.MESH
LAYER_ROWS = 2304
NORM_ROWS = 64


def bounds_reader(bounds_ref, total):
    base = lax.axis_index("seq") * bounds_ref.shape[1] + lax.axis_index("mp") * total

    def read(at, count):
        start = lax.axis_index("mp") * total + at
        lanes = pl.ds(start if isinstance(start, int) else pl.multiple_of(start, TILE), count)
        return bounds_ref[0:1, lanes] - base, bounds_ref[1:2, lanes] - base

    return read


def seat_of(seq=None, mp=None):
    return {
        "seq": lax.axis_index("seq") if seq is None else seq,
        "mp": lax.axis_index("mp") if mp is None else mp,
    }


class Reducer:
    def __init__(self, group, table, parts, out, small_out, bufs, sems):
        place, seat = lax.axis_index("seq"), lax.axis_index("mp")
        self.group, self.table, self.count = group, table, len(table)
        self.parts, self.out, self.small_out = parts, out, small_out
        self.low, self.high = place % 2, place // 2
        self.core = seat_of(mp=seat + 1 - 2 * (seat % 2))
        self.across = seat_of(mp=(seat + 2) % 4)
        self.beside = seat_of(seq=place + 1 - 2 * self.low)
        self.others = [
            seat_of(seq=((self.high + step) % group) * 2 + self.low) for step in range(1, group)
        ]
        (self.own_v, self.core_v, self.across_v, self.cross_v, self.first_v, self.give_v,
         self.half_v, self.keep_v, self.piece_v, self.slab_v, self.sum_v, self.done_v) = bufs
        (self.local_s, self.core_s, self.core_r, self.x_s, self.x_r, self.y_s, self.y_r,
         self.z_s, self.z_r, self.g_s, self.g_r, self.f_s, self.f_r, self.f_l) = sems
        self.half = parts.shape[-1] // 2
        self.stages = (
            self.step_zero, self.step_core, self.step_x, self.step_y, self.step_z, self.step_gather,
            self.step_end,
        )
        self.order, self.done, self.ready, self.free = [], {}, {}, {}
        self.clock, self.made = 0.0, 0

    def remote(self, source, target, send, recv, device):
        return pltpu.make_async_remote_copy(
            src_ref=source, dst_ref=target, send_sem=send, recv_sem=recv,
            device_id=device, device_id_type=MESH,
        )

    def size(self, c):
        return self.table[c][1]

    def chunk_rows(self, c):
        return pl.ds(*self.table[c])

    def used(self, c):
        return pl.ds(0, self.size(c))

    def piece(self, c, index):
        rows = self.size(c) // self.group
        return pl.ds(pl.multiple_of(index * rows, rows), rows)

    def local_copy(self, c):
        return pltpu.make_async_copy(
            self.parts.at[pl.ds(0, 2), self.chunk_rows(c)], self.own_v.at[c % 2, :, self.used(c)],
            self.local_s.at[c % 2]
        )

    def core_copy(self, c):
        return self.remote(
            self.parts.at[pl.ds(2, 2), self.chunk_rows(c)], self.core_v.at[c % CORE_RING, :, self.used(c)],
            self.core_s.at[c], self.core_r.at[c], self.core,
        )

    def x_copy(self, c):
        return self.remote(
            self.across_v.at[c % SENT_RING, self.used(c)], self.cross_v.at[c % LAND_RING, self.used(c)],
            self.x_s.at[c], self.x_r.at[c], self.across,
        )

    def y_copy(self, c):
        return self.remote(
            self.give_v.at[c % SENT_RING, self.used(c)], self.half_v.at[c % LAND_RING, self.used(c)],
            self.y_s.at[c], self.y_r.at[c], self.beside,
        )

    def z_copy(self, c, step):
        to = (self.high + step) % self.group
        return self.remote(
            self.slab_v.at[c % SENT_RING, self.piece(c, to)],
            self.piece_v.at[c % LAND_RING, step - 1, pl.ds(0, self.size(c) // self.group)],
            self.z_s.at[c, step - 1], self.z_r.at[c, step - 1], self.others[step - 1],
        )

    def own_rows(self, c):
        return self.piece(c, self.high)

    def g_copy(self, c, step):
        mine = self.done_v.at[c % DONE_RING, self.own_rows(c)]
        return self.remote(
            mine, mine, self.g_s.at[c, step - 1], self.g_r.at[c, step - 1], self.others[step - 1]
        )

    def target(self, c):
        lanes = pl.ds(pl.multiple_of(self.low * self.half, 128), self.half)
        start, rows = self.table[c]
        if start >= LAYERS * LAYER_ROWS:
            return self.small_out.at[pl.ds(0, rows), lanes]
        turned = (start + (LAYERS - 1) * LAYER_ROWS) % (LAYERS * LAYER_ROWS)
        return self.out.at[pl.ds(turned, rows), lanes]

    def f_copy(self, c):
        return self.remote(
            self.done_v.at[c % DONE_RING, self.used(c)], self.target(c), self.f_s.at[c], self.f_r.at[c], self.beside
        )

    def f_own(self, c):
        return pltpu.make_async_copy(
            self.done_v.at[c % DONE_RING, self.used(c)], self.target(c), self.f_l.at[c]
        )

    def step_zero(self, c):
        self.local_copy(c).start()
        self.core_copy(c).start()

    def step_core(self, c):
        self.local_copy(c).wait()
        self.core_copy(c).wait()
        used = self.used(c)
        own, came = self.own_v.at[c % 2], self.core_v.at[c % CORE_RING]
        self.first_v[c % SENT_RING, used, :] = own[0, used, :].astype(F32) + came[0, used, :].astype(F32)
        self.across_v[c % SENT_RING, used, :] = (
            own[1, used, :].astype(F32) + came[1, used, :].astype(F32)
        ).astype(BF16)
        self.x_copy(c).start()

    def step_x(self, c):
        self.x_copy(c).wait()
        used = self.used(c)
        total = self.first_v[c % SENT_RING, used, :] + self.cross_v[c % LAND_RING, used, :].astype(F32)
        left, right = total[:, : self.half], total[:, self.half :]
        self.keep_v[c % SENT_RING, used, :] = jnp.where(self.low == 0, left, right)
        self.give_v[c % SENT_RING, used, :] = jnp.where(self.low == 0, right, left).astype(BF16)
        self.y_copy(c).start()

    def step_y(self, c):
        self.y_copy(c).wait()
        used = self.used(c)
        total = self.keep_v[c % SENT_RING, used, :] + self.half_v[c % LAND_RING, used, :].astype(F32)
        self.sum_v[c % SENT_RING, used, :] = total
        self.slab_v[c % SENT_RING, used, :] = total.astype(BF16)
        for step in range(1, self.group):
            self.z_copy(c, step).start()

    def step_z(self, c):
        total = self.sum_v[c % SENT_RING, self.own_rows(c), :]
        for step in range(1, self.group):
            self.z_copy(c, step).wait()
            total = total + self.piece_v[c % LAND_RING, step - 1, : self.size(c) // self.group, :].astype(F32)
        self.done_v[c % DONE_RING, self.own_rows(c), :] = total.astype(BF16)
        for step in range(1, self.group):
            self.g_copy(c, step).start()

    def step_gather(self, c):
        for step in range(1, self.group):
            self.g_copy(c, step).wait()
        self.f_copy(c).start()
        self.f_own(c).start()

    def step_end(self, c):
        self.f_own(c).wait()
        self.f_copy(c).wait()

    def passed(self, k, c, sent_after, pairs):
        for send, receive in pairs:
            for other in range(self.count):
                at = self.done.get((other, send))
                if at is not None and at > sent_after and (other, receive) in self.done:
                    return True
        return False

    def may(self, c, k):
        done = self.done
        if k and (c, k - 1) not in done:
            return False
        if c and (c - 1, k) not in done:
            return False
        kept = {0: (2, 1), 1: (SENT_RING, 2), 2: (SENT_RING, 3), 3: (SENT_RING, 4), 4: (DONE_RING, 6)}
        if k in kept:
            ring, use = kept[k]
            if c >= ring and (c - ring, use) not in done:
                return False
        landing = {
            0: (CORE_RING, 1, ((0, 1),)),
            1: (LAND_RING, 2, ((1, 2),)),
            2: (LAND_RING, 3, ((2, 3), (5, 6))),
            3: (LAND_RING, 4, ((3, 4), (4, 5))),
            4: (DONE_RING, 6, ((3, 4), (4, 5))),
        }
        if k in landing:
            ring, use, pairs = landing[k]
            if c >= ring:
                read = done.get((c - ring, use))
                if read is None or not self.passed(k, c, read, pairs):
                    return False
        return k > 0 or c < self.made

    def issue(self, c, k):
        self.stages[k](c)
        self.done[c, k] = len(self.done)
        part = self.size(c) / CHUNK
        self.clock = max(self.clock, self.ready.get((c, k), 0.0)) + 0.15 + 0.2 * part
        if k < 6:
            link, rate = LINKS[k]
            begin = max(self.clock, self.free.get(link, 0.0))
            self.free[link] = begin + rate * part
            self.ready[c, k + 1] = self.free[link] + LATENCY

    def waiting(self):
        for c in range(self.count):
            for k in range(7):
                if (c, k) not in self.done:
                    if self.may(c, k):
                        yield self.ready.get((c, k), 0.0), -k, c
                    break

    def tick(self, spent, made=0):
        self.clock += PACE * spent
        self.made = max(self.made, made)
        while True:
            now = [op for op in self.waiting() if op[0] <= self.clock]
            now = [op for op in now if op[1] or self.free.get("x", 0.0) < self.clock + AHEAD]
            if not now:
                return
            _, k, c = min(now)
            self.issue(c, -k)

    def drain(self):
        self.made = self.count
        while len(self.done) < 7 * self.count:
            ready, k, c = min((max(at, self.clock), k, c) for at, k, c in self.waiting())
            self.issue(c, -k)


def reducer_scratch(count, group, width):
    vmem, dma = pltpu.VMEM, pltpu.SemaphoreType.DMA
    half, piece, rows = width // 2, CHUNK // group, CHUNK
    bufs = [
        vmem((2, 2, rows, width), BF16),
        vmem((CORE_RING, 2, rows, width), BF16),
        vmem((SENT_RING, rows, width), BF16),
        vmem((LAND_RING, rows, width), BF16),
        vmem((SENT_RING, rows, width), F32),
        vmem((SENT_RING, rows, half), BF16),
        vmem((LAND_RING, rows, half), BF16),
        vmem((SENT_RING, rows, half), F32),
        vmem((LAND_RING, group - 1, piece, half), BF16),
        vmem((SENT_RING, rows, half), BF16),
        vmem((SENT_RING, rows, half), F32),
        vmem((DONE_RING, rows, half), BF16),
    ]
    sems = [dma((2,))] + [dma((count,))] * 6 + [dma((count, group - 1))] * 4 + [dma((count,))] * 3
    return bufs, sems


LAYER_NAMES = (
    "act", "slope", "normed", "unit_one", "unit_two", "mixed", "q", "k", "v", "pooled_k",
    "pooled_v", "entry", "down", "up", "out", "qkv",
)
LOCAL_NAMES = ("inverse_one", "inverse_two", "lse")


def backward_kernel(group, table, *refs):
    count = len(table)
    refs = list(refs)
    take = lambda n: [refs.pop(0) for _ in range(n)]
    cot_ref, gains_ref, conv_ref, bounds_ref, keep_ref = take(5)
    layers = []
    for _ in range(LAYERS):
        names = LAYER_NAMES + LOCAL_NAMES
        layers.append(dict(zip(names, take(len(names)))))
    sums_ref, small_out_ref, grad_in_ref, parts_ref = take(4)
    bufs, sems = take(12), take(14)
    (g_ref, gm_ref, gr_low, gmix_ref, send_left, send_right, from_right, from_left,
     split_ref, up_ref, whole_ref, load_s, halo_s, store_s, out_s) = take(15)
    total, width = g_ref.shape
    read = bounds_reader(bounds_ref, total)
    place, seat = lax.axis_index("seq"), lax.axis_index("mp")
    seqs = lax.axis_size("seq")
    red = Reducer(group, table, parts_ref, sums_ref, small_out_ref, bufs, sems)
    ahead = seat_of(seq=(place + (seat + 1) // 4) % seqs, mp=(seat + 1) % 4)
    behind = seat_of(seq=(place + seqs - (3 - seat + 1) // 4) % seqs, mp=(seat + 3) % 4)
    barrier = pltpu.get_barrier_semaphore()
    devices = [red.core, red.across, red.beside, ahead, behind] + red.others
    for device in devices:
        pl.semaphore_signal(barrier, inc=1, device_id=device, device_id_type=MESH)
    pl.semaphore_wait(barrier, len(devices))

    split_ref[...] = jnp.zeros_like(split_ref)
    up_ref[...] = jnp.zeros_like(up_ref)
    whole_ref[...] = jnp.zeros_like(whole_ref)
    quarter = width // 4
    feed = 4 * width

    def load(source, target, index):
        copy = pltpu.make_async_copy(source, target, load_s.at[index])
        copy.start()
        return copy

    def place_of(part):
        return (part % 2) * 2 + part // 2

    def norm_back(layer, grad, unit, inverse, gain, result, low_ref, rows_at):
        gain_row, shift_row, bias_row = rows_at

        @pl.loop(0, total // NORM_ROWS)
        def _(block):
            rows = pl.ds(pl.multiple_of(block * NORM_ROWS, NORM_ROWS), NORM_ROWS)
            g, n = grad[rows, :], unit[rows, :]
            a = g * gain
            mean = jnp.sum(a, axis=1, keepdims=True) * (1.0 / width)
            tilt = jnp.sum(a * n, axis=1, keepdims=True) * (1.0 / width)
            back = (a - mean - n * tilt) * inverse[rows, :]
            result[rows, :] = back
            low_ref[rows, :] = back.astype(BF16)
            for at, value in ((gain_row, g * n), (shift_row, g), (bias_row, back)):
                whole_ref[layer, at : at + 1, :] += jnp.sum(value, axis=0, keepdims=True)

    def feed_scope(layer, base, ready, down, up, act, slope, normed, unit_one, unit_two, out, mixed,
                   gm_low, gn_ref, ga_ref, gp_low, stage, normed_t):
        ref = layers[layer]
        pairs = ((ref["unit_two"], unit_two), (ref["act"], act), (ref["down"], down),
                 (ref["slope"], slope), (ref["normed"], normed), (ref["up"], up),
                 (ref["unit_one"], unit_one), (ref["out"], out), (ref["mixed"], mixed))
        copies = [load(a, b, i) for i, (a, b) in enumerate(pairs)]
        copies[0].wait()
        norm_back(layer, g_ref, unit_two, ref["inverse_two"], gains_ref[layer, 1:2, :], gm_ref,
                  gm_low, (1, 5, 4))
        red.tick(4.0)
        stores = []

        def store(part, at):
            copy = pltpu.make_async_copy(
                stage.at[part % 2], parts_ref.at[place_of(part), pl.ds(at, width)], store_s.at[part % 2]
            )
            copy.start()
            stores.append(copy)

        def settle(keep):
            while len(stores) > keep:
                stores.pop(0).wait()

        copies[1].wait()
        for part in range(4):
            settle(1)
            cols = slice(part * width, (part + 1) * width)
            stage[part % 2] = product_left_t(act[:, cols], gm_low[...]).astype(BF16)
            store(part, base)
            if part == 1:
                red.tick(2.5)
        settle(0)
        red.tick(2.5, ready + 3)
        for copy in copies[2:6]:
            copy.wait()
        normed_t[...] = normed[...].T
        for part in range(4):
            cols = slice(part * width, (part + 1) * width)
            ga_ref[...] = product_right_t(gm_low[...], down[cols, :])
            up_ref[layer, part : part + 1, :] = jnp.zeros((1, width), F32)

            @pl.loop(0, total // NORM_ROWS)
            def _(block):
                rows = pl.ds(pl.multiple_of(block * NORM_ROWS, NORM_ROWS), NORM_ROWS)
                gp = ga_ref[rows, :] * slope[rows, cols].astype(F32)
                gp_low[rows, :] = gp.astype(BF16)
                up_ref[layer, part : part + 1, :] += jnp.sum(gp, axis=0, keepdims=True)

            made = product_right_t(gp_low[...], up[:, cols])
            if part == 0:
                gn_ref[...] = gm_ref[...] + made
            else:
                gn_ref[...] += made
            red.tick(3.0)
            settle(1)
            stage[part % 2] = product(normed_t[...], gp_low[...]).astype(BF16)
            store(part, base + width)
            red.tick(1.5)
        for copy in copies[6:]:
            copy.wait()
        norm_back(layer, gn_ref, unit_one, ref["inverse_one"], gains_ref[layer, 0:1, :], gm_ref,
                  gr_low, (0, 3, 2))
        settle(0)
        red.tick(3.0, ready + 6)
        gmix_ref[...] = product_right_t(gr_low[...], out[...]).astype(BF16)
        stage[0] = product_left_t(mixed[...], gr_low[...]).astype(BF16)
        store_parts(stage.at[0], base + 2 * width, 0)
        red.tick(3.0)

    def part_copies(source, at, bank):
        return [
            pltpu.make_async_copy(
                source.at[pl.ds(part * quarter, quarter)],
                parts_ref.at[place_of(part), pl.ds(at, quarter)],
                out_s.at[bank, part],
            )
            for part in range(4)
        ]

    def store_parts(source, at, bank):
        copies = part_copies(source, at, bank)
        for copy in copies:
            copy.start()
        for copy in copies:
            copy.wait()

    def attend_scope(layer, grad_q, grad_k, grad_v, q, k, v, pooled_k, pooled_v,
                     wide_k, wide_v, far_k, far_v, wide_f32):
        ref = layers[layer]
        names = ("q", "k", "v", "pooled_k", "pooled_v")
        copies = [load(ref[n], b, i) for i, (n, b) in enumerate(zip(names, (q, k, v, pooled_k, pooled_v)))]
        for copy in copies:
            copy.wait()
        attend_backward_body(
            q, k, v, pooled_k, pooled_v, gmix_ref, ref["lse"],
            lambda tile: read(tile * TILE, TILE), keep_ref,
            conv_ref.at[layer], grad_q, grad_k, grad_v, split_ref.at[layer],
            wide_k, wide_v, far_k, far_v, wide_f32, red.tick,
        )

    def project_scope(layer, base, ready, grad_q, grad_k, grad_v, qkv, entry, wide, full):
        ref = layers[layer]
        copies = [load(ref["qkv"], qkv, 0), load(ref["entry"], entry, 1)]
        red.tick(3.0)
        for copy in copies:
            copy.wait()
        wide[...] = product(grad_k[...], qkv[1])
        wide[...] += product(grad_v[...], qkv[2])
        send_left[...] = wide[LEFT - LEFT_SENT : LEFT, :].astype(BF16)
        send_right[...] = wide[LEFT + total :, :].astype(BF16)
        for copy in halo(layer):
            copy.start()
        red.tick(4.0)
        own = slice(LEFT, LEFT + total)
        gm_ref[...] += wide[own, :]
        gm_ref[...] += product(grad_q[...], qkv[0])
        banks = []
        for which, (grad, rows) in enumerate(((grad_q, own), (grad_k, slice(None)), (grad_v, slice(None)))):
            bank = which % 2
            if which >= 2:
                for copy in banks[which - 2]:
                    copy.wait()
            full[bank] = product_left_t(grad[...], entry[rows, :]).astype(BF16)
            copies = part_copies(full.at[bank], base + 2 * width + (which + 1) * quarter, bank)
            for copy in copies:
                copy.start()
            banks.append(copies)
            red.tick(2.5)
        for copies in banks[1:]:
            for copy in copies:
                copy.wait()
        red.tick(0.5, ready + 9 if layer else count - 1)

    def halo(layer):
        return [
            red.remote(send_left, from_right, halo_s.at[layer, 0], halo_s.at[layer, 1], behind),
            red.remote(send_right, from_left, halo_s.at[layer, 2], halo_s.at[layer, 3], ahead),
        ]

    def add_halo(layer):
        for copy in halo(layer):
            copy.wait()
        index = place * 4 + seat
        right = jnp.where(index == 4 * seqs - 1, 0.0, 1.0)
        left = jnp.where(index == 0, 0.0, 1.0)
        gm_ref[total - LEFT_SENT :, :] += from_right[...].astype(F32) * right
        gm_ref[:RIGHT, :] += from_left[...].astype(F32) * left

    start = load(cot_ref, gr_low, 0)
    start.wait()
    g_ref[...] = gr_low[...].astype(F32)
    vmem = pltpu.VMEM
    block = (total, width)
    wide_rows = total + LEFT + RIGHT
    far_rows = total // 4 + 2 * POOL_REACH
    pairs = width // PAIR
    for turn, layer in enumerate(reversed(range(LAYERS))):
        base = turn * LAYER_ROWS
        ready = turn * (LAYER_ROWS // CHUNK)

        pl.run_scoped(
            functools.partial(feed_scope, layer, base, ready),
            vmem((feed, width), BF16), vmem((width, feed), BF16), vmem((total, feed), BF16),
            vmem((total, feed), BF16), vmem(block, BF16), vmem(block, F32), vmem(block, F32),
            vmem((width, width), BF16), vmem(block, BF16), vmem(block, BF16), vmem(block, F32),
            vmem(block, F32), vmem(block, BF16), vmem((2, width, width), BF16), vmem((width, total), BF16),
        )

        def attention(grad_q, grad_k, grad_v):
            pl.run_scoped(
                functools.partial(attend_scope, layer, grad_q, grad_k, grad_v),
                vmem(block, BF16), vmem((wide_rows, width), BF16), vmem((wide_rows, width), BF16),
                vmem((far_rows, width), BF16), vmem((far_rows, width), BF16),
                vmem((pairs, wide_rows, PAIR), F32), vmem((pairs, wide_rows, PAIR), F32),
                vmem((far_rows, width), F32), vmem((far_rows, width), F32),
                vmem((wide_rows, PAIR), F32),
            )
            pl.run_scoped(
                functools.partial(project_scope, layer, base, ready, grad_q, grad_k, grad_v),
                vmem((3, width, width), BF16), vmem((wide_rows, width), BF16),
                vmem((wide_rows, width), F32), vmem((2, width, width), BF16),
            )

        pl.run_scoped(
            attention, vmem(block, BF16), vmem((wide_rows, width), BF16), vmem((wide_rows, width), BF16)
        )
        if turn < LAYERS - 1:
            add_halo(layer)
            red.tick(3.0)
            g_ref[...] = gm_ref[...]

    def small_scope(stage):
        stage[...] = jnp.zeros_like(stage)
        for layer in range(LAYERS):
            at = 32 * layer
            for part in range(4):
                pos = place_of(part)
                rolled = split_ref[layer]
                if part:
                    rolled = pltpu.roll(rolled, width - part * quarter, 1)
                stage[pos, at : at + 16, :] = rolled.astype(BF16)
                rest = jnp.concatenate([whole_ref[layer], up_ref[layer, part : part + 1, :]] + [jnp.zeros((7, width), F32)], axis=0)
                stage[pos, at + 16 : at + 32, :] = rest.astype(BF16)
        copy = pltpu.make_async_copy(
            stage, parts_ref.at[:, pl.ds(LAYERS * LAYER_ROWS, table[-1][1])], store_s.at[0]
        )
        copy.start()
        copy.wait()

    pl.run_scoped(small_scope, vmem((4, table[-1][1], width), BF16))

    red.tick(1.0, count)
    add_halo(0)
    final = pltpu.make_async_copy(gm_ref, grad_in_ref, load_s.at[0])
    final.start()
    red.drain()
    final.wait()


def backward(cot, gains, conv, bounds, keep, saved):
    total, width = cot.shape
    group = lax.axis_size("seq") // 2
    last = max(CHUNK // 2, 16 * group)
    small_rows = max(64, 16 * group)
    rows = LAYERS * LAYER_ROWS
    cut = rows - width
    table = [(at, CHUNK) for at in range(0, cut, CHUNK)]
    table += [(at, last) for at in range(cut, rows, last)]
    table.append((rows, small_rows))
    rows += small_rows
    count = len(table)
    vmem, dma = pltpu.VMEM, pltpu.SemaphoreType.DMA
    anywhere = pl.BlockSpec(memory_space=pl.ANY)
    local = pl.BlockSpec(memory_space=pltpu.VMEM)
    args = [cot, gains, conv, bounds, keep]
    specs = [anywhere] + [local] * 4
    for layer in saved:
        args += [layer[name] for name in LAYER_NAMES + LOCAL_NAMES]
        specs += [anywhere] * len(LAYER_NAMES) + [local] * len(LOCAL_NAMES)
    bufs, sems = reducer_scratch(count, group, width)
    shape = jax.ShapeDtypeStruct
    return pl.pallas_call(
        functools.partial(backward_kernel, group, tuple(table)),
        out_shape=(
            shape((LAYERS * LAYER_ROWS, width), BF16),
            shape((small_rows, width), BF16),
            shape((total, width), F32),
            shape((4, rows, width), BF16),
        ),
        in_specs=specs,
        out_specs=(anywhere,) * 4,
        scratch_shapes=bufs + sems + [
            vmem((total, width), F32),
            vmem((total, width), F32),
            vmem((total, width), BF16),
            vmem((total, width), BF16),
            vmem((LEFT_SENT, width), BF16),
            vmem((RIGHT, width), BF16),
            vmem((LEFT_SENT, width), BF16),
            vmem((RIGHT, width), BF16),
            vmem((LAYERS, 16, width), F32),
            vmem((LAYERS, 8, width), F32),
            vmem((LAYERS, 8, width), F32),
            dma((9,)),
            dma((LAYERS, 4)),
            dma((6,)),
            dma((2, 4)),
        ],
        compiler_params=pltpu.CompilerParams(
            collective_id=0, has_side_effects=True, vmem_limit_bytes=60 * 1024 * 1024
        ),
        name="backward",
    )(*args)


def row_blocks(total, size, body):
    @pl.loop(0, total // size)
    def _(block):
        body(pl.ds(pl.multiple_of(block * size, size), size))


def attend_forward_body(
    q_ref, k_ref, v_ref, bounds_of, keep_ref, taps, shifts,
    mixed_ref, lse_ref, pooled_k_ref, pooled_v_ref, wide_f32, pairs, tick,
):
    for which, (source, pooled) in enumerate(((k_ref, pooled_k_ref), (v_ref, pooled_v_ref))):
        pool_into(source, wide_f32, keep_ref, taps[which], shifts[which], pooled, pairs)

    tick(0.7 * len(pairs))

    def one_tile(tile):
        rows = pl.ds(pl.multiple_of(tile * TILE, TILE), TILE)
        bias = tile_bias(tile, *bounds_of(tile))
        bias = jnp.concatenate([bias, bias], axis=1)
        for pair in pairs:
            lanes = slice(pair * PAIR, (pair + 1) * PAIR)
            query = stacked(q_ref[rows, lanes] * BF16(HEAD_DIM**-0.5))
            key = keys_of(k_ref, pooled_k_ref, tile, lanes)
            value = keys_of(v_ref, pooled_v_ref, tile, lanes)
            scores = product_right_t(key, query) + bias
            most = jnp.max(scores, axis=0, keepdims=True)
            weight = jnp.exp(scores - most)
            total = jnp.sum(weight, axis=0, keepdims=True)
            both = product_left_t(value, weight.astype(BF16)) * (1.0 / total)
            mixed_ref[rows, lanes] = unstack(both).T.astype(BF16)
            lse_ref[tile, pair : pair + 1, :] = most + jnp.log(total)

    tiles = q_ref.shape[0] // TILE
    for begin in range(0, tiles, 2):
        pl.loop(begin, begin + 2)(one_tile)
        tick(1.0 * len(pairs))


SAVED_NAMES = LAYER_NAMES
KINDS = 8
TENSORS = KINDS * LAYERS


def forward_kernel(*refs):
    refs = list(refs)
    take = lambda n: [refs.pop(0) for _ in range(n)]
    (x_ref, qkv_ref, out_ref, up_ref, down_ref, qv_ref, taps_ref, pool_ref, feed_ref, gains_ref,
     biases_ref, bounds_ref) = take(12)
    hidden_ref, conv_ref, keep_ref = take(3)
    results = [dict(zip(SAVED_NAMES + LOCAL_NAMES, take(len(SAVED_NAMES + LOCAL_NAMES)))) for _ in range(LAYERS)]
    (qkv_v, out_v, up_v, down_v, entry_v, q_v, k_v, v_v, far_k, far_v, mixed_v, hidden_v, acc_v,
     unit_one, low_v, act_v, slope_v, pre_v, wide_f32, small_v, full_v,
     own_s, x_s, x_r, y_s, y_r, c_s, c_r, d_s, d_r, halo_s, save_s, load_s) = take(33)
    total, width = hidden_v.shape
    quarter, half = width // 4, width // 2
    place, seat, seqs = lax.axis_index("seq"), lax.axis_index("mp"), lax.axis_size("seq")
    low = place % 2
    core = seat_of(mp=seat + 1 - 2 * (seat % 2))
    across = seat_of(mp=(seat + 2) % 4)
    beside = seat_of(seq=place + 1 - 2 * low)
    ahead = seat_of(seq=(place + (seat + 1) // 4) % seqs, mp=(seat + 1) % 4)
    behind = seat_of(seq=(place + seqs - (4 - seat) // 4) % seqs, mp=(seat + 3) % 4)
    barrier = pltpu.get_barrier_semaphore()
    devices = [core, across, beside, ahead, behind]
    for device in devices:
        pl.semaphore_signal(barrier, inc=1, device_id=device, device_id_type=MESH)
    entry_own = pl.ds(LEFT, total)
    first_load = pltpu.make_async_copy(x_ref, entry_v.at[0, entry_own], load_s.at[0])
    first_load.start()
    small_v[0] = jnp.zeros(small_v.shape[1:], F32)
    for layer in range(LAYERS):
        for which in range(2):
            at = 2 * layer + which
            small_v[0, at : at + 1, :quarter] = qv_ref[layer, which : which + 1, :]
            small_v[0, 24 + at : 25 + at, :quarter] = pool_ref[layer, which : which + 1, :]
            at = 4 + 10 * layer + 5 * which
            small_v[0, at : at + 5, :quarter] = taps_ref[layer, which]
        small_v[0, 32 + layer : 33 + layer, :] = feed_ref[layer : layer + 1, :]
    read = bounds_reader(bounds_ref, total)
    far = 4 * POOL_REACH
    edges = []
    for one in read(0, total):
        wide_f32[:total, :] = jnp.broadcast_to(one.astype(F32), (PAIR, total)).T
        edges.append(jnp.concatenate(
            [
                jnp.broadcast_to(wide_f32[0:1, :], (POOL_REACH, PAIR)),
                wide_f32[pl.ds(0, total // 4, stride=4), :],
                jnp.broadcast_to(wide_f32[total - 1 : total, :], (POOL_REACH, PAIR)),
            ],
            axis=0,
        ))
    token = 4 * lax.broadcasted_iota(jnp.int32, edges[0].shape, 0) - far - 2
    for tap in range(5):
        at = (token + tap).astype(F32)
        keep_ref[tap] = jnp.where((at >= edges[0]) & (at < edges[1]), 1.0, 0.0)
    for layer in range(LAYERS):
        entry_v[layer, : LEFT - LEFT_SENT, :] = jnp.zeros((LEFT - LEFT_SENT, width), BF16)
    pl.semaphore_wait(barrier, len(devices))

    def remote(source, target, send, recv, device):
        return pltpu.make_async_remote_copy(
            src_ref=source, dst_ref=target, send_sem=send, recv_sem=recv,
            device_id=device, device_id_type=MESH,
        )

    def span(size, side):
        if side is None:
            return 0, size
        return pl.multiple_of(side * (size // 2), size // 2), size // 2

    def shard(tensor, side=None):
        layer, kind = tensor // KINDS, tensor % KINDS
        if kind < 3:
            return qkv_ref.at[layer, (1, 2, 0)[kind], pl.ds(*span(quarter, side))]
        if kind == 3:
            return out_ref.at[layer, pl.ds(*span(quarter, side))]
        piece = (kind - 4) // 2 * half
        at, count = span(half, side)
        if kind % 2 == 0:
            at, count = span(width, side)
            return up_ref.at[layer, pl.ds(at, count), pl.ds(piece, half)]
        return down_ref.at[layer, pl.ds(piece + at, count)]

    def landed(tensor, part, side=None):
        layer, kind = tensor // KINDS, tensor % KINDS
        if kind < 4:
            at, count = span(quarter, side)
            rows = pl.ds(part * quarter + at, count)
            if kind < 3:
                return qkv_v.at[layer, (1, 2, 0)[kind], rows]
            return out_v.at[layer, rows]
        piece = part * width + (kind - 4) // 2 * half
        if kind % 2 == 0:
            return up_v.at[layer, pl.ds(*span(width, side)), pl.ds(piece, half)]
        at, count = span(half, side)
        return down_v.at[layer, pl.ds(piece + at, count)]

    def own_copy(t):
        return pltpu.make_async_copy(shard(t), landed(t, 0), own_s.at[t])

    def x_copy(t):
        return remote(shard(t, low), landed(t, 2, low), x_s.at[t], x_r.at[t], across)

    def y_copy(t):
        return remote(landed(t, 2, low), landed(t, 2, low), y_s.at[t], y_r.at[t], beside)

    def c_copy(t):
        return remote(shard(t), landed(t, 1), c_s.at[t], c_r.at[t], core)

    def d_copy(t):
        return remote(landed(t, 2), landed(t, 3), d_s.at[t], d_r.at[t], core)

    model = {"clock": 0.0, "x": 5.0, "y": 5.0, "next": [0, 0, 0], "at": {}}

    def issue(k):
        t = model["next"][k]
        model["next"][k] += 1
        cost = 3.3 if t % KINDS < 4 else 6.6
        model["clock"] = max(model["clock"], model["at"].get((t, k), 0.0)) + 0.15
        if k == 0:
            own_copy(t).start()
            c_copy(t).start()
            x_copy(t).start()
        elif k == 1:
            x_copy(t).wait_recv()
            y_copy(t).start()
        else:
            y_copy(t).wait_recv()
            d_copy(t).start()
        if k < 2:
            link = "xy"[k]
            model[link] = max(model[link], model["clock"]) + cost
            model["at"][t, k + 1] = model[link] + LATENCY + 1.0

    def tick(spent):
        model["clock"] += spent
        while True:
            clock = model["clock"]
            for k in (2, 1, 0):
                t = model["next"][k]
                if t >= TENSORS or (k and t >= model["next"][k - 1]):
                    continue
                if model["at"].get((t, k), 0.0) <= clock if k else model["x"] < clock + 2 * AHEAD:
                    issue(k)
                    break
            else:
                return

    arrived = set()

    def need(t, part):
        if (t, part) in arrived:
            return
        arrived.add((t, part))
        for k in range(1 if part < 2 else 3):
            while model["next"][k] <= t:
                issue(k)
        if part == 0:
            own_copy(t).wait()
        elif part == 1:
            c_copy(t).wait_recv()
        elif part == 3:
            d_copy(t).wait_recv()

    small_index = TENSORS
    small_x = remote(small_v.at[0], small_v.at[2], x_s.at[small_index], x_r.at[small_index], across)
    small_c = remote(small_v.at[0], small_v.at[1], c_s.at[small_index], c_r.at[small_index], core)
    small_d = remote(small_v.at[2], small_v.at[3], d_s.at[small_index], d_r.at[small_index], core)

    def halo(layer):
        entry = entry_v.at[layer]
        return (
            remote(
                entry.at[pl.ds(LEFT + total - LEFT_SENT, LEFT_SENT)],
                entry.at[pl.ds(LEFT - LEFT_SENT, LEFT_SENT)],
                halo_s.at[layer, 0], halo_s.at[layer, 1], ahead,
            ),
            remote(
                entry.at[pl.ds(LEFT, RIGHT)], entry.at[pl.ds(LEFT + total, RIGHT)],
                halo_s.at[layer, 2], halo_s.at[layer, 3], behind,
            ),
        )

    saves = {}

    def save(layer, name, source):
        index = SAVED_NAMES.index(name)
        copy = pltpu.make_async_copy(source, results[layer][name], save_s.at[layer, index])
        copy.start()
        saves[layer, name] = copy

    def settle(layer, *names):
        for name in names:
            if (layer, name) in saves:
                saves.pop((layer, name)).wait()

    def norm(layer, which, extra, result, low_ref, unit, inverse):
        gain = gains_ref[layer, which : which + 1, :]
        offset = biases_ref[layer, 2 * which + 1 : 2 * which + 2, :]
        shift_row = biases_ref[layer, 2 * which : 2 * which + 1, :]

        def body(rows):
            value = hidden_v[rows, :] + (extra[rows, :] + shift_row)
            average = jnp.sum(value, axis=1, keepdims=True) * (1.0 / width)
            centered = value - average
            spread = jnp.sum(centered * centered, axis=1, keepdims=True) * (1.0 / width)
            scale = lax.rsqrt(spread + NORM_EPSILON)
            one = centered * scale
            out = one * gain + offset
            unit[rows, :] = one
            inverse[rows, :] = scale
            result[rows, :] = out
            if low_ref is not None:
                low_ref[rows, :] = out.astype(BF16)

        row_blocks(total, NORM_ROWS, body)

    first_load.wait()
    for copy in halo(0):
        copy.start()
    small_x.start()
    small_c.start()
    tick(3.0)
    row_blocks(total, NORM_ROWS, lambda rows: hidden_v.__setitem__(
        (rows, slice(None)), entry_v[0, pl.ds(rows.start + LEFT, NORM_ROWS), :].astype(F32)))

    for layer in range(LAYERS):
        entry = entry_v.at[layer]
        tensor = KINDS * layer
        settle(layer - 1, "q", "k", "v", "pooled_k", "pooled_v", "mixed", "normed")

        def project(which, target, side, rows):
            lanes = slice(side * half, (side + 1) * half)
            kind = (2, 0, 1)[which]
            for part in (2 * side, 2 * side + 1):
                need(tensor + kind, part)
            into = rows if which else slice(0, total)
            made = product_right_t(entry[rows, :], qkv_v[layer, which, lanes, :])
            if which != 1:
                row = 2 * layer + which // 2
                made = made + full_v[row : row + 1, lanes]
            target[into, lanes] = made.astype(BF16)

        own = slice(LEFT, LEFT + total)
        outer = (slice(0, LEFT), slice(LEFT + total, LEFT + total + RIGHT))

        def project_own(side):
            project(1, k_v, side, own)
            if layer == 0 and side == 0:
                small_params()
            project(2, v_v, side, own)
            project(0, q_v, side, own)
            tick(3.0)

        def project_outer(side):
            for rows in outer:
                project(1, k_v, side, rows)
                project(2, v_v, side, rows)
            tick(2.0)

        def small_params():
            small_c.wait_recv()
            small_x.wait_recv()
            small_d.start()
            small_d.wait_recv()
            rows = [small_v[0, :32, :]] + [
                pltpu.roll(small_v[part, :32, :], part * quarter, 1) for part in range(1, 4)
            ]
            full_v[...] = rows[0] + rows[1] + rows[2] + rows[3]
            for one in range(LAYERS):
                for which in range(2):
                    at = 4 + 10 * one + 5 * which
                    conv_ref[one, which] = full_v[at : at + 5, :]

        def attend(pairs):
            taps = [
                lambda tap, at=4 + 10 * layer + 5 * which: full_v[at + tap : at + tap + 1, :]
                for which in range(2)
            ]
            shifts = [full_v[24 + 2 * layer + which : 25 + 2 * layer + which, :] for which in range(2)]
            attend_forward_body(
                q_v, k_v, v_v, lambda tile: read(tile * TILE, TILE), keep_ref, taps, shifts,
                mixed_v, results[layer]["lse"], far_k, far_v, wide_f32, pairs, tick,
            )

        pairs = width // PAIR
        if layer == 0:
            project_own(0)
            for copy in halo(layer):
                copy.wait_recv()
            tick(4.0)
            project_outer(0)
            attend(range(pairs // 2))
            project_own(1)
            project_outer(1)
            attend(range(pairs // 2, pairs))
        else:
            project_own(0)
            project_own(1)
            for copy in halo(layer):
                copy.wait_recv()
            tick(4.0)
            project_outer(0)
            project_outer(1)
            attend(range(pairs))
        for name, source in (("entry", entry), ("q", q_v), ("k", k_v), ("v", v_v),
                             ("pooled_k", far_k), ("pooled_v", far_v), ("mixed", mixed_v)):
            save(layer, name, source)
        for part in range(4):
            need(tensor + 3, part)
        acc_v[...] = product(mixed_v[...], out_v[layer])
        settle(layer - 1, "unit_one", "unit_two", "act", "slope")
        norm(layer, 0, acc_v, hidden_v, low_v, unit_one, results[layer]["inverse_one"])
        save(layer, "unit_one", unit_one)
        save(layer, "normed", low_v)
        tick(4.0)
        begun = False
        for part, piece in ((0, 0), (0, 1), (1, 0), (1, 1), (2, 0), (3, 0), (2, 1), (3, 1)):
            need(tensor + 4 + 2 * piece, part)
            need(tensor + 5 + 2 * piece, part)
            at = part * width + piece * half
            cols = slice(at, at + half)
            pre_v[...] = product(low_v[...], up_v[layer, :, cols])
            up_row = small_v[part, 32 + layer : 33 + layer, piece * half : (piece + 1) * half]

            def body(rows, cols=cols, up_row=up_row):
                act, slope = gelu_parts(pre_v[rows, :] + up_row)
                act_v[rows, cols] = act.astype(BF16)
                slope_v[rows, cols] = slope.astype(BF16)

            row_blocks(total, NORM_ROWS, body)
            made = product(act_v[:, cols], down_v[layer, cols, :])
            if begun:
                acc_v[...] += made
            else:
                acc_v[...] = made
            begun = True
            tick(3.0)
        save(layer, "act", act_v)
        save(layer, "slope", slope_v)
        save(layer, "qkv", qkv_v.at[layer])
        save(layer, "out", out_v.at[layer])
        save(layer, "up", up_v.at[layer])
        save(layer, "down", down_v.at[layer])
        settle(layer, "unit_one")
        norm(layer, 1, acc_v, hidden_v, None, unit_one, results[layer]["inverse_two"])
        save(layer, "unit_two", unit_one)
        if layer + 1 < LAYERS:
            later = entry_v.at[layer + 1]
            row_blocks(total, NORM_ROWS, lambda rows: later.__setitem__(
                (pl.ds(rows.start + LEFT, NORM_ROWS), slice(None)), hidden_v[rows, :].astype(BF16)))
            for copy in halo(layer + 1):
                copy.start()
            tick(4.0)
    last = pltpu.make_async_copy(hidden_v, hidden_ref, load_s.at[0])
    last.start()
    for key in list(saves):
        settle(*key)
    small_x.wait_send()
    small_c.wait_send()
    small_d.wait_send()
    for t in range(TENSORS):
        for copy in (x_copy(t), y_copy(t), c_copy(t), d_copy(t)):
            copy.wait_send()
    for layer in range(LAYERS):
        for copy in halo(layer):
            copy.wait_send()
    last.wait()


def forward(x, qkv_t, out, up, down, *rest):
    total, width = x.shape
    vmem, dma, shape = pltpu.VMEM, pltpu.SemaphoreType.DMA, jax.ShapeDtypeStruct
    anywhere = pl.BlockSpec(memory_space=pl.ANY)
    local = pl.BlockSpec(memory_space=pltpu.VMEM)
    feed, wide_rows, far_rows = 4 * width, total + LEFT + RIGHT, total // 4 + 2 * POOL_REACH
    block, wide, far, square = (total, width), (wide_rows, width), (far_rows, width), (width, width)
    saved = dict(
        act=((total, feed), BF16), slope=((total, feed), BF16), normed=(block, BF16),
        unit_one=(block, F32), unit_two=(block, F32), mixed=(block, BF16), q=(block, BF16),
        k=(wide, BF16), v=(wide, BF16), pooled_k=(far, BF16), pooled_v=(far, BF16), entry=(wide, BF16),
        down=((feed, width), BF16), up=((width, feed), BF16), out=(square, BF16),
        qkv=((3, width, width), BF16), inverse_one=((total, 1), F32), inverse_two=((total, 1), F32),
        lse=((total // TILE, width // PAIR, 2 * TILE), F32),
    )
    names = SAVED_NAMES + LOCAL_NAMES
    shapes = [shape(block, F32), shape((LAYERS, 2, 5, width), F32), shape((5, far_rows, PAIR), F32)]
    specs = [anywhere, local, local]
    for _ in range(LAYERS):
        shapes += [shape(*saved[name]) for name in names]
        specs += [anywhere] * len(SAVED_NAMES) + [local] * len(LOCAL_NAMES)
    tensors = dma((TENSORS + 1,))
    outs = pl.pallas_call(
        forward_kernel,
        out_shape=tuple(shapes),
        in_specs=[anywhere] * 5 + [local] * len(rest),
        out_specs=tuple(specs),
        scratch_shapes=[
            vmem((LAYERS, 3, width, width), BF16), vmem((LAYERS, width, width), BF16),
            vmem((LAYERS, width, feed), BF16), vmem((LAYERS, feed, width), BF16),
            vmem((LAYERS, wide_rows, width), BF16),
            vmem(block, BF16), vmem(wide, BF16), vmem(wide, BF16), vmem(far, BF16), vmem(far, BF16),
            vmem(block, BF16), vmem(block, F32), vmem(block, F32), vmem(block, F32),
            vmem(block, BF16), vmem((total, feed), BF16), vmem((total, feed), BF16),
            vmem((total, width // 2), F32), vmem((wide_rows, PAIR), F32), vmem((4, 40, width), F32),
            vmem((32, width), F32),
            tensors, tensors, tensors, tensors, tensors, tensors, tensors, tensors, tensors,
            dma((LAYERS, 4)), dma((LAYERS, len(SAVED_NAMES))), dma((2,)),
        ],
        compiler_params=pltpu.CompilerParams(
            collective_id=1, has_side_effects=True, vmem_limit_bytes=60 * 1024 * 1024
        ),
        name="forward",
    )(x, qkv_t, out, up, down, *rest)
    size = len(names)
    stack = [dict(zip(names, outs[3 + size * one : 3 + size * (one + 1)])) for one in range(LAYERS)]
    return outs[0], outs[1], outs[2], stack


def unpack_kernel(
    down_in, up_in, out_in, qkv_in, small_in,
    down_ref, up_ref, out_ref, qkv_ref, qv_ref, taps_ref, pool_ref, feed_ref, gains_ref, biases_ref,
):
    down_ref[0] = down_in[0].astype(F32)
    up_ref[0] = up_in[0].astype(F32)
    out_ref[0] = out_in[0].astype(F32)
    qkv_ref[0, 0] = qkv_in[0].astype(F32)
    quarter = qv_ref.shape[-1]

    @pl.when((pl.program_id(0) == 0) & (pl.program_id(1) == 0))
    def _():
        for layer in range(LAYERS):
            rows = small_in[32 * layer : 32 * layer + 32, :].astype(F32)
            qv_ref[layer] = rows[0:2, :quarter]
            for which in range(2):
                at = 2 + 5 * which
                taps_ref[layer, which] = rows[at : at + 5, :quarter]
            pool_ref[layer] = rows[12:14, :quarter]
            gains_ref[layer] = rows[16:18]
            biases_ref[layer] = rows[18:22]
            feed_ref[layer : layer + 1, :] = rows[24:25]


def unpack(sums, small):
    width = sums.shape[1]
    quarter = width // 4
    shape = jax.ShapeDtypeStruct
    by_layer = sums.reshape(LAYERS, LAYER_ROWS, width)
    third = width // 3

    def view(rows, first):
        return pl.BlockSpec((1, rows, width), lambda layer, j: (layer, first // rows + j, 0))

    def whole(*dims):
        return pl.BlockSpec(dims, lambda layer, j: (0,) * len(dims))

    rest = ((LAYERS, 2, quarter), (LAYERS, 2, 5, quarter), (LAYERS, 2, quarter), (LAYERS, width),
            (LAYERS, 2, width), (LAYERS, 4, width))
    return pl.pallas_call(
        unpack_kernel,
        grid=(LAYERS, 3),
        out_shape=(
            shape((LAYERS, width, width), F32), shape((LAYERS, width, width), F32),
            shape((LAYERS, quarter, width), F32), shape((LAYERS, 3, quarter, width), F32),
        ) + tuple(shape(dims, F32) for dims in rest),
        in_specs=[
            view(third, 0), view(third, width), view(quarter // 3, 2 * width),
            view(quarter, 2 * width + quarter), whole(*small.shape),
        ],
        out_specs=[
            view(third, 0), view(third, 0), view(quarter // 3, 0),
            pl.BlockSpec((1, 1, quarter, width), lambda layer, j: (layer, j, 0, 0)),
        ] + [whole(*dims) for dims in rest],
        compiler_params=pltpu.CompilerParams(vmem_limit_bytes=32 * 1024 * 1024),
        name="unpack",
    )(by_layer, by_layer, by_layer, by_layer, small)


def shards(
    inputs,
    doc_bounds,
    qkv_weight,
    qv_bias,
    conv_weight,
    conv_bias,
    out_weight,
    up_weight,
    up_bias,
    down_weight,
    norm_gains,
    shared_biases,
    cotangent,
):
    hidden, conv_all, keep, stack = forward(
        inputs, qkv_weight.transpose(0, 1, 3, 2), out_weight, up_weight, down_weight, qv_bias, conv_weight,
        conv_bias, up_bias, norm_gains, shared_biases, doc_bounds,
    )
    sums, small, gradient, _ = backward(cotangent, norm_gains, conv_all, doc_bounds, keep, stack)
    down, up, out, qkv, qv, taps, pool, feed, gains, biases = unpack(sums, small)
    return (hidden, gradient, qkv.transpose(0, 1, 3, 2), qv, taps, pool, out, up, feed, down, gains, biases)


def solution(mesh):
    return jax.shard_map(
        shards,
        mesh=mesh,
        in_specs=(
            P(BOTH, None),
            P(None, "seq"),
            P(None, None, None, "mp"),
            P(None, None, "mp"),
            P(None, None, None, "mp"),
            P(None, None, "mp"),
            P(None, "mp", None),
            P(None, None, "mp"),
            P(None, "mp"),
            P(None, "mp", None),
            P(),
            P(),
            P(BOTH, None),
        ),
        out_specs=(
            P(BOTH, None),
            P(BOTH, None),
            P(None, None, None, "mp"),
            P(None, None, "mp"),
            P(None, None, None, "mp"),
            P(None, None, "mp"),
            P(None, "mp", None),
            P(None, None, "mp"),
            P(None, "mp"),
            P(None, "mp", None),
            P(),
            P(),
        ),
        check_vma=False,
    )
```
